128 devices in a mesh: row: 8 (over y, z_hi), col: 8 (over z_lo, x), grp: 2 (over core).
Axes of the slice: x: 4, y: 4, z: 4 (z_hi: 2, z_lo: 2; z = z_hi * 2 + z_lo), core: 2. Of those that a mesh axis runs over, the one named last changes fastest.
Arguments:
- krylov_basis: float32 [30, 8, 32768], P(None, None, 'row'), may hold values from -6 to 6
- lattice: int32 [3, 32768], P(None, 'row'), may hold values from 0 to 95, as said below
- strength_index: int32 [32768], P('row'), may hold values from 0 to 15
- strength_table: float32 [16], replicated, may hold values from 0.05 to 0.4
Outputs:
- new_block: float32 [8, 32768], P(None, 'row')
- hessenberg: float32 [30, 2, 4, 4], replicated
- block_gram: float32 [2, 4, 4], replicated
The draws below stay inside these ranges and needn't reach their ends.
Inputs may be any that keep to these rules, and one draw needn't show every extreme that they name: The 32768 scatterers stand on distinct lattice points.
All inputs are finite; a program needn't handle non-finite values.
Results may differ from the reference program's by a relative error of at most 0.0003.
Values may be sent and summed in bfloat16 or wider, within the bound.
No kernel may reach another device: no remote copies, remote signals or barrier semaphores. Data moves between devices by JAX's collectives and lax.ppermute only.
A program may use at most 64 MiB of HBM per device.

```python
import math
import jax
import jax.numpy as jnp
from jax import lax

INC = 4
BASIS = 30
TABLE = 16
GRID = 96
POINTS = 32768


def draw_lattice(key, part):
    cells = jax.random.permutation(key, GRID * GRID * GRID)[:POINTS]
    return jnp.stack([cells // (GRID * GRID), cells // GRID % GRID, cells % GRID]).astype(jnp.int32)


def set_ends(result, rng, smallest, top_value):
    shape = result.shape
    index_at = [jax.random.randint(jax.random.fold_in(rng, axis), (), 0, shape[axis]) for axis in range(len(shape))]
    result = result.at[tuple(index_at)].set(smallest)
    longest = shape.index(max(shape))
    index_at[longest] = (index_at[longest] + 1) % shape[longest]
    return result.at[tuple(index_at)].set(top_value)


def block_scale(key, dims, pieces, least, largest):
    def one(axis_at, parts):
        draws = jax.random.uniform(jax.random.fold_in(jax.random.fold_in(key, 6), axis_at), (parts,), jnp.float32, least / len(pieces), largest / len(pieces))
        return jnp.repeat(jnp.exp(draws), dims[axis_at] // parts).reshape((-1,) + (1,) * (len(dims) - axis_at - 1))

    level = one(*pieces[0])
    for cut in pieces[1:]:
        level = level * one(*cut)
    return level


def bell_draw(rng, dims, width, bound, split=(), kind=jnp.bfloat16):
    gain = block_scale(rng, dims, split, -0.22, 0.18) if split else 1.0
    result = jax.random.normal(rng, dims, jnp.float32) * width * gain
    return jnp.minimum(jnp.maximum(result, -bound), bound).astype(kind)


def setup_inputs(seed: int = 0) -> dict:
    streams_of = jax.random.split(jax.random.key(seed), 5)
    return {
        "krylov_basis": bell_draw(streams_of[0], (BASIS, 2 * INC, POINTS), 1.0, 6.0, ((2, 8),), jnp.float32),
        "lattice": draw_lattice(jax.random.fold_in(streams_of[4], 71), 0),
        "strength_index": set_ends(jax.random.randint(streams_of[2], (POINTS,), 0, TABLE), jax.random.fold_in(streams_of[2], 1), 0, TABLE - 1).astype(jnp.int32),
        "strength_table": jnp.clip(jnp.exp(jax.random.uniform(streams_of[3], (TABLE,), jnp.float32, math.log(0.05), math.log(0.4))), 0.05, 0.4),
    }


wave_number = 2.0
highest = lax.Precision.HIGHEST

def strength_of(strength_table, strength_index):
    matches = strength_index[:, None] == jnp.arange(strength_table.shape[0], dtype=jnp.int32)[None, :]
    return lax.optimization_barrier(jnp.sum(jnp.where(matches, strength_table[None, :], jnp.zeros((), strength_table.dtype)), axis=1))

def green_pair(target, source):
    squared = jnp.zeros((target.shape[1], source.shape[1]), jnp.float32)
    for axis_id in range(3):
        offset = target[axis_id][:, None] - source[axis_id][None, :]
        squared = squared + offset * offset
    distance = jnp.sqrt(jnp.maximum(squared, 1.0))
    phases = wave_number * distance
    inverse = 1.0 / distance
    distinct = squared > 0.5
    real_part = jnp.where(distinct, jnp.cos(phases) * inverse, 0.0)
    imag_part = jnp.where(distinct, jnp.sin(phases) * inverse, 0.0)
    return jnp.concatenate([real_part, imag_part], 0).astype(jnp.bfloat16)

def combine(product, tile_size):
    half_rows = product.shape[0] // 2
    direct = product[:, :tile_size]
    turned = product[:, tile_size:]
    return jnp.concatenate([direct[:half_rows] - turned[half_rows:], direct[half_rows:] + turned[:half_rows]], 0)

def scatter_block(target, source, weighted):
    stacked = green_pair(target, source)
    product = lax.dot_general(weighted, stacked, (((1,), (1,)), ((), ())), preferred_element_type=jnp.float32)
    return combine(product, target.shape[1])

def project(krylov_basis, field):
    return jnp.einsum('jan,bn->jab', krylov_basis, field, precision=highest)

def self_gram(field):
    return jnp.dot(field, field.T, precision=highest)

def complex_parts(gram):
    half_rows = gram.shape[-1] // 2
    real_part = gram[..., :half_rows, :half_rows] + gram[..., half_rows:, half_rows:]
    imag_part = gram[..., :half_rows, half_rows:] - gram[..., half_rows:, :half_rows]
    return (real_part, imag_part)

def subtract(krylov_basis, field, real_part, imag_part):
    upper = jnp.concatenate([real_part, imag_part], -1)
    lower = jnp.concatenate([-imag_part, real_part], -1)
    mixing = jnp.concatenate([upper, lower], -2)
    return field - jnp.einsum('jab,jan->bn', mixing, krylov_basis, precision=highest)

def reference(krylov_basis, lattice, strength_index, strength_table):
    point_total = lattice.shape[1]
    direction = krylov_basis[krylov_basis.shape[0] - 1]
    weighted = (direction * strength_of(strength_table, strength_index)[None, :]).astype(jnp.bfloat16)
    located = lattice.astype(jnp.float32)
    tile_size = math.gcd(point_total, 512)
    targets = located.reshape(3, point_total // tile_size, tile_size).transpose(1, 0, 2)
    tiles = lax.map(lambda target: scatter_block(target, located, weighted), targets)
    scattered = tiles.transpose(1, 0, 2).reshape(direction.shape[0], point_total)
    initial = direction - scattered
    once_real, once_imag = complex_parts(project(krylov_basis, initial) / point_total)
    once = subtract(krylov_basis, initial, once_real, once_imag)
    twice_real, twice_imag = complex_parts(project(krylov_basis, once) / point_total)
    new_block = subtract(krylov_basis, once, twice_real, twice_imag)
    hessenberg = jnp.stack([once_real + twice_real, once_imag + twice_imag], 1)
    norm_real, norm_imag = complex_parts(self_gram(new_block) / point_total)
    block_gram = jnp.stack([norm_real, norm_imag], 0)
    return (new_block, hessenberg, block_gram)
```

```python
import functools

import jax
import jax.numpy as jnp
import numpy as np
from jax import lax
from jax.experimental import pallas as pl
from jax.experimental.pallas import tpu as pltpu
from jax.sharding import PartitionSpec as P

f32 = jnp.float32
bf16 = jnp.bfloat16
highest = lax.Precision.HIGHEST
NT = (((1,), (1,)), ((), ()))
TN = (((0,), (0,)), ((), ()))

SINE = (4.442867902958593, -7.30744341838288, 3.5947880506690506, -0.7843739567334573)
SUB = 256
STEP = 512


def green_pair(squared, masked):
    if masked:
        distinct = squared > 0.5
        squared = jnp.maximum(squared, 1.0)
    inverse = lax.rsqrt(squared)
    turns = (squared * inverse) * np.float32(1.0 / np.pi)
    part = turns - jnp.round(turns)
    z = part * part
    poly = z * np.float32(SINE[3]) + np.float32(SINE[2])
    poly = poly * z + np.float32(SINE[1])
    poly = poly * z + np.float32(SINE[0])
    sine = part * poly
    cosine_2 = 1.0 - sine * sine
    rest = jnp.maximum(cosine_2 + 1.0, 1e-12)
    real_part = cosine_2 * inverse
    imag_part = (sine * inverse) * (rest * lax.rsqrt(rest))
    if masked:
        real_part = jnp.where(distinct, real_part, 0.0)
        imag_part = jnp.where(distinct, imag_part, 0.0)
    return real_part.astype(bf16), imag_part.astype(bf16)


def scatter_tiles(tiles, read, targets, held, acc, masked):
    width = targets.shape[1]

    def fill(i, slot):
        sites = read(i, 8)
        held[slot] = lax.dot_general(sites, targets[...], TN, preferred_element_type=f32)

    def work(i, slot):
        weights = read(i, 0)
        for k in range(width // SUB):
            cut = slice(k * SUB, (k + 1) * SUB)
            real_part, imag_part = green_pair(held[slot, :, cut], masked)
            acc[0:8, cut] += jnp.dot(weights, real_part, preferred_element_type=f32)
            acc[8:16, cut] += jnp.dot(weights, imag_part, preferred_element_type=f32)

    fill(0, 0)

    def body(h, carry):
        i = 2 * h
        fill(i + 1, 1)
        work(i, 0)
        fill(jnp.minimum(i + 2, tiles - 1), 0)
        work(i + 1, 1)
        return carry

    lax.fori_loop(0, tiles // 2, body, 0)


def local_kernel(targets, sources, acc, held):
    acc[...] = jnp.zeros_like(acc)

    def read(i, first):
        return sources[first : first + 8, pl.ds(pl.multiple_of(i * STEP, STEP), STEP)]

    scatter_tiles(sources.shape[1] // STEP, read, targets, held, acc, True)


def remote_kernel(place, targets, sources, begun, keep, send, held, acc):
    rows, _, length = sources.shape
    per_row = length // STEP
    row = place[0]
    acc[...] = begun[...]

    def read(i, first):
        chunk = lax.rem(row + 1 + i // per_row, rows)
        off = pl.multiple_of(lax.rem(i, per_row) * STEP, STEP)
        return sources[chunk, first : first + 8, pl.ds(off, STEP)]

    scatter_tiles((rows - 1) * per_row, read, targets, held, acc, False)
    real = acc[0:8]
    imag = acc[8:16]
    upper = real[0:4] - imag[4:8]
    lower = real[4:8] + imag[0:4]
    both = jnp.concatenate([upper, lower], 0)
    half = both.shape[1] // 2
    first, second = both[:, :half], both[:, half:]
    mine = place[1] == 0
    keep[...] = jnp.where(mine, first, second)
    send[...] = jnp.where(mine, second, first)


def split(x):
    high = x.astype(bf16)
    return high, (x - high.astype(f32)).astype(bf16)


def gram_kernel(place, basis, out):
    @pl.when(pl.program_id(0) == 0)
    def _():
        out[...] = jnp.zeros_like(out)

    rows = out.shape[0]
    own = basis[pl.ds(pl.multiple_of(place[2], 8), rows), :]
    own_high, own_low = split(own)
    high, low = split(basis[...])
    both = jnp.concatenate([own_high, own_low], 0)
    first = lax.dot_general(both, high, NT, preferred_element_type=f32)
    second = lax.dot_general(own_high, low, NT, preferred_element_type=f32)
    out[:, : basis.shape[0]] += first[:rows] + first[rows:] + second


def project_kernel(place, keep, got, direction, basis, gram, initial, packed):
    field = direction[...] - (keep[...] + got[...])
    initial[...] = field
    count = basis.shape[0]
    packed[...] = jnp.zeros_like(packed)
    packed[0:8, 0:count] = lax.dot_general(
        field, basis[...], NT, preferred_element_type=f32, precision=highest
    )
    packed[0:8, count : count + 8] = lax.dot_general(
        field, field, NT, preferred_element_type=f32, precision=highest
    )
    packed[8:, :] = gram[...]


def complex_mix(products, total):
    lane = lax.broadcasted_iota(jnp.int32, products.shape, 1)
    sub = lax.broadcasted_iota(jnp.int32, products.shape, 0)
    upper = (lane & 4) == 0
    width = products.shape[1]
    rolled = pltpu.roll(products, 4, 0)
    swapped = jnp.where(upper, pltpu.roll(rolled, width - 4, 1), pltpu.roll(rolled, 4, 1))
    same = upper == (sub < 4)
    return (products + jnp.where(same, swapped, -swapped)) * np.float32(1.0 / total)


def dot3(left, right):
    left_high, left_low = split(left)
    right_high, right_low = split(right)
    rows = left.shape[0]
    first = jnp.dot(
        jnp.concatenate([left_high, left_low], 0), right_high, preferred_element_type=f32
    )
    second = jnp.dot(left_high, right_low, preferred_element_type=f32)
    return first[:rows] + first[rows:] + second


def final_kernel(total, shared, basis, new, coef, norm, mix):
    parts = shared.shape[0]
    count = basis.shape[0]

    @pl.when(pl.program_id(0) == 0)
    def _():
        sums = shared[0, 8:16, :]
        for q in range(1, parts):
            sums = sums + shared[q, 8:16, :]
        products = sums[:, :count]
        own = sums[:, count : count + 8]
        gram = jnp.concatenate([shared[q, 16:32, :] for q in range(count // 16)], 0)[:, :count]
        dot = functools.partial(jnp.dot, preferred_element_type=f32, precision=highest)
        once = complex_mix(sums, total)[:, :count]
        twice_products = products - dot(once, gram)
        pad = jnp.concatenate([twice_products, jnp.zeros_like(sums[:, count:])], 1)
        both = once + complex_mix(pad, total)[:, :count]
        mix[...] = both
        coef[...] = both
        cross = lax.dot_general(both, products, NT, preferred_element_type=f32, precision=highest)
        cross_t = lax.dot_general(products, both, NT, preferred_element_type=f32, precision=highest)
        square = lax.dot_general(
            dot(both, gram), both, NT, preferred_element_type=f32, precision=highest
        )
        norm[...] = own - cross - cross_t + square

    width = basis.shape[1]
    per = width // shared.shape[2]
    base = pl.program_id(0) * per
    field = jnp.concatenate([shared[base + k, 0:8, :] for k in range(per)], 1)
    new[...] = field - dot3(mix[...], basis[...])


def gather_all(x, axis):
    length = lax.axis_size(axis)
    return lax.all_to_all(jnp.broadcast_to(x[None], (length, *x.shape)), axis, 0, 0, tiled=True)


VMEM = pl.BlockSpec(memory_space=pltpu.VMEM)
SMEM = pl.BlockSpec(memory_space=pltpu.SMEM)


def params(**more):
    return pltpu.CompilerParams(vmem_limit_bytes=40 << 20, **more)


def local(krylov_basis, lattice, strength_index, strength_table):
    blocks, channels, points = krylov_basis.shape
    count = blocks * channels
    rows = lax.axis_size("row")
    groups = lax.axis_size("grp")
    parts = lax.axis_size(("col", "grp"))
    row, col, grp = lax.axis_index("row"), lax.axis_index("col"), lax.axis_index("grp")
    part = lax.axis_index(("col", "grp"))
    total = points * rows
    own = points // parts
    wide = own * groups
    length = points // groups
    flat = krylov_basis.reshape(count, points)
    place = jnp.stack([row, grp, jnp.minimum(part * 16, count - 16), part]).astype(jnp.int32)

    direction = krylov_basis[blocks - 1]
    matches = strength_index[None, :] == jnp.arange(strength_table.shape[0], dtype=jnp.int32)[:, None]
    strength = jnp.sum(jnp.where(matches, strength_table[:, None], 0.0), axis=0)
    weighted = (direction * strength[None, :]).astype(bf16)
    x, y, z = lattice[0], lattice[1], lattice[2]
    norm = x * x + y * y + z * z
    high = norm // 256
    low = norm - 256 * high
    one = jnp.ones_like(x)
    sites = jnp.stack([x, y, z, high, low, one, one, 0 * one]).astype(bf16)
    aims = jnp.stack([-2 * x, -2 * y, -2 * z, 256 * one, one, 256 * high, low, 0 * one]).astype(bf16)
    packed = jnp.concatenate([weighted, sites], 0)
    sources = lax.dynamic_slice_in_dim(packed, grp * length, length, 1)
    targets = lax.dynamic_slice_in_dim(aims, col * wide, wide, 1)
    gathered = gather_all(sources, "row")

    held = pltpu.VMEM((2, STEP, wide), f32)
    sums = jax.ShapeDtypeStruct((16, wide), f32)
    begun = pl.pallas_call(
        local_kernel,
        out_shape=sums,
        in_specs=[VMEM, VMEM],
        out_specs=VMEM,
        scratch_shapes=[held],
        compiler_params=params(),
        cost_estimate=pl.CostEstimate(flops=3_000_000_000, bytes_accessed=200_000, transcendentals=0),
        name="scatter_local",
    )(targets, sources)

    gram = pl.pallas_call(
        gram_kernel,
        grid_spec=pltpu.PrefetchScalarGridSpec(
            num_scalar_prefetch=1,
            grid=(4,),
            in_specs=[pl.BlockSpec((count, points // 4), lambda k, s: (0, k))],
            out_specs=pl.BlockSpec((16, 256), lambda k, s: (0, 0)),
        ),
        out_shape=jax.ShapeDtypeStruct((16, 256), f32),
        compiler_params=params(),
        cost_estimate=pl.CostEstimate(flops=2_000_000_000, bytes_accessed=4_000_000, transcendentals=0),
        name="basis_gram",
    )(place, flat)

    half = jax.ShapeDtypeStruct((8, own), f32)
    keep, send = pl.pallas_call(
        remote_kernel,
        out_shape=(half, half),
        in_specs=[SMEM, VMEM, VMEM, VMEM],
        out_specs=(VMEM, VMEM),
        scratch_shapes=[held, pltpu.VMEM((16, wide), f32)],
        compiler_params=params(),
        cost_estimate=pl.CostEstimate(flops=20_000_000_000, bytes_accessed=800_000, transcendentals=0),
        name="scatter_remote",
    )(place, targets, gathered, begun)
    got = lax.ppermute(send, "grp", [(i, groups - 1 - i) for i in range(groups)])

    initial, partial = pl.pallas_call(
        project_kernel,
        grid_spec=pltpu.PrefetchScalarGridSpec(
            num_scalar_prefetch=1,
            grid=(1,),
            in_specs=[
                pl.BlockSpec((8, own), lambda k, s: (0, 0)),
                pl.BlockSpec((8, own), lambda k, s: (0, 0)),
                pl.BlockSpec((8, own), lambda k, s: (blocks - 1, s[3])),
                pl.BlockSpec((count, own), lambda k, s: (0, s[3])),
                pl.BlockSpec((16, 256), lambda k, s: (0, 0)),
            ],
            out_specs=[
                pl.BlockSpec((8, own), lambda k, s: (0, 0)),
                pl.BlockSpec((24, 256), lambda k, s: (0, 0)),
            ],
        ),
        out_shape=(half, jax.ShapeDtypeStruct((24, 256), f32)),
        compiler_params=params(),
        name="project",
    )(place, keep, got, flat, flat, gram)

    row_sums = jnp.sum(gather_all(partial, "row"), axis=0)
    shared = gather_all(jnp.concatenate([initial, row_sums], 0), ("col", "grp"))

    new_block, coef, norm = pl.pallas_call(
        functools.partial(final_kernel, total),
        grid=(4,),
        in_specs=[
            pl.BlockSpec((parts, 32, 256), lambda k: (0, 0, 0)),
            pl.BlockSpec((count, points // 4), lambda k: (0, k)),
        ],
        out_specs=[
            pl.BlockSpec((8, points // 4), lambda k: (0, k)),
            pl.BlockSpec((8, count), lambda k: (0, 0)),
            pl.BlockSpec((8, 8), lambda k: (0, 0)),
        ],
        out_shape=(
            jax.ShapeDtypeStruct((8, points), f32),
            jax.ShapeDtypeStruct((8, count), f32),
            jax.ShapeDtypeStruct((8, 8), f32),
        ),
        scratch_shapes=[pltpu.VMEM((8, count), f32)],
        compiler_params=params(),
        name="finish",
    )(shared, flat)

    inc = channels // 2
    hessenberg = coef.reshape(2, inc, blocks, channels)[..., :inc].transpose(2, 0, 3, 1)
    norm = norm / total
    real_part = norm[:inc, :inc] + norm[inc:, inc:]
    imag_part = norm[:inc, inc:] - norm[inc:, :inc]
    return new_block, hessenberg, jnp.stack([real_part, imag_part], 0)


def solution(mesh):
    in_specs = (P(None, None, "row"), P(None, "row"), P("row"), P())
    out_specs = (P(None, "row"), P(), P())
    return jax.shard_map(local, mesh=mesh, in_specs=in_specs, out_specs=out_specs, check_vma=False)
```

```python
import functools

import jax
import jax.numpy as jnp
import numpy as np
from jax import lax
from jax.experimental import pallas as pl
from jax.experimental.pallas import tpu as pltpu
from jax.sharding import PartitionSpec as P

f32 = jnp.float32
bf16 = jnp.bfloat16
highest = lax.Precision.HIGHEST
NT = (((1,), (1,)), ((), ()))
TN = (((0,), (0,)), ((), ()))

SINE = (4.4428816249751035, -7.307782340256801, 3.5971494246649565, -0.7893218692014636)
SUB = 256
STEP = 512


def green_pair(squared, masked):
    if masked:
        distinct = squared > 0.5
        squared = jnp.maximum(squared, 1.0)
    inverse = lax.rsqrt(squared)
    turns = (squared * inverse) * np.float32(1.0 / np.pi)
    part = turns - jnp.round(turns)
    z = part * part
    poly = z * np.float32(SINE[3]) + np.float32(SINE[2])
    poly = poly * z + np.float32(SINE[1])
    poly = poly * z + np.float32(SINE[0])
    sine = part * poly
    rest = 2.0 - sine * sine
    both = rest * inverse
    real_part = both - inverse
    imag_part = (sine * both) * lax.rsqrt(rest)
    if masked:
        real_part = jnp.where(distinct, real_part, 0.0)
        imag_part = jnp.where(distinct, imag_part, 0.0)
    return real_part.astype(bf16), imag_part.astype(bf16)


def scatter_tiles(tiles, read, targets, held, acc, masked):
    width = targets.shape[1]

    def fill(i, slot):
        sites = read(i, 8)
        held[slot] = lax.dot_general(sites, targets[...], TN, preferred_element_type=f32)

    def work(i, slot):
        weights = read(i, 0)
        for k in range(width // SUB):
            cut = slice(k * SUB, (k + 1) * SUB)
            real_part, imag_part = green_pair(held[slot, :, cut], masked)
            acc[0:8, cut] += jnp.dot(weights, real_part, preferred_element_type=f32)
            acc[8:16, cut] += jnp.dot(weights, imag_part, preferred_element_type=f32)

    fill(0, 0)

    def body(h, carry):
        i = 2 * h
        fill(i + 1, 1)
        work(i, 0)
        fill(jnp.minimum(i + 2, tiles - 1), 0)
        work(i + 1, 1)
        return carry

    lax.fori_loop(0, tiles // 2, body, 0)


def local_kernel(targets, sources, gram, acc, held):
    del gram
    acc[...] = jnp.zeros_like(acc)

    def read(i, first):
        return sources[first : first + 8, pl.ds(pl.multiple_of(i * STEP, STEP), STEP)]

    scatter_tiles(sources.shape[1] // STEP, read, targets, held, acc, True)


def remote_kernel(place, targets, sources, begun, keep, send, held, acc):
    rows, _, length = sources.shape
    per_row = length // STEP
    row = place[0]
    acc[...] = begun[...]

    def read(i, first):
        chunk = lax.rem(row + 1 + i // per_row, rows)
        off = pl.multiple_of(lax.rem(i, per_row) * STEP, STEP)
        return sources[chunk, first : first + 8, pl.ds(off, STEP)]

    scatter_tiles((rows - 1) * per_row, read, targets, held, acc, False)
    real = acc[0:8]
    imag = acc[8:16]
    upper = real[0:4] - imag[4:8]
    lower = real[4:8] + imag[0:4]
    both = jnp.concatenate([upper, lower], 0)
    half = both.shape[1] // 2
    first, second = both[:, :half], both[:, half:]
    mine = place[1] == 0
    keep[...] = jnp.where(mine, first, second)
    send[...] = jnp.where(mine, second, first)


def split(x):
    high = x.astype(bf16)
    return high, (x - high.astype(f32)).astype(bf16)


def swap_parts(x, rows):
    lane = lax.broadcasted_iota(jnp.int32, x.shape, 1)
    width = x.shape[1]
    rolled = pltpu.roll(x, rows - 4, 0)
    return jnp.where((lane & 4) == 0, pltpu.roll(rolled, width - 4, 1), pltpu.roll(rolled, 4, 1))


def complex_mix(products):
    lane = lax.broadcasted_iota(jnp.int32, products.shape, 1)
    sub = lax.broadcasted_iota(jnp.int32, products.shape, 0)
    swapped = swap_parts(products, products.shape[0])
    same = ((lane & 4) == 0) == ((sub & 4) == 0)
    return products + jnp.where(same, swapped, -swapped)


def prepare_kernel(place, table, direction, lattice, index, spread, sources, targets):
    rows, _, length = spread.shape
    wide = targets.shape[1]

    def sites(first, count, aim):
        part = lattice[:, pl.ds(pl.multiple_of(first, 128), count)]
        x, y, z = part[0:1], part[1:2], part[2:3]
        norm = x * x + y * y + z * z
        high = lax.shift_right_logical(norm, 8)
        low = norm & 255
        one = jnp.ones_like(x)
        if aim:
            parts = [-2 * x, -2 * y, -2 * z, 256 * one, one, 256 * high, low, 0 * one]
        else:
            parts = [x, y, z, high, low, one, one, 0 * one]
        return jnp.concatenate([p.astype(f32) for p in parts], 0).astype(bf16)

    targets[...] = sites(place[4], wide, True)
    start = pl.multiple_of(place[5], 128)
    chosen = index[:, pl.ds(start, length)]
    strength = jnp.zeros(chosen.shape, f32)
    for k in range(table.shape[0]):
        strength = jnp.where(chosen == k, table[k], strength)
    weighted = (direction[:, pl.ds(start, length)] * strength).astype(bf16)
    packed = jnp.concatenate([weighted, sites(start, length, False)], 0)
    sources[...] = packed
    for k in range(rows):
        spread[k] = packed


def gram_kernel(place, basis, gram, high, low):
    count, points = basis.shape
    chunk = 512
    start = pl.multiple_of(place[2], 16)
    total = jnp.zeros((16, count), f32)
    for k in range(points // chunk):
        cut = slice(k * chunk, (k + 1) * chunk)
        top, rest = split(basis[:, cut])
        high[:, cut] = top
        low[:, cut] = rest
        own = jnp.concatenate([high[pl.ds(start, 16), cut], low[pl.ds(start, 16), cut]], 0)
        first = lax.dot_general(own, top, NT, preferred_element_type=f32)
        second = lax.dot_general(own[:16], rest, NT, preferred_element_type=f32)
        total = total + (first[:16] + first[16:] + second)
    total = jnp.concatenate([total, jnp.zeros((16, 256 - count), f32)], 1)
    mixed = complex_mix(total)
    gram[...] = jnp.concatenate([mixed[0:4], mixed[8:12]], 0)


def project_kernel(place, keep, got, direction, high, low, gram, initial, packed):
    field = direction[...] - (keep[...] + got[...])
    initial[...] = field
    count = high.shape[0]
    width = field.shape[1]
    cut = pl.ds(pl.multiple_of(place[3] * width, 128), width)
    field_high, field_low = split(field)
    both = jnp.concatenate([field_high, field_low], 0)
    first = lax.dot_general(both, high[:, cut], NT, preferred_element_type=f32)
    second = lax.dot_general(field_high, low[:, cut], NT, preferred_element_type=f32)
    own = lax.dot_general(field, field, NT, preferred_element_type=f32, precision=highest)
    rest = jnp.zeros((8, 256 - count - 8), f32)
    packed[0:8, :] = jnp.concatenate([first[:8] + first[8:] + second, own, rest], 1)
    packed[8:, :] = gram[...]


def final_kernel(total, shared, high, low, new, coef, norm, grams):
    parts = shared.shape[0]
    count, points = high.shape
    width = shared.shape[2]
    scale = np.float32(1.0 / total)
    sums = shared[0, 8:16, :]
    for q in range(1, parts):
        sums = sums + shared[q, 8:16, :]
    lane = lax.broadcasted_iota(jnp.int32, sums.shape, 1)
    sub = lax.broadcasted_iota(jnp.int32, sums.shape, 0)
    grams[...] = jnp.zeros_like(grams)
    for q in range(count // 16):
        part = shared[q, 16:24, :]
        grams[16 * q : 16 * q + 8, :] = jnp.where(sub < 4, part, 0.0)
        grams[16 * q + 8 : 16 * q + 16, :] = jnp.where(sub < 4, pltpu.roll(part, 4, 0), 0.0)

    def times_gram(x):
        return complex_mix(
            jnp.dot(x, grams[...], preferred_element_type=f32, precision=highest)
        )

    products = jnp.where(lane < count, complex_mix(sums), 0.0)
    once = products * scale
    mix = 2.0 * once - times_gram(once) * scale
    seen = products - 0.5 * times_gram(mix)
    cross = lax.dot_general(mix, seen, NT, preferred_element_type=f32, precision=highest)
    cross_t = lax.dot_general(seen, mix, NT, preferred_element_type=f32, precision=highest)
    own = complex_mix(pltpu.roll(sums, width - count, 1))[:, 0:8]
    result = (own - cross - cross_t) * scale
    norm[0] = result[0:4, 0:4]
    norm[1] = result[0:4, 4:8]

    row = lax.broadcasted_iota(jnp.int32, (width, 128), 0)
    column = lax.broadcasted_iota(jnp.int32, (width, 128), 1)
    wanted = ((row & 4) == 0) & (column == (row & 7) * 32 + lax.shift_right_logical(row, 3))
    chosen = jnp.dot(
        mix, jnp.where(wanted, 1.0, 0.0), preferred_element_type=f32, precision=highest
    )
    blocks = coef.shape[3]
    for k in range(4):
        moved = pltpu.roll(chosen, (128 - 32 * k) % 128, 1)
        coef[0, k] = moved[0:4, 0:blocks]
        coef[1, k] = moved[4:8, 0:blocks]

    mix_high, mix_low = split(mix[:, :count])
    both = jnp.concatenate([mix_high, mix_low], 0)
    chunk = 4 * width
    for k in range(points // chunk):
        cut = slice(k * chunk, (k + 1) * chunk)
        first = jnp.dot(both, high[:, cut], preferred_element_type=f32)
        second = jnp.dot(mix_high, low[:, cut], preferred_element_type=f32)
        field = jnp.concatenate([shared[4 * k + i, 0:8, :] for i in range(4)], 1)
        new[:, cut] = field - (first[:8] + first[8:] + second)


def gather_all(x, axis):
    length = lax.axis_size(axis)
    return lax.all_to_all(jnp.broadcast_to(x[None], (length, *x.shape)), axis, 0, 0, tiled=True)


VMEM = pl.BlockSpec(memory_space=pltpu.VMEM)
SMEM = pl.BlockSpec(memory_space=pltpu.SMEM)
ANY = pl.BlockSpec(memory_space=pl.ANY)


def params():
    return pltpu.CompilerParams(vmem_limit_bytes=16 << 20)


def cost(flops, size):
    return pl.CostEstimate(flops=flops, bytes_accessed=size, transcendentals=0)


def local(krylov_basis, lattice, strength_index, strength_table):
    blocks, channels, points = krylov_basis.shape
    inc = channels // 2
    count = blocks * channels
    rows = lax.axis_size("row")
    groups = lax.axis_size("grp")
    parts = lax.axis_size(("col", "grp"))
    row, col, grp = lax.axis_index("row"), lax.axis_index("col"), lax.axis_index("grp")
    part = lax.axis_index(("col", "grp"))
    total = points * rows
    own = points // parts
    wide = own * groups
    length = points // groups
    flat = krylov_basis.reshape(count, points)
    place = jnp.stack(
        [row, grp, jnp.minimum(part * 16, count - 16), part, col * wide, grp * length]
    ).astype(jnp.int32)

    spread, sources, targets = pl.pallas_call(
        prepare_kernel,
        grid=(1,),
        in_specs=[
            SMEM,
            SMEM,
            pl.BlockSpec((channels, points), lambda k: (blocks - 1, 0)),
            pl.BlockSpec((3, points), lambda k: (0, 0)),
            pl.BlockSpec((1, points), lambda k: (0, 0)),
        ],
        out_specs=(VMEM, VMEM, VMEM),
        out_shape=(
            jax.ShapeDtypeStruct((rows, 16, length), bf16),
            jax.ShapeDtypeStruct((16, length), bf16),
            jax.ShapeDtypeStruct((8, wide), bf16),
        ),
        compiler_params=params(),
        name="prepare",
    )(place, strength_table, flat, lattice, strength_index[None, :])
    gathered = lax.all_to_all(spread, "row", 0, 0, tiled=True)

    gram, high, low = pl.pallas_call(
        gram_kernel,
        in_specs=[SMEM, VMEM],
        out_specs=(VMEM, VMEM, VMEM),
        out_shape=(
            jax.ShapeDtypeStruct((8, 256), f32),
            jax.ShapeDtypeStruct((count, points), bf16),
            jax.ShapeDtypeStruct((count, points), bf16),
        ),
        compiler_params=params(),
        cost_estimate=cost(2_000_000_000, 8_000_000),
        name="basis_gram",
    )(place, flat)

    held = pltpu.VMEM((2, STEP, wide), f32)
    begun = pl.pallas_call(
        local_kernel,
        out_shape=jax.ShapeDtypeStruct((16, wide), f32),
        in_specs=[VMEM, VMEM, ANY],
        out_specs=VMEM,
        scratch_shapes=[held],
        compiler_params=params(),
        cost_estimate=cost(3_000_000_000, 200_000),
        name="scatter_local",
    )(targets, sources, gram)

    half = jax.ShapeDtypeStruct((channels, own), f32)
    keep, send = pl.pallas_call(
        remote_kernel,
        out_shape=(half, half),
        in_specs=[SMEM, VMEM, VMEM, VMEM],
        out_specs=(VMEM, VMEM),
        scratch_shapes=[held, pltpu.VMEM((16, wide), f32)],
        compiler_params=params(),
        cost_estimate=cost(20_000_000_000, 800_000),
        name="scatter_remote",
    )(place, targets, gathered, begun)
    got = lax.ppermute(send, "grp", [(i, groups - 1 - i) for i in range(groups)])

    initial, partial = pl.pallas_call(
        project_kernel,
        grid_spec=pltpu.PrefetchScalarGridSpec(
            num_scalar_prefetch=1,
            grid=(1,),
            in_specs=[
                VMEM,
                VMEM,
                pl.BlockSpec((channels, own), lambda k, s: (blocks - 1, s[3])),
                VMEM,
                VMEM,
                VMEM,
            ],
            out_specs=[VMEM, VMEM],
        ),
        out_shape=(half, jax.ShapeDtypeStruct((16, 256), f32)),
        compiler_params=params(),
        name="project",
    )(place, keep, got, flat, high, low, gram)

    row_sums = jnp.sum(gather_all(partial, "row"), axis=0)
    shared = gather_all(jnp.concatenate([initial, row_sums], 0), ("col", "grp"))

    new_block, coef, norm = pl.pallas_call(
        functools.partial(final_kernel, total),
        in_specs=[VMEM, VMEM, VMEM],
        out_specs=(VMEM, VMEM, VMEM),
        out_shape=(
            jax.ShapeDtypeStruct((channels, points), f32),
            jax.ShapeDtypeStruct((2, inc, inc, blocks), f32),
            jax.ShapeDtypeStruct((2, inc, inc), f32),
        ),
        scratch_shapes=[pltpu.VMEM((256, 256), f32)],
        compiler_params=params(),
        name="finish",
    )(shared, high, low)
    return new_block, coef.transpose(3, 0, 1, 2), norm


def solution(mesh):
    in_specs = (P(None, None, "row"), P(None, "row"), P("row"), P())
    out_specs = (P(None, "row"), P(), P())
    return jax.shard_map(local, mesh=mesh, in_specs=in_specs, out_specs=out_specs, check_vma=False)
```

```python
import functools

import jax
import jax.numpy as jnp
import numpy as np
from jax import lax
from jax.experimental import pallas as pl
from jax.experimental.pallas import tpu as pltpu
from jax.sharding import PartitionSpec as P

f32 = jnp.float32
bf16 = jnp.bfloat16
highest = lax.Precision.HIGHEST
NT = (((1,), (1,)), ((), ()))
TN = (((0,), (0,)), ((), ()))

SINE = (4.4428816249751035, -7.307782340256801, 3.5971494246649565, -0.7893218692014636)
SUB = 256
STEP = 512


def green_pair(squared, masked):
    if masked:
        distinct = squared > 0.5
        squared = jnp.maximum(squared, 1.0)
    inverse = lax.rsqrt(squared)
    turns = (squared * inverse) * np.float32(1.0 / np.pi)
    part = turns - jnp.round(turns)
    z = part * part
    poly = z * np.float32(SINE[3]) + np.float32(SINE[2])
    poly = poly * z + np.float32(SINE[1])
    poly = poly * z + np.float32(SINE[0])
    sine = part * poly
    rest = 2.0 - sine * sine
    both = rest * inverse
    real_part = both - inverse
    imag_part = (sine * both) * lax.rsqrt(rest)
    if masked:
        real_part = jnp.where(distinct, real_part, 0.0)
        imag_part = jnp.where(distinct, imag_part, 0.0)
    return real_part.astype(bf16), imag_part.astype(bf16)


def scatter_tiles(tiles, read, targets, held, acc, masked):
    width = targets.shape[1]

    def fill(i, slot):
        sites = read(i, 8)
        held[slot] = lax.dot_general(sites, targets[...], TN, preferred_element_type=f32)

    def work(i, slot):
        weights = read(i, 0)
        for k in range(width // SUB):
            cut = slice(k * SUB, (k + 1) * SUB)
            real_part, imag_part = green_pair(held[slot, :, cut], masked)
            acc[0:8, cut] += jnp.dot(weights, real_part, preferred_element_type=f32)
            acc[8:16, cut] += jnp.dot(weights, imag_part, preferred_element_type=f32)

    fill(0, 0)

    def body(h, carry):
        i = 2 * h
        fill(i + 1, 1)
        work(i, 0)
        fill(jnp.minimum(i + 2, tiles - 1), 0)
        work(i + 1, 1)
        return carry

    lax.fori_loop(0, tiles // 2, body, 0)


def remote_kernel(place, targets, sources, begun, keep, send, held, acc):
    rows, _, length = sources.shape
    per_row = length // STEP
    row = place[0]
    acc[...] = begun[...]

    def read(i, first):
        chunk = lax.rem(row + 1 + i // per_row, rows)
        off = pl.multiple_of(lax.rem(i, per_row) * STEP, STEP)
        return sources[chunk, first : first + 8, pl.ds(off, STEP)]

    scatter_tiles((rows - 1) * per_row, read, targets, held, acc, False)
    real = acc[0:8]
    imag = acc[8:16]
    upper = real[0:4] - imag[4:8]
    lower = real[4:8] + imag[0:4]
    both = jnp.concatenate([upper, lower], 0)
    half = both.shape[1] // 2
    first, second = both[:, :half], both[:, half:]
    mine = place[1] == 0
    keep[...] = jnp.where(mine, first, second)
    send[...] = jnp.where(mine, second, first)


def split(x):
    high = x.astype(bf16)
    return high, (x - high.astype(f32)).astype(bf16)


def swap_parts(x, rows):
    lane = lax.broadcasted_iota(jnp.int32, x.shape, 1)
    width = x.shape[1]
    rolled = pltpu.roll(x, rows - 4, 0)
    return jnp.where((lane & 4) == 0, pltpu.roll(rolled, width - 4, 1), pltpu.roll(rolled, 4, 1))


def complex_mix(products):
    lane = lax.broadcasted_iota(jnp.int32, products.shape, 1)
    sub = lax.broadcasted_iota(jnp.int32, products.shape, 0)
    swapped = swap_parts(products, products.shape[0])
    same = ((lane & 4) == 0) == ((sub & 4) == 0)
    return products + jnp.where(same, swapped, -swapped)


def prepare_kernel(place, basis, lattice, index, table, spread, sources, targets, *scratch):
    direction, chosen, held_table, points, aims, sems = scratch
    rows, _, length = spread.shape
    wide = targets.shape[1]
    channels = direction.shape[0]
    aim = pl.multiple_of(place[4], 128)
    start = pl.multiple_of(place[5], 128)
    last = basis.shape[0] - channels
    copies = [
        pltpu.make_async_copy(lattice.at[:, pl.ds(start, length)], points, sems.at[0]),
        pltpu.make_async_copy(index.at[:, pl.ds(start, length)], chosen, sems.at[1]),
        pltpu.make_async_copy(table, held_table, sems.at[2]),
        pltpu.make_async_copy(
            basis.at[last : last + channels, pl.ds(start, length)], direction, sems.at[3]
        ),
        pltpu.make_async_copy(lattice.at[:, pl.ds(aim, wide)], aims, sems.at[4]),
    ]
    for copy in copies:
        copy.start()

    def shared_rows(part):
        x, y, z = part[0:1], part[1:2], part[2:3]
        norm = x * x + y * y + z * z
        return x, y, z, lax.shift_right_logical(norm, 8), norm & 255, jnp.ones_like(x)

    def stacked(parts):
        return jnp.concatenate([p.astype(f32) for p in parts], 0)

    copies[0].wait()
    x, y, z, high, low, one = shared_rows(points[...])
    sites = stacked([x, y, z, high, low, one, one, 0 * one])
    copies[1].wait()
    copies[2].wait()
    strength = jnp.zeros(chosen.shape, f32)
    for k in range(table.shape[1]):
        strength = jnp.where(chosen[...] == k, held_table[0:1, k : k + 1], strength)
    copies[3].wait()
    packed = jnp.concatenate([direction[...] * strength, sites], 0).astype(bf16)
    sources[...] = packed
    for k in range(rows):
        spread[k] = packed
    copies[4].wait()
    x, y, z, high, low, one = shared_rows(aims[...])
    targets[...] = stacked(
        [-2 * x, -2 * y, -2 * z, 256 * one, one, 256 * high, low, 0 * one]
    ).astype(bf16)


def local_kernel(place, targets, sources, basis, *rest):
    acc, gram, direction, own_high, own_low, tiles, held, high, low, sems = rest
    count, points = basis.shape
    chunk = points // sems.shape[0]
    channels, width = direction.shape
    start = pl.multiple_of(place[2], 16)
    copies = []
    for k in range(points // chunk):
        cut = slice(k * chunk, (k + 1) * chunk)
        copies.append(pltpu.make_async_copy(basis.at[:, cut], held.at[:, cut], sems.at[k]))
        copies[-1].start()

    acc[...] = jnp.zeros_like(acc)

    def read(i, first):
        return sources[first : first + 8, pl.ds(pl.multiple_of(i * STEP, STEP), STEP)]

    scatter_tiles(sources.shape[1] // STEP, read, targets, tiles, acc, True)

    total = jnp.zeros((16, count), f32)
    for k in range(points // chunk):
        cut = slice(k * chunk, (k + 1) * chunk)
        copies[k].wait()
        top, rest = split(held[:, cut])
        high[:, cut] = top
        low[:, cut] = rest
        own = jnp.concatenate([high[pl.ds(start, 16), cut], low[pl.ds(start, 16), cut]], 0)
        first = lax.dot_general(own, top, NT, preferred_element_type=f32)
        second = lax.dot_general(own[:16], rest, NT, preferred_element_type=f32)
        total = total + (first[:16] + first[16:] + second)
    total = jnp.concatenate([total, jnp.zeros((16, 256 - count), f32)], 1)
    mixed = complex_mix(total)
    gram[...] = stack_halves(jnp.concatenate([mixed[0:4], mixed[8:12]], 0))
    here = pl.ds(pl.multiple_of(place[3] * width, 128), width)
    direction[...] = held[count - channels : count, here]
    own_high[...] = high[:, here]
    own_low[...] = low[:, here]


def stack_halves(x):
    return jnp.concatenate([x[:, :128], x[:, 128:]], 0)


def join_halves(x):
    rows = x.shape[0] // 2
    return jnp.concatenate([x[:rows], x[rows:]], 1)


def project_kernel(keep, got, direction, high, low, gram, initial, packed):
    field = direction[...] - (keep[...] + got[...])
    initial[...] = stack_halves(field)
    count = high.shape[0]
    field_high, field_low = split(field)
    both = jnp.concatenate([field_high, field_low], 0)
    first = lax.dot_general(both, high[...], NT, preferred_element_type=f32)
    second = lax.dot_general(field_high, low[...], NT, preferred_element_type=f32)
    own = lax.dot_general(field, field, NT, preferred_element_type=f32, precision=highest)
    rest = jnp.zeros((8, 256 - count - 8), f32)
    products = jnp.concatenate([first[:8] + first[8:] + second, own, rest], 1)
    packed[0:8, :] = stack_halves(complex_mix(products)[0:4])
    packed[8:, :] = gram[...]


def final_kernel(total, shared, basis, new, coef, norm, grams, held, sems):
    parts = shared.shape[0]
    count, points = basis.shape
    width = 256
    chunk = points // sems.shape[0]
    copies = []
    for k in range(points // chunk):
        cut = slice(k * chunk, (k + 1) * chunk)
        copies.append(pltpu.make_async_copy(basis.at[:, cut], held.at[:, cut], sems.at[k]))
        copies[-1].start()
    scale = np.float32(1.0 / total)
    sums = shared[0, 16:24, :]
    for q in range(1, parts):
        sums = sums + shared[q, 16:24, :]
    upper = join_halves(sums)
    lane = lax.broadcasted_iota(jnp.int32, upper.shape, 1)
    lower = jnp.where(
        (lane & 4) == 0, -pltpu.roll(upper, width - 4, 1), pltpu.roll(upper, 4, 1)
    )
    sums = jnp.concatenate([upper, lower], 0)
    lane = lax.broadcasted_iota(jnp.int32, sums.shape, 1)
    sub = lax.broadcasted_iota(jnp.int32, sums.shape, 0)
    grams[...] = jnp.zeros_like(grams)
    for q in range(count // 16):
        part = join_halves(shared[q, 24:40, :])
        grams[16 * q : 16 * q + 8, :] = jnp.where(sub < 4, part, 0.0)
        grams[16 * q + 8 : 16 * q + 16, :] = jnp.where(sub < 4, pltpu.roll(part, 4, 0), 0.0)

    def times_gram(x):
        return complex_mix(
            jnp.dot(x, grams[...], preferred_element_type=f32, precision=highest)
        )

    products = jnp.where(lane < count, sums, 0.0)
    once = products * scale
    mix = 2.0 * once - times_gram(once) * scale
    seen = products - 0.5 * times_gram(mix)
    cross = lax.dot_general(mix, seen, NT, preferred_element_type=f32, precision=highest)
    cross_t = lax.dot_general(seen, mix, NT, preferred_element_type=f32, precision=highest)
    own = pltpu.roll(sums, width - count, 1)[:, 0:8]
    result = (own - cross - cross_t) * scale
    norm[0] = result[0:4, 0:4]
    norm[1] = result[0:4, 4:8]

    row = lax.broadcasted_iota(jnp.int32, (width, 128), 0)
    column = lax.broadcasted_iota(jnp.int32, (width, 128), 1)
    wanted = ((row & 4) == 0) & (column == (row & 7) * 32 + lax.shift_right_logical(row, 3))
    chosen = jnp.dot(
        mix, jnp.where(wanted, 1.0, 0.0), preferred_element_type=f32, precision=highest
    )
    blocks = coef.shape[3]
    for k in range(4):
        moved = pltpu.roll(chosen, (128 - 32 * k) % 128, 1)
        coef[0, k] = moved[0:4, 0:blocks]
        coef[1, k] = moved[4:8, 0:blocks]

    mix_high, mix_low = split(mix[:, :count])
    both = jnp.concatenate([mix_high, mix_low], 0)
    for k in range(points // chunk):
        cut = slice(k * chunk, (k + 1) * chunk)
        copies[k].wait()
        top, rest = split(held[:, cut])
        first = jnp.dot(both, top, preferred_element_type=f32)
        second = jnp.dot(mix_high, rest, preferred_element_type=f32)
        each = chunk // width
        field = jnp.concatenate(
            [join_halves(shared[each * k + i, 0:16, :]) for i in range(each)], 1
        )
        new[:, cut] = field - (first[:8] + first[8:] + second)


def gather_all(x, axis):
    length = lax.axis_size(axis)
    return lax.all_to_all(jnp.broadcast_to(x[None], (length, *x.shape)), axis, 0, 0, tiled=True)


VMEM = pl.BlockSpec(memory_space=pltpu.VMEM)
SMEM = pl.BlockSpec(memory_space=pltpu.SMEM)
HBM = pl.BlockSpec(memory_space=pltpu.HBM)


def params(room=16 << 20):
    return pltpu.CompilerParams(vmem_limit_bytes=room)


def cost(flops, size):
    return pl.CostEstimate(flops=flops, bytes_accessed=size, transcendentals=0)


def local(krylov_basis, lattice, strength_index, strength_table):
    blocks, channels, points = krylov_basis.shape
    inc = channels // 2
    count = blocks * channels
    rows = lax.axis_size("row")
    groups = lax.axis_size("grp")
    parts = lax.axis_size(("col", "grp"))
    row, col, grp = lax.axis_index("row"), lax.axis_index("col"), lax.axis_index("grp")
    part = lax.axis_index(("col", "grp"))
    total = points * rows
    own = points // parts
    wide = own * groups
    length = points // groups
    flat = krylov_basis.reshape(count, points)
    place = jnp.stack(
        [row, grp, jnp.minimum(part * 16, count - 16), part, col * wide, grp * length]
    ).astype(jnp.int32)

    spread, sources, targets = pl.pallas_call(
        prepare_kernel,
        in_specs=[SMEM, HBM, HBM, HBM, HBM],
        out_specs=(VMEM, VMEM, VMEM),
        out_shape=(
            jax.ShapeDtypeStruct((rows, 16, length), bf16),
            jax.ShapeDtypeStruct((16, length), bf16),
            jax.ShapeDtypeStruct((8, wide), bf16),
        ),
        scratch_shapes=[
            pltpu.VMEM((channels, length), f32),
            pltpu.VMEM((1, length), jnp.int32),
            pltpu.VMEM((1, strength_table.shape[0]), f32),
            pltpu.VMEM((3, length), jnp.int32),
            pltpu.VMEM((3, wide), jnp.int32),
            pltpu.SemaphoreType.DMA((5,)),
        ],
        compiler_params=params((64 << 20) - (64 << 10)),
        name="prepare",
    )(place, flat, lattice, strength_index[None, :], strength_table[None, :])
    gathered = lax.all_to_all(spread, "row", 0, 0, tiled=True)

    half = jax.ShapeDtypeStruct((channels, own), f32)
    held = pltpu.VMEM((2, STEP, wide), f32)
    begun, gram, direction, high, low = pl.pallas_call(
        local_kernel,
        in_specs=[SMEM, VMEM, VMEM, HBM],
        out_specs=(VMEM,) * 5,
        out_shape=(
            jax.ShapeDtypeStruct((16, wide), f32),
            jax.ShapeDtypeStruct((16, 128), f32),
            half,
            jax.ShapeDtypeStruct((count, own), bf16),
            jax.ShapeDtypeStruct((count, own), bf16),
        ),
        scratch_shapes=[
            held,
            pltpu.VMEM((count, points), f32),
            pltpu.VMEM((count, points), bf16),
            pltpu.VMEM((count, points), bf16),
            pltpu.SemaphoreType.DMA((8,)),
        ],
        compiler_params=params(52 << 20),
        cost_estimate=cost(5_000_000_000, 8_000_000),
        name="scatter_local",
    )(place, targets, sources, flat)

    keep, send = pl.pallas_call(
        remote_kernel,
        out_shape=(half, half),
        in_specs=[SMEM, VMEM, VMEM, VMEM],
        out_specs=(VMEM, VMEM),
        scratch_shapes=[held, pltpu.VMEM((16, wide), f32)],
        compiler_params=params(),
        cost_estimate=cost(20_000_000_000, 800_000),
        name="scatter_remote",
    )(place, targets, gathered, begun)
    got = lax.ppermute(send, "grp", [(i, groups - 1 - i) for i in range(groups)])

    initial, partial = pl.pallas_call(
        project_kernel,
        in_specs=[VMEM] * 6,
        out_specs=(VMEM, VMEM),
        out_shape=(jax.ShapeDtypeStruct((16, 128), f32), jax.ShapeDtypeStruct((24, 128), f32)),
        compiler_params=params(),
        name="project",
    )(keep, got, direction, high, low, gram)

    row_sums = jnp.sum(gather_all(partial, "row"), axis=0)
    shared = gather_all(jnp.concatenate([initial, row_sums], 0), ("col", "grp"))

    new_block, coef, norm = pl.pallas_call(
        functools.partial(final_kernel, total),
        in_specs=[VMEM, HBM],
        out_specs=(VMEM, VMEM, VMEM),
        out_shape=(
            jax.ShapeDtypeStruct((channels, points), f32),
            jax.ShapeDtypeStruct((2, inc, inc, blocks), f32),
            jax.ShapeDtypeStruct((2, inc, inc), f32),
        ),
        scratch_shapes=[
            pltpu.VMEM((256, 256), f32),
            pltpu.VMEM((count, points), f32),
            pltpu.SemaphoreType.DMA((4,)),
        ],
        compiler_params=params(52 << 20),
        name="finish",
    )(shared, flat)
    return new_block, coef.transpose(3, 0, 1, 2), norm


def solution(mesh):
    in_specs = (P(None, None, "row"), P(None, "row"), P("row"), P())
    out_specs = (P(None, "row"), P(), P())
    return jax.shard_map(local, mesh=mesh, in_specs=in_specs, out_specs=out_specs, check_vma=False)
```

```python
import functools

import jax
import jax.numpy as jnp
import numpy as np
from jax import lax
from jax.experimental import pallas as pl
from jax.experimental.pallas import tpu as pltpu
from jax.sharding import PartitionSpec as P

f32 = jnp.float32
bf16 = jnp.bfloat16
highest = lax.Precision.HIGHEST
NT = (((1,), (1,)), ((), ()))
TN = (((0,), (0,)), ((), ()))

SINE = (4.4428816249751035, -7.307782340256801, 3.5971494246649565, -0.7893218692014636)
SUB = 256
STEP = 512


def green_pair(squared, masked):
    if masked:
        distinct = squared > 0.5
        squared = jnp.maximum(squared, 1.0)
    inverse = lax.rsqrt(squared)
    turns = (squared * inverse) * np.float32(1.0 / np.pi)
    part = turns - jnp.round(turns)
    z = part * part
    poly = z * np.float32(SINE[3]) + np.float32(SINE[2])
    poly = poly * z + np.float32(SINE[1])
    poly = poly * z + np.float32(SINE[0])
    sine = part * poly
    rest = 2.0 - sine * sine
    both = rest * inverse
    real_part = both - inverse
    imag_part = (sine * both) * lax.rsqrt(rest)
    if masked:
        real_part = jnp.where(distinct, real_part, 0.0)
        imag_part = jnp.where(distinct, imag_part, 0.0)
    return real_part.astype(bf16), imag_part.astype(bf16)


def scatter_tiles(tiles, read, targets, held, acc, masked):
    width = targets.shape[1]

    def fill(i, slot):
        sites = read(i, 8)
        held[slot] = lax.dot_general(sites, targets[...], TN, preferred_element_type=f32)

    def work(i, slot):
        weights = read(i, 0)
        for k in range(width // SUB):
            cut = slice(k * SUB, (k + 1) * SUB)
            real_part, imag_part = green_pair(held[slot, :, cut], masked)
            acc[0:8, cut] += jnp.dot(weights, real_part, preferred_element_type=f32)
            acc[8:16, cut] += jnp.dot(weights, imag_part, preferred_element_type=f32)

    fill(0, 0)

    def body(h, carry):
        i = 2 * h
        fill(i + 1, 1)
        work(i, 0)
        fill(jnp.minimum(i + 2, tiles - 1), 0)
        work(i + 1, 1)
        return carry

    lax.fori_loop(0, tiles // 2, body, 0)


def remote_kernel(ready, sources, begun, keep, send, held, acc):
    rows, _, length = sources.shape
    per_row = length // STEP
    row = lax.axis_index("row")
    targets = ready.at[8:16, length:]
    acc[...] = begun[...]

    def read(i, first):
        chunk = lax.rem(row + 1 + i // per_row, rows)
        off = pl.multiple_of(lax.rem(i, per_row) * STEP, STEP)
        return sources[chunk, first : first + 8, pl.ds(off, STEP)]

    scatter_tiles((rows - 1) * per_row, read, targets, held, acc, False)
    real = acc[0:8]
    imag = acc[8:16]
    upper = real[0:4] - imag[4:8]
    lower = real[4:8] + imag[0:4]
    both = jnp.concatenate([upper, lower], 0)
    half = both.shape[1] // 2
    first, second = both[:, :half], both[:, half:]
    mine = lax.axis_index("grp") == 0
    keep[...] = jnp.where(mine, first, second)
    send[...] = jnp.where(mine, second, first)


def split(x):
    high = x.astype(bf16)
    return high, (x - high.astype(f32)).astype(bf16)


def swap_parts(x, rows):
    lane = lax.broadcasted_iota(jnp.int32, x.shape, 1)
    width = x.shape[1]
    rolled = pltpu.roll(x, rows - 4, 0)
    return jnp.where((lane & 4) == 0, pltpu.roll(rolled, width - 4, 1), pltpu.roll(rolled, 4, 1))


def complex_mix(products):
    lane = lax.broadcasted_iota(jnp.int32, products.shape, 1)
    sub = lax.broadcasted_iota(jnp.int32, products.shape, 0)
    swapped = swap_parts(products, products.shape[0])
    same = ((lane & 4) == 0) == ((sub & 4) == 0)
    return products + jnp.where(same, swapped, -swapped)


def prepare_kernel(basis, lattice, index, table, spread, ready, *scratch):
    direction, chosen, held_table, points, aims, sems = scratch
    rows, _, length = spread.shape
    wide = aims.shape[1]
    channels = direction.shape[0]
    aim = pl.multiple_of(lax.axis_index("col") * wide, 128)
    start = pl.multiple_of(lax.axis_index("grp") * length, 128)
    last = basis.shape[0] - channels
    copies = [
        pltpu.make_async_copy(lattice.at[:, pl.ds(start, length)], points, sems.at[0]),
        pltpu.make_async_copy(index.at[:, pl.ds(start, length)], chosen, sems.at[1]),
        pltpu.make_async_copy(table, held_table, sems.at[2]),
        pltpu.make_async_copy(
            basis.at[last : last + channels, pl.ds(start, length)], direction, sems.at[3]
        ),
        pltpu.make_async_copy(lattice.at[:, pl.ds(aim, wide)], aims, sems.at[4]),
    ]
    for copy in copies:
        copy.start()

    def shared_rows(part):
        x, y, z = part[0:1], part[1:2], part[2:3]
        norm = x * x + y * y + z * z
        return x, y, z, lax.shift_right_logical(norm, 8), norm & 255, jnp.ones_like(x)

    def stacked(parts):
        return jnp.concatenate([p.astype(f32) for p in parts], 0)

    copies[0].wait()
    x, y, z, high, low, one = shared_rows(points[...])
    sites = stacked([x, y, z, high, low, one, one, 0 * one])
    copies[1].wait()
    copies[2].wait()
    strength = jnp.zeros(chosen.shape, f32)
    for k in range(table.shape[1]):
        strength = jnp.where(chosen[...] == k, held_table[0:1, k : k + 1], strength)
    copies[3].wait()
    packed = jnp.concatenate([direction[...] * strength, sites], 0).astype(bf16)
    ready[:, :length] = packed
    for k in range(rows):
        spread[k] = packed
    copies[4].wait()
    x, y, z, high, low, one = shared_rows(aims[...])
    sites = stacked([-2 * x, -2 * y, -2 * z, 256 * one, one, 256 * high, low, 0 * one])
    ready[:, length:] = jnp.concatenate([jnp.zeros_like(sites), sites], 0).astype(bf16)


def local_kernel(ready, basis, *rest):
    acc, gram, direction, own_high, own_low, kept, tiles, held, high, low, sems = rest
    half = kept.shape[1]
    length = ready.shape[1] - tiles.shape[2]
    targets = ready.at[8:16, length:]
    part = lax.axis_index(("col", "grp"))
    count, points = basis.shape
    pieces = sems.shape[0] - 1
    chunk = points // pieces
    channels, width = direction.shape
    here = pl.ds(pl.multiple_of(part * width, 128), width)
    own = pltpu.make_async_copy(
        basis.at[count - channels : count, here], direction, sems.at[pieces]
    )
    own.start()
    start = pl.multiple_of(jnp.minimum(part * 16, count - 16), 16)

    def place_of(k):
        first = k * chunk
        if first < half:
            return kept.at[:, first : first + chunk]
        return held.at[:, first - half : first - half + chunk]

    copies = []
    for k in range(points // chunk):
        cut = slice(k * chunk, (k + 1) * chunk)
        copies.append(pltpu.make_async_copy(basis.at[:, cut], place_of(k), sems.at[k]))
        copies[-1].start()

    acc[...] = jnp.zeros_like(acc)

    def read(i, first):
        return ready[first : first + 8, pl.ds(pl.multiple_of(i * STEP, STEP), STEP)]

    scatter_tiles(length // STEP, read, targets, tiles, acc, True)

    total = jnp.zeros((16, count), f32)
    for k in range(points // chunk):
        cut = slice(k * chunk, (k + 1) * chunk)
        copies[k].wait()
        top, rest = split(place_of(k)[...])
        high[:, cut] = top
        low[:, cut] = rest
        mine = jnp.concatenate([high[pl.ds(start, 16), cut], low[pl.ds(start, 16), cut]], 0)
        first = lax.dot_general(mine, top, NT, preferred_element_type=f32)
        second = lax.dot_general(mine[:16], rest, NT, preferred_element_type=f32)
        total = total + (first[:16] + first[16:] + second)
    total = jnp.concatenate([total, jnp.zeros((16, 256 - count), f32)], 1)
    mixed = complex_mix(total)
    gram[...] = stack_halves(jnp.concatenate([mixed[0:4], mixed[8:12]], 0))
    own.wait()
    own_high[...] = high[:, here]
    own_low[...] = low[:, here]


def stack_halves(x):
    return jnp.concatenate([x[:, :128], x[:, 128:]], 0)


def join_halves(x):
    rows = x.shape[0] // 2
    return jnp.concatenate([x[:rows], x[rows:]], 1)


def project_kernel(keep, got, direction, high, low, gram, initial, packed):
    field = direction[...] - (keep[...] + got[...])
    initial[...] = stack_halves(field)
    count = high.shape[0]
    field_high, field_low = split(field)
    both = jnp.concatenate([field_high, field_low], 0)
    first = lax.dot_general(both, high[...], NT, preferred_element_type=f32)
    second = lax.dot_general(field_high, low[...], NT, preferred_element_type=f32)
    own = lax.dot_general(field, field, NT, preferred_element_type=f32, precision=highest)
    rest = jnp.zeros((8, 256 - count - 8), f32)
    products = jnp.concatenate([first[:8] + first[8:] + second, own, rest], 1)
    packed[0:8, :] = stack_halves(complex_mix(products)[0:4])
    packed[8:, :] = gram[...]


def final_kernel(total, shared, kept, basis, new, coef, norm, grams, held, sems):
    parts = shared.shape[0]
    count, points = basis.shape
    width = 256
    chunk = 512
    half = points - held.shape[1]
    copies = []
    for k in range(sems.shape[0]):
        cut = slice(k * chunk, (k + 1) * chunk)
        there = slice(half + k * chunk, half + (k + 1) * chunk)
        copies.append(pltpu.make_async_copy(basis.at[:, there], held.at[:, cut], sems.at[k]))
        copies[-1].start()
    scale = np.float32(1.0 / total)
    sums = shared[0, 16:24, :]
    for q in range(1, parts):
        sums = sums + shared[q, 16:24, :]
    upper = join_halves(sums)
    lane = lax.broadcasted_iota(jnp.int32, upper.shape, 1)
    lower = jnp.where(
        (lane & 4) == 0, -pltpu.roll(upper, width - 4, 1), pltpu.roll(upper, 4, 1)
    )
    sums = jnp.concatenate([upper, lower], 0)
    lane = lax.broadcasted_iota(jnp.int32, sums.shape, 1)
    sub = lax.broadcasted_iota(jnp.int32, sums.shape, 0)
    grams[...] = jnp.zeros_like(grams)
    for q in range(count // 16):
        part = join_halves(shared[q, 24:40, :])
        grams[16 * q : 16 * q + 8, :] = jnp.where(sub < 4, part, 0.0)
        grams[16 * q + 8 : 16 * q + 16, :] = jnp.where(sub < 4, pltpu.roll(part, 4, 0), 0.0)

    def times_gram(x):
        return complex_mix(
            jnp.dot(x, grams[...], preferred_element_type=f32, precision=highest)
        )

    products = jnp.where(lane < count, sums, 0.0)
    once = products * scale
    mix = 2.0 * once - times_gram(once) * scale
    seen = products - 0.5 * times_gram(mix)
    cross = lax.dot_general(mix, seen, NT, preferred_element_type=f32, precision=highest)
    cross_t = lax.dot_general(seen, mix, NT, preferred_element_type=f32, precision=highest)
    own = pltpu.roll(sums, width - count, 1)[:, 0:8]
    result = (own - cross - cross_t) * scale
    norm[0] = result[0:4, 0:4]
    norm[1] = result[0:4, 4:8]

    row = lax.broadcasted_iota(jnp.int32, (width, 128), 0)
    column = lax.broadcasted_iota(jnp.int32, (width, 128), 1)
    wanted = ((row & 4) == 0) & (column == (row & 7) * 32 + lax.shift_right_logical(row, 3))
    chosen = jnp.dot(
        mix, jnp.where(wanted, 1.0, 0.0), preferred_element_type=f32, precision=highest
    )
    blocks = coef.shape[3]
    for k in range(4):
        moved = pltpu.roll(chosen, (128 - 32 * k) % 128, 1)
        coef[0, k] = moved[0:4, 0:blocks]
        coef[1, k] = moved[4:8, 0:blocks]

    mix_high, mix_low = split(mix[:, :count])
    both = jnp.concatenate([mix_high, mix_low], 0)
    for k in range(points // chunk):
        cut = slice(k * chunk, (k + 1) * chunk)
        if k * chunk < half:
            columns = kept[:, cut]
        else:
            later = k - half // chunk
            copies[later].wait()
            columns = held[:, later * chunk : (later + 1) * chunk]
        top, rest = split(columns)
        first = jnp.dot(both, top, preferred_element_type=f32)
        second = jnp.dot(mix_high, rest, preferred_element_type=f32)
        each = chunk // width
        field = jnp.concatenate(
            [join_halves(shared[each * k + i, 0:16, :]) for i in range(each)], 1
        )
        new[:, cut] = field - (first[:8] + first[8:] + second)


def gather_all(x, axis):
    length = lax.axis_size(axis)
    return lax.all_to_all(jnp.broadcast_to(x[None], (length, *x.shape)), axis, 0, 0, tiled=True)


VMEM = pl.BlockSpec(memory_space=pltpu.VMEM)
SMEM = pl.BlockSpec(memory_space=pltpu.SMEM)
HBM = pl.BlockSpec(memory_space=pltpu.HBM)


def params(room=16 << 20):
    return pltpu.CompilerParams(vmem_limit_bytes=room)


def cost(flops, size):
    return pl.CostEstimate(flops=flops, bytes_accessed=size, transcendentals=0)


def local(krylov_basis, lattice, strength_index, strength_table):
    blocks, channels, points = krylov_basis.shape
    inc = channels // 2
    count = blocks * channels
    rows = lax.axis_size("row")
    groups = lax.axis_size("grp")
    parts = lax.axis_size(("col", "grp"))
    total = points * rows
    own = points // parts
    wide = own * groups
    length = points // groups
    flat = krylov_basis.reshape(count, points)
    spread, ready = pl.pallas_call(
        prepare_kernel,
        in_specs=[HBM, HBM, HBM, HBM],
        out_specs=(VMEM, VMEM),
        out_shape=(
            jax.ShapeDtypeStruct((rows, 16, length), bf16),
            jax.ShapeDtypeStruct((16, length + wide), bf16),
        ),
        scratch_shapes=[
            pltpu.VMEM((channels, length), f32),
            pltpu.VMEM((1, length), jnp.int32),
            pltpu.VMEM((1, strength_table.shape[0]), f32),
            pltpu.VMEM((3, length), jnp.int32),
            pltpu.VMEM((3, wide), jnp.int32),
            pltpu.SemaphoreType.DMA((5,)),
        ],
        compiler_params=params((64 << 20) - (64 << 10)),
        name="prepare",
    )(flat, lattice, strength_index[None, :], strength_table[None, :])
    gathered = lax.all_to_all(spread, "row", 0, 0, tiled=True)

    half = jax.ShapeDtypeStruct((channels, own), f32)
    held = pltpu.VMEM((2, STEP, wide), f32)
    begun, gram, direction, high, low, kept = pl.pallas_call(
        local_kernel,
        in_specs=[VMEM, HBM],
        out_specs=(VMEM,) * 6,
        out_shape=(
            jax.ShapeDtypeStruct((16, wide), f32),
            jax.ShapeDtypeStruct((16, 128), f32),
            half,
            jax.ShapeDtypeStruct((count, own), bf16),
            jax.ShapeDtypeStruct((count, own), bf16),
            jax.ShapeDtypeStruct((count, points // 2), f32),
        ),
        scratch_shapes=[
            held,
            pltpu.VMEM((count, points // 2), f32),
            pltpu.VMEM((count, points), bf16),
            pltpu.VMEM((count, points), bf16),
            pltpu.SemaphoreType.DMA((9,)),
        ],
        compiler_params=params(50 << 20),
        cost_estimate=cost(5_000_000_000, 8_000_000),
        name="scatter_local",
    )(ready, flat)

    keep, send = pl.pallas_call(
        remote_kernel,
        out_shape=(half, half),
        in_specs=[VMEM, VMEM, VMEM],
        out_specs=(VMEM, VMEM),
        scratch_shapes=[held, pltpu.VMEM((16, wide), f32)],
        compiler_params=params(),
        cost_estimate=cost(20_000_000_000, 800_000),
        name="scatter_remote",
    )(ready, gathered, begun)
    got = lax.ppermute(send, "grp", [(i, groups - 1 - i) for i in range(groups)])

    initial, partial = pl.pallas_call(
        project_kernel,
        in_specs=[VMEM] * 6,
        out_specs=(VMEM, VMEM),
        out_shape=(jax.ShapeDtypeStruct((16, 128), f32), jax.ShapeDtypeStruct((24, 128), f32)),
        compiler_params=params(),
        name="project",
    )(keep, got, direction, high, low, gram)

    row_sums = jnp.sum(gather_all(partial, "row"), axis=0)
    shared = gather_all(jnp.concatenate([initial, row_sums], 0), ("col", "grp"))

    new_block, coef, norm = pl.pallas_call(
        functools.partial(final_kernel, total),
        in_specs=[VMEM, VMEM, HBM],
        out_specs=(VMEM, VMEM, VMEM),
        out_shape=(
            jax.ShapeDtypeStruct((channels, points), f32),
            jax.ShapeDtypeStruct((2, inc, inc, blocks), f32),
            jax.ShapeDtypeStruct((2, inc, inc), f32),
        ),
        scratch_shapes=[
            pltpu.VMEM((256, 256), f32),
            pltpu.VMEM((count, points // 2), f32),
            pltpu.SemaphoreType.DMA((points // 2 // 512,)),
        ],
        compiler_params=params(50 << 20),
        name="finish",
    )(shared, kept, flat)
    return new_block, coef.transpose(3, 0, 1, 2), norm


def solution(mesh):
    in_specs = (P(None, None, "row"), P(None, "row"), P("row"), P())
    out_specs = (P(None, "row"), P(), P())
    return jax.shard_map(local, mesh=mesh, in_specs=in_specs, out_specs=out_specs, check_vma=False)
```

```python
import functools

import jax
import jax.numpy as jnp
import numpy as np
from jax import lax
from jax.experimental import pallas as pl
from jax.experimental.pallas import tpu as pltpu
from jax.sharding import PartitionSpec as P

f32 = jnp.float32
bf16 = jnp.bfloat16
highest = lax.Precision.HIGHEST
NT = (((1,), (1,)), ((), ()))
TN = (((0,), (0,)), ((), ()))

SINE = (4.4428816249751035, -7.307782340256801, 3.5971494246649565, -0.7893218692014636)
SUB = 256
STEP = 512


def green_pair(squared, masked):
    if masked:
        distinct = squared > 0.5
        squared = jnp.maximum(squared, 1.0)
    inverse = lax.rsqrt(squared)
    turns = (squared * inverse) * np.float32(1.0 / np.pi)
    part = turns - jnp.round(turns)
    z = part * part
    poly = z * np.float32(SINE[3]) + np.float32(SINE[2])
    poly = poly * z + np.float32(SINE[1])
    poly = poly * z + np.float32(SINE[0])
    sine = part * poly
    rest = 2.0 - sine * sine
    both = rest * inverse
    real_part = both - inverse
    imag_part = (sine * both) * lax.rsqrt(rest)
    if masked:
        real_part = jnp.where(distinct, real_part, 0.0)
        imag_part = jnp.where(distinct, imag_part, 0.0)
    return real_part.astype(bf16), imag_part.astype(bf16)


def scatter_tiles(tiles, sites_of, weights_of, targets, held, acc, masked, unroll):
    width = targets.shape[1]

    def fill(i, slot):
        held[slot] = lax.dot_general(sites_of(i), targets[...], TN, preferred_element_type=f32)

    def work(i, slot):
        weights = weights_of(i)
        for k in range(width // SUB):
            cut = slice(k * SUB, (k + 1) * SUB)
            real_part, imag_part = green_pair(held[slot, :, cut], masked)
            acc[0:8, cut] += jnp.dot(weights, real_part, preferred_element_type=f32)
            acc[8:16, cut] += jnp.dot(weights, imag_part, preferred_element_type=f32)

    fill(0, 0)

    def body(h, carry):
        for u in range(unroll):
            i = unroll * h + u
            fill(jnp.minimum(i + 1, tiles - 1), 1 - u % 2)
            work(i, u % 2)
        return carry

    lax.fori_loop(0, tiles // unroll, body, 0)


def remote_kernel(ready, sources, begun, keep, send, held, acc, spots):
    rows, _, length = spots.shape
    per_row = length // STEP
    row = lax.axis_index("row")
    targets = ready.at[8:16, length:]
    acc[...] = begun[...]
    width = length // 8

    def spread_sites(c, carry):
        x, y, z = [
            sources[c, :, length + k * width : length + (k + 1) * width].astype(f32)
            for k in range(3)
        ]
        norm = x * x + y * y + z * z
        high = jnp.floor(norm * np.float32(1.0 / 256.0))
        low = norm - 256.0 * high
        one = jnp.ones((2, width), f32)
        for k in range(8):
            parts = [p[k : k + 1] for p in (x, y, z, high, low)] + [one, 0.0 * one[0:1]]
            spots[c, :, k * width : (k + 1) * width] = jnp.concatenate(parts, 0).astype(bf16)
        return carry

    lax.fori_loop(0, rows, spread_sites, 0)

    def where(i):
        chunk = lax.rem(row + 1 + i // per_row, rows)
        return chunk, pl.ds(pl.multiple_of(lax.rem(i, per_row) * STEP, STEP), STEP)

    def sites_of(i):
        chunk, cut = where(i)
        return spots[chunk, :, cut]

    def weights_of(i):
        chunk, cut = where(i)
        return sources[chunk, :, cut]

    scatter_tiles((rows - 1) * per_row, sites_of, weights_of, targets, held, acc, False, 4)
    real = acc[0:8]
    imag = acc[8:16]
    upper = real[0:4] - imag[4:8]
    lower = real[4:8] + imag[0:4]
    both = jnp.concatenate([upper, lower], 0)
    half = both.shape[1] // 2
    first, second = both[:, :half], both[:, half:]
    mine = lax.axis_index("grp") == 0
    keep[...] = jnp.where(mine, first, second)
    send[...] = jnp.where(mine, second, first)


def split(x):
    high = x.astype(bf16)
    return high, (x - high.astype(f32)).astype(bf16)


def swap_parts(x, rows):
    lane = lax.broadcasted_iota(jnp.int32, x.shape, 1)
    width = x.shape[1]
    rolled = pltpu.roll(x, rows - 4, 0)
    return jnp.where((lane & 4) == 0, pltpu.roll(rolled, width - 4, 1), pltpu.roll(rolled, 4, 1))


def complex_mix(products):
    lane = lax.broadcasted_iota(jnp.int32, products.shape, 1)
    sub = lax.broadcasted_iota(jnp.int32, products.shape, 0)
    swapped = swap_parts(products, products.shape[0])
    same = ((lane & 4) == 0) == ((sub & 4) == 0)
    return products + jnp.where(same, swapped, -swapped)


def prepare_kernel(basis, lattice, index, table, spread, ready, *scratch):
    direction, chosen, held_table, points, aims, sems = scratch
    rows = spread.shape[0]
    length = points.shape[1]
    wide = aims.shape[1]
    channels = direction.shape[0]
    aim = pl.multiple_of(lax.axis_index("col") * wide, 128)
    start = pl.multiple_of(lax.axis_index("grp") * length, 128)
    last = basis.shape[0] - channels
    copies = [
        pltpu.make_async_copy(lattice.at[:, pl.ds(start, length)], points, sems.at[0]),
        pltpu.make_async_copy(index.at[:, pl.ds(start, length)], chosen, sems.at[1]),
        pltpu.make_async_copy(table, held_table, sems.at[2]),
        pltpu.make_async_copy(
            basis.at[last : last + channels, pl.ds(start, length)], direction, sems.at[3]
        ),
        pltpu.make_async_copy(lattice.at[:, pl.ds(aim, wide)], aims, sems.at[4]),
    ]
    for copy in copies:
        copy.start()

    def shared_rows(part):
        x, y, z = part[0:1], part[1:2], part[2:3]
        norm = x * x + y * y + z * z
        return x, y, z, lax.shift_right_logical(norm, 8), norm & 255, jnp.ones_like(x)

    def stacked(parts):
        return jnp.concatenate([p.astype(f32) for p in parts], 0)

    copies[0].wait()
    x, y, z, high, low, one = shared_rows(points[...])
    sites = stacked([x, y, z, high, low, one, one, 0 * one])
    copies[1].wait()
    copies[2].wait()
    strength = jnp.zeros(chosen.shape, f32)
    for k in range(table.shape[1]):
        strength = jnp.where(chosen[...] == k, held_table[0:1, k : k + 1], strength)
    copies[3].wait()
    weighted = (direction[...] * strength).astype(bf16)
    ready[0:8, :length] = weighted
    ready[8:16, :length] = sites.astype(bf16)
    width = length // 8
    dense = [
        jnp.concatenate([sites[p : p + 1, k * width : (k + 1) * width] for k in range(8)], 0)
        for p in range(3)
    ]
    packed = jnp.concatenate([weighted] + [d.astype(bf16) for d in dense], 1)
    for k in range(rows):
        spread[k] = packed
    copies[4].wait()
    x, y, z, high, low, one = shared_rows(aims[...])
    sites = stacked([-2 * x, -2 * y, -2 * z, 256 * one, one, 256 * high, low, 0 * one])
    ready[:, length:] = jnp.concatenate([jnp.zeros_like(sites), sites], 0).astype(bf16)


def local_kernel(ready, basis, *rest):
    acc, gram, direction, own_high, own_low, kept, tiles, held, high, low, sems = rest
    half = kept.shape[1]
    length = ready.shape[1] - tiles.shape[2]
    targets = ready.at[8:16, length:]
    part = lax.axis_index(("col", "grp"))
    count, points = basis.shape
    pieces = sems.shape[0] - 1
    chunk = points // pieces
    channels, width = direction.shape
    here = pl.ds(pl.multiple_of(part * width, 128), width)
    own = pltpu.make_async_copy(
        basis.at[count - channels : count, here], direction, sems.at[pieces]
    )
    own.start()
    start = pl.multiple_of(jnp.minimum(part * 16, count - 16), 16)

    def place_of(k):
        first = k * chunk
        if first < half:
            return kept.at[:, first : first + chunk]
        return held.at[:, first - half : first - half + chunk]

    copies = []
    for k in range(points // chunk):
        cut = slice(k * chunk, (k + 1) * chunk)
        copies.append(pltpu.make_async_copy(basis.at[:, cut], place_of(k), sems.at[k]))
        copies[-1].start()

    acc[...] = jnp.zeros_like(acc)

    def sites_of(i):
        return ready[8:16, pl.ds(pl.multiple_of(i * STEP, STEP), STEP)]

    def weights_of(i):
        return ready[0:8, pl.ds(pl.multiple_of(i * STEP, STEP), STEP)]

    scatter_tiles(length // STEP, sites_of, weights_of, targets, tiles, acc, True, 2)

    total = jnp.zeros((16, count), f32)
    for k in range(points // chunk):
        cut = slice(k * chunk, (k + 1) * chunk)
        copies[k].wait()
        top, rest = split(place_of(k)[...])
        high[:, cut] = top
        low[:, cut] = rest
        mine = jnp.concatenate([high[pl.ds(start, 16), cut], low[pl.ds(start, 16), cut]], 0)
        first = lax.dot_general(mine, top, NT, preferred_element_type=f32)
        second = lax.dot_general(mine[:16], rest, NT, preferred_element_type=f32)
        total = total + (first[:16] + first[16:] + second)
    total = jnp.concatenate([total, jnp.zeros((16, 256 - count), f32)], 1)
    mixed = complex_mix(total)
    gram[...] = stack_halves(jnp.concatenate([mixed[0:4], mixed[8:12]], 0))
    own.wait()
    own_high[...] = high[:, here]
    own_low[...] = low[:, here]


def stack_halves(x):
    return jnp.concatenate([x[:, :128], x[:, 128:]], 0)


def join_halves(x):
    rows = x.shape[0] // 2
    return jnp.concatenate([x[:rows], x[rows:]], 1)


def project_kernel(keep, got, direction, high, low, gram, initial, packed):
    field = direction[...] - (keep[...] + got[...])
    initial[...] = stack_halves(field)
    count = high.shape[0]
    field_high, field_low = split(field)
    both = jnp.concatenate([field_high, field_low], 0)
    first = lax.dot_general(both, high[...], NT, preferred_element_type=f32)
    second = lax.dot_general(field_high, low[...], NT, preferred_element_type=f32)
    own = lax.dot_general(field, field, NT, preferred_element_type=f32, precision=highest)
    rest = jnp.zeros((8, 256 - count - 8), f32)
    products = jnp.concatenate([first[:8] + first[8:] + second, own, rest], 1)
    packed[0:8, :] = stack_halves(complex_mix(products)[0:4])
    packed[8:, :] = gram[...]


def final_kernel(total, shared, kept, basis, new, coef, norm, gram_high, gram_low, held, sems):
    parts = shared.shape[0]
    count, points = basis.shape
    width = 256
    chunk = 512
    half = points - held.shape[1]
    copies = []
    for k in range(sems.shape[0]):
        cut = slice(k * chunk, (k + 1) * chunk)
        there = slice(half + k * chunk, half + (k + 1) * chunk)
        copies.append(pltpu.make_async_copy(basis.at[:, there], held.at[:, cut], sems.at[k]))
        copies[-1].start()
    scale = np.float32(1.0 / total)
    sums = shared[0, 16:24, :]
    for q in range(1, parts):
        sums = sums + shared[q, 16:24, :]
    upper = join_halves(sums)
    lane = lax.broadcasted_iota(jnp.int32, upper.shape, 1)
    lower = jnp.where(
        (lane & 4) == 0, -pltpu.roll(upper, width - 4, 1), pltpu.roll(upper, 4, 1)
    )
    sums = jnp.concatenate([upper, lower], 0)
    lane = lax.broadcasted_iota(jnp.int32, sums.shape, 1)
    sub = lax.broadcasted_iota(jnp.int32, sums.shape, 0)
    gram_high[...] = jnp.zeros_like(gram_high)
    gram_low[...] = jnp.zeros_like(gram_low)
    for q in range(count // 16):
        part = join_halves(shared[q, 24:40, :])
        pair = jnp.concatenate(
            [jnp.where(sub < 4, part, 0.0), jnp.where(sub < 4, pltpu.roll(part, 4, 0), 0.0)], 0
        )
        top, rest = split(pair)
        gram_high[16 * q : 16 * q + 16, :] = top
        gram_low[16 * q : 16 * q + 16, :] = rest

    def times_gram(x):
        top, rest = split(x)
        first = jnp.dot(
            jnp.concatenate([top, rest], 0), gram_high[...], preferred_element_type=f32
        )
        second = jnp.dot(top, gram_low[...], preferred_element_type=f32)
        return complex_mix(first[:8] + first[8:] + second)

    products = jnp.where(lane < count, sums, 0.0)
    once = products * scale
    mix = 2.0 * once - times_gram(once) * scale
    mix_high, mix_low = split(mix[:, :count])
    both = jnp.concatenate([mix_high, mix_low], 0)
    for k in range(points // chunk):
        cut = slice(k * chunk, (k + 1) * chunk)
        if k * chunk < half:
            columns = kept[:, cut]
        else:
            later = k - half // chunk
            copies[later].wait()
            columns = held[:, later * chunk : (later + 1) * chunk]
        top, rest = split(columns)
        first = jnp.dot(both, top, preferred_element_type=f32)
        second = jnp.dot(mix_high, rest, preferred_element_type=f32)
        each = chunk // width
        field = jnp.concatenate(
            [join_halves(shared[each * k + i, 0:16, :]) for i in range(each)], 1
        )
        new[:, cut] = field - (first[:8] + first[8:] + second)

    seen = products - 0.5 * times_gram(mix)
    cross = lax.dot_general(mix, seen, NT, preferred_element_type=f32, precision=highest)
    cross_t = lax.dot_general(seen, mix, NT, preferred_element_type=f32, precision=highest)
    own = pltpu.roll(sums, width - count, 1)[:, 0:8]
    result = (own - cross - cross_t) * scale
    norm[0] = result[0:4, 0:4]
    norm[1] = result[0:4, 4:8]

    row = lax.broadcasted_iota(jnp.int32, (width, 128), 0)
    column = lax.broadcasted_iota(jnp.int32, (width, 128), 1)
    wanted = ((row & 4) == 0) & (column == (row & 7) * 32 + lax.shift_right_logical(row, 3))
    top, rest = split(mix)
    least = (mix - top.astype(f32) - rest.astype(f32)).astype(bf16)
    chosen = jnp.dot(
        jnp.concatenate([top, rest, least], 0),
        jnp.where(wanted, 1.0, 0.0).astype(bf16),
        preferred_element_type=f32,
    )
    chosen = chosen[:8] + chosen[8:16] + chosen[16:]
    blocks = coef.shape[3]
    for k in range(4):
        moved = pltpu.roll(chosen, (128 - 32 * k) % 128, 1)
        coef[0, k] = moved[0:4, 0:blocks]
        coef[1, k] = moved[4:8, 0:blocks]


def gather_all(x, axis):
    length = lax.axis_size(axis)
    return lax.all_to_all(jnp.broadcast_to(x[None], (length, *x.shape)), axis, 0, 0, tiled=True)


VMEM = pl.BlockSpec(memory_space=pltpu.VMEM)
SMEM = pl.BlockSpec(memory_space=pltpu.SMEM)
HBM = pl.BlockSpec(memory_space=pltpu.HBM)


def params(room=16 << 20):
    return pltpu.CompilerParams(vmem_limit_bytes=room)


def cost(flops, size):
    return pl.CostEstimate(flops=flops, bytes_accessed=size, transcendentals=0)


def local(krylov_basis, lattice, strength_index, strength_table):
    blocks, channels, points = krylov_basis.shape
    inc = channels // 2
    count = blocks * channels
    rows = lax.axis_size("row")
    groups = lax.axis_size("grp")
    parts = lax.axis_size(("col", "grp"))
    total = points * rows
    own = points // parts
    wide = own * groups
    length = points // groups
    flat = krylov_basis.reshape(count, points)
    spread, ready = pl.pallas_call(
        prepare_kernel,
        in_specs=[HBM, HBM, HBM, HBM],
        out_specs=(VMEM, VMEM),
        out_shape=(
            jax.ShapeDtypeStruct((rows, 8, length + 3 * (length // 8)), bf16),
            jax.ShapeDtypeStruct((16, length + wide), bf16),
        ),
        scratch_shapes=[
            pltpu.VMEM((channels, length), f32),
            pltpu.VMEM((1, length), jnp.int32),
            pltpu.VMEM((1, strength_table.shape[0]), f32),
            pltpu.VMEM((3, length), jnp.int32),
            pltpu.VMEM((3, wide), jnp.int32),
            pltpu.SemaphoreType.DMA((5,)),
        ],
        compiler_params=params((64 << 20) - (64 << 10)),
        name="prepare",
    )(flat, lattice, strength_index[None, :], strength_table[None, :])
    gathered = lax.all_to_all(spread, "row", 0, 0, tiled=True)

    half = jax.ShapeDtypeStruct((channels, own), f32)
    held = pltpu.VMEM((2, STEP, wide), f32)
    begun, gram, direction, high, low, kept = pl.pallas_call(
        local_kernel,
        in_specs=[VMEM, HBM],
        out_specs=(VMEM,) * 6,
        out_shape=(
            jax.ShapeDtypeStruct((16, wide), f32),
            jax.ShapeDtypeStruct((16, 128), f32),
            half,
            jax.ShapeDtypeStruct((count, own), bf16),
            jax.ShapeDtypeStruct((count, own), bf16),
            jax.ShapeDtypeStruct((count, points // 2), f32),
        ),
        scratch_shapes=[
            held,
            pltpu.VMEM((count, points // 2), f32),
            pltpu.VMEM((count, points), bf16),
            pltpu.VMEM((count, points), bf16),
            pltpu.SemaphoreType.DMA((9,)),
        ],
        compiler_params=params(50 << 20),
        cost_estimate=cost(5_000_000_000, 8_000_000),
        name="scatter_local",
    )(ready, flat)

    keep, send = pl.pallas_call(
        remote_kernel,
        out_shape=(half, half),
        in_specs=[VMEM, VMEM, VMEM],
        out_specs=(VMEM, VMEM),
        scratch_shapes=[
            held,
            pltpu.VMEM((16, wide), f32),
            pltpu.VMEM((rows, 8, length), bf16),
        ],
        compiler_params=params(),
        cost_estimate=cost(20_000_000_000, 800_000),
        name="scatter_remote",
    )(ready, gathered, begun)
    got = lax.ppermute(send, "grp", [(i, groups - 1 - i) for i in range(groups)])

    initial, partial = pl.pallas_call(
        project_kernel,
        in_specs=[VMEM] * 6,
        out_specs=(VMEM, VMEM),
        out_shape=(jax.ShapeDtypeStruct((16, 128), f32), jax.ShapeDtypeStruct((24, 128), f32)),
        compiler_params=params(),
        name="project",
    )(keep, got, direction, high, low, gram)

    row_sums = jnp.sum(gather_all(partial, "row"), axis=0)
    shared = gather_all(jnp.concatenate([initial, row_sums], 0), ("col", "grp"))

    new_block, coef, norm = pl.pallas_call(
        functools.partial(final_kernel, total),
        in_specs=[VMEM, VMEM, HBM],
        out_specs=(VMEM, VMEM, VMEM),
        out_shape=(
            jax.ShapeDtypeStruct((channels, points), f32),
            jax.ShapeDtypeStruct((2, inc, inc, blocks), f32),
            jax.ShapeDtypeStruct((2, inc, inc), f32),
        ),
        scratch_shapes=[
            pltpu.VMEM((256, 256), bf16),
            pltpu.VMEM((256, 256), bf16),
            pltpu.VMEM((count, points // 2), f32),
            pltpu.SemaphoreType.DMA((points // 2 // 512,)),
        ],
        compiler_params=params(50 << 20),
        name="finish",
    )(shared, kept, flat)
    return new_block, coef.transpose(3, 0, 1, 2), norm


def solution(mesh):
    in_specs = (P(None, None, "row"), P(None, "row"), P("row"), P())
    out_specs = (P(None, "row"), P(), P())
    return jax.shard_map(local, mesh=mesh, in_specs=in_specs, out_specs=out_specs, check_vma=False)
```

```python
import functools

import jax
import jax.numpy as jnp
import numpy as np
from jax import lax
from jax.experimental import pallas as pl
from jax.experimental.pallas import tpu as pltpu
from jax.sharding import PartitionSpec as P

f32 = jnp.float32
bf16 = jnp.bfloat16
highest = lax.Precision.HIGHEST
NT = (((1,), (1,)), ((), ()))
TN = (((0,), (0,)), ((), ()))

SINE = (4.4428816249751035, -7.307782340256801, 3.5971494246649565, -0.7893218692014636)
SUB = 256
STEP = 512


def green_pair(squared, masked):
    if masked:
        distinct = squared > 0.5
        squared = jnp.maximum(squared, 1.0)
    inverse = lax.rsqrt(squared)
    turns = (squared * inverse) * np.float32(1.0 / np.pi)
    part = turns - jnp.round(turns)
    z = part * part
    poly = z * np.float32(SINE[3]) + np.float32(SINE[2])
    poly = poly * z + np.float32(SINE[1])
    poly = poly * z + np.float32(SINE[0])
    sine = part * poly
    rest = 2.0 - sine * sine
    both = rest * inverse
    real_part = both - inverse
    imag_part = (sine * both) * lax.rsqrt(rest)
    if masked:
        real_part = jnp.where(distinct, real_part, 0.0)
        imag_part = jnp.where(distinct, imag_part, 0.0)
    return real_part.astype(bf16), imag_part.astype(bf16)


def scatter_tiles(tiles, sites_of, weights_of, targets, held, acc, masked, unroll):
    width = targets.shape[1]

    def fill(i, slot):
        held[slot] = lax.dot_general(sites_of(i), targets[...], TN, preferred_element_type=f32)

    def work(i, slot):
        weights = weights_of(i)
        for k in range(width // SUB):
            cut = slice(k * SUB, (k + 1) * SUB)
            real_part, imag_part = green_pair(held[slot, :, cut], masked)
            acc[0:8, cut] += jnp.dot(weights, real_part, preferred_element_type=f32)
            acc[8:16, cut] += jnp.dot(weights, imag_part, preferred_element_type=f32)

    fill(0, 0)

    def body(h, carry):
        for u in range(unroll):
            i = unroll * h + u
            fill(jnp.minimum(i + 1, tiles - 1), 1 - u % 2)
            work(i, u % 2)
        return carry

    lax.fori_loop(0, tiles // unroll, body, 0)


def remote_kernel(ready, sources, begun, keep, send, held, acc, spots):
    rows, _, length = spots.shape
    per_row = length // STEP
    row = lax.axis_index("row")
    targets = ready.at[8:16, length:]
    acc[...] = begun[...]
    width = length // 8

    def spread_sites(c, carry):
        x, y, z = [
            sources[c, :, length + k * width : length + (k + 1) * width].astype(f32)
            for k in range(3)
        ]
        norm = x * x + y * y + z * z
        high = jnp.floor(norm * np.float32(1.0 / 256.0))
        low = norm - 256.0 * high
        one = jnp.ones((2, width), f32)
        for k in range(8):
            parts = [p[k : k + 1] for p in (x, y, z, high, low)] + [one, 0.0 * one[0:1]]
            spots[c, :, k * width : (k + 1) * width] = jnp.concatenate(parts, 0).astype(bf16)
        return carry

    lax.fori_loop(0, rows, spread_sites, 0)

    def where(i):
        chunk = lax.rem(row + 1 + i // per_row, rows)
        return chunk, pl.ds(pl.multiple_of(lax.rem(i, per_row) * STEP, STEP), STEP)

    def sites_of(i):
        chunk, cut = where(i)
        return spots[chunk, :, cut]

    def weights_of(i):
        chunk, cut = where(i)
        return sources[chunk, :, cut]

    scatter_tiles((rows - 1) * per_row, sites_of, weights_of, targets, held, acc, False, 4)
    real = acc[0:8]
    imag = acc[8:16]
    upper = real[0:4] - imag[4:8]
    lower = real[4:8] + imag[0:4]
    both = jnp.concatenate([upper, lower], 0)
    half = both.shape[1] // 2
    first, second = both[:, :half], both[:, half:]
    mine = lax.axis_index("grp") == 0
    keep[...] = jnp.where(mine, first, second)
    send[...] = jnp.where(mine, second, first)


def split(x):
    high = x.astype(bf16)
    return high, (x - high.astype(f32)).astype(bf16)


def swap_parts(x, rows):
    lane = lax.broadcasted_iota(jnp.int32, x.shape, 1)
    width = x.shape[1]
    rolled = pltpu.roll(x, rows - 4, 0)
    return jnp.where((lane & 4) == 0, pltpu.roll(rolled, width - 4, 1), pltpu.roll(rolled, 4, 1))


def complex_mix(products):
    lane = lax.broadcasted_iota(jnp.int32, products.shape, 1)
    sub = lax.broadcasted_iota(jnp.int32, products.shape, 0)
    swapped = swap_parts(products, products.shape[0])
    same = ((lane & 4) == 0) == ((sub & 4) == 0)
    return products + jnp.where(same, swapped, -swapped)


def prepare_kernel(basis, lattice, index, table, spread, ready, *scratch):
    direction, chosen, held_table, points, aims, sems = scratch
    rows = spread.shape[0]
    length = points.shape[1]
    wide = aims.shape[1]
    channels = direction.shape[0]
    aim = pl.multiple_of(lax.axis_index("col") * wide, 128)
    start = pl.multiple_of(lax.axis_index("grp") * length, 128)
    last = basis.shape[0] - channels
    copies = [
        pltpu.make_async_copy(lattice.at[:, pl.ds(start, length)], points, sems.at[0]),
        pltpu.make_async_copy(index.at[:, pl.ds(start, length)], chosen, sems.at[1]),
        pltpu.make_async_copy(table, held_table, sems.at[2]),
        pltpu.make_async_copy(
            basis.at[last : last + channels, pl.ds(start, length)], direction, sems.at[3]
        ),
        pltpu.make_async_copy(lattice.at[:, pl.ds(aim, wide)], aims, sems.at[4]),
    ]
    for copy in copies:
        copy.start()

    def shared_rows(part):
        x, y, z = part[0:1], part[1:2], part[2:3]
        norm = x * x + y * y + z * z
        return x, y, z, lax.shift_right_logical(norm, 8), norm & 255, jnp.ones_like(x)

    def stacked(parts):
        return jnp.concatenate([p.astype(f32) for p in parts], 0)

    copies[0].wait()
    x, y, z, high, low, one = shared_rows(points[...])
    sites = stacked([x, y, z, high, low, one, one, 0 * one])
    copies[1].wait()
    copies[2].wait()
    strength = jnp.zeros(chosen.shape, f32)
    for k in range(table.shape[1]):
        strength = jnp.where(chosen[...] == k, held_table[0:1, k : k + 1], strength)
    copies[3].wait()
    weighted = (direction[...] * strength).astype(bf16)
    ready[0:8, :length] = weighted
    ready[8:16, :length] = sites.astype(bf16)
    width = length // 8
    dense = [
        jnp.concatenate([sites[p : p + 1, k * width : (k + 1) * width] for k in range(8)], 0)
        for p in range(3)
    ]
    packed = jnp.concatenate([weighted] + [d.astype(bf16) for d in dense], 1)
    for k in range(rows):
        spread[k] = packed
    copies[4].wait()
    x, y, z, high, low, one = shared_rows(aims[...])
    sites = stacked([-2 * x, -2 * y, -2 * z, 256 * one, one, 256 * high, low, 0 * one])
    ready[:, length:] = jnp.concatenate([jnp.zeros_like(sites), sites], 0).astype(bf16)


def local_kernel(ready, basis, *rest):
    acc, gram, direction, own_high, own_low, kept, tiles, held, high, low, sems = rest
    half = kept.shape[1]
    length = ready.shape[1] - tiles.shape[2]
    targets = ready.at[8:16, length:]
    part = lax.axis_index(("col", "grp"))
    count, points = basis.shape
    pieces = sems.shape[0] - 1
    chunk = points // pieces
    channels, width = direction.shape
    here = pl.ds(pl.multiple_of(part * width, 128), width)
    own = pltpu.make_async_copy(
        basis.at[count - channels : count, here], direction, sems.at[pieces]
    )
    own.start()
    start = pl.multiple_of(jnp.minimum(part * 16, count - 16), 16)

    def place_of(k):
        first = k * chunk
        if first < half:
            return kept.at[:, first : first + chunk]
        return held.at[:, first - half : first - half + chunk]

    copies = []
    for k in range(points // chunk):
        cut = slice(k * chunk, (k + 1) * chunk)
        copies.append(pltpu.make_async_copy(basis.at[:, cut], place_of(k), sems.at[k]))
        copies[-1].start()

    acc[...] = jnp.zeros_like(acc)

    def sites_of(i):
        return ready[8:16, pl.ds(pl.multiple_of(i * STEP, STEP), STEP)]

    def weights_of(i):
        return ready[0:8, pl.ds(pl.multiple_of(i * STEP, STEP), STEP)]

    scatter_tiles(length // STEP, sites_of, weights_of, targets, tiles, acc, True, 2)

    total = jnp.zeros((16, count), f32)
    for k in range(points // chunk):
        cut = slice(k * chunk, (k + 1) * chunk)
        copies[k].wait()
        top, rest = split(place_of(k)[...])
        high[:, cut] = top
        low[:, cut] = rest
        mine = jnp.concatenate([high[pl.ds(start, 16), cut], low[pl.ds(start, 16), cut]], 0)
        first = lax.dot_general(mine, top, NT, preferred_element_type=f32)
        second = lax.dot_general(mine[:16], rest, NT, preferred_element_type=f32)
        total = total + (first[:16] + first[16:] + second)
    total = jnp.concatenate([total, jnp.zeros((16, 256 - count), f32)], 1)
    mixed = complex_mix(total)
    gram[...] = stack_halves(jnp.concatenate([mixed[0:4], mixed[8:12]], 0))
    own.wait()
    own_high[...] = high[:, here]
    own_low[...] = low[:, here]


def stack_halves(x):
    return jnp.concatenate([x[:, :128], x[:, 128:]], 0)


def join_halves(x):
    rows = x.shape[0] // 2
    return jnp.concatenate([x[:rows], x[rows:]], 1)


def project_kernel(keep, got, direction, high, low, gram, initial, packed):
    field = direction[...] - (keep[...] + got[...])
    initial[...] = stack_halves(field)
    count = high.shape[0]
    field_high, field_low = split(field)
    both = jnp.concatenate([field_high, field_low], 0)
    first = lax.dot_general(both, high[...], NT, preferred_element_type=f32)
    second = lax.dot_general(field_high, low[...], NT, preferred_element_type=f32)
    own = lax.dot_general(field, field, NT, preferred_element_type=f32, precision=highest)
    rest = jnp.zeros((8, 256 - count - 8), f32)
    products = jnp.concatenate([first[:8] + first[8:] + second, own, rest], 1)
    packed[0:8, :] = stack_halves(complex_mix(products)[0:4])
    packed[8:, :] = gram[...]


def final_kernel(total, shared, kept, basis, new, coef, norm, *scratch):
    gram_high, gram_low, held, result, sems, out_sems = scratch
    parts = shared.shape[0]
    count, points = basis.shape
    width = 256
    chunk = 512
    half = points - held.shape[1]
    copies = []
    for k in range(sems.shape[0]):
        cut = slice(k * chunk, (k + 1) * chunk)
        there = slice(half + k * chunk, half + (k + 1) * chunk)
        copies.append(pltpu.make_async_copy(basis.at[:, there], held.at[:, cut], sems.at[k]))
        copies[-1].start()
    scale = np.float32(1.0 / total)
    sums = shared[0, 16:24, :]
    for q in range(1, parts):
        sums = sums + shared[q, 16:24, :]
    upper = join_halves(sums)
    lane = lax.broadcasted_iota(jnp.int32, upper.shape, 1)
    lower = jnp.where(
        (lane & 4) == 0, -pltpu.roll(upper, width - 4, 1), pltpu.roll(upper, 4, 1)
    )
    sums = jnp.concatenate([upper, lower], 0)
    lane = lax.broadcasted_iota(jnp.int32, sums.shape, 1)
    sub = lax.broadcasted_iota(jnp.int32, sums.shape, 0)
    gram_high[...] = jnp.zeros_like(gram_high)
    gram_low[...] = jnp.zeros_like(gram_low)
    for q in range(count // 16):
        part = join_halves(shared[q, 24:40, :])
        pair = jnp.concatenate(
            [jnp.where(sub < 4, part, 0.0), jnp.where(sub < 4, pltpu.roll(part, 4, 0), 0.0)], 0
        )
        top, rest = split(pair)
        gram_high[16 * q : 16 * q + 16, :] = top
        gram_low[16 * q : 16 * q + 16, :] = rest

    def times_gram(x):
        top, rest = split(x)
        first = jnp.dot(
            jnp.concatenate([top, rest], 0), gram_high[...], preferred_element_type=f32
        )
        second = jnp.dot(top, gram_low[...], preferred_element_type=f32)
        return complex_mix(first[:8] + first[8:] + second)

    products = jnp.where(lane < count, sums, 0.0)
    once = products * scale
    mix = 2.0 * once - times_gram(once) * scale
    mix_high, mix_low = split(mix[:, :count])
    both = jnp.concatenate([mix_high, mix_low], 0)
    writes = []
    for k in range(points // chunk):
        cut = slice(k * chunk, (k + 1) * chunk)
        if k * chunk < half:
            columns = kept[:, cut]
        else:
            later = k - half // chunk
            copies[later].wait()
            columns = held[:, later * chunk : (later + 1) * chunk]
        top, rest = split(columns)
        first = jnp.dot(both, top, preferred_element_type=f32)
        second = jnp.dot(mix_high, rest, preferred_element_type=f32)
        each = chunk // width
        field = jnp.concatenate(
            [join_halves(shared[each * k + i, 0:16, :]) for i in range(each)], 1
        )
        result[:, cut] = field - (first[:8] + first[8:] + second)
        writes.append(pltpu.make_async_copy(result.at[:, cut], new.at[:, cut], out_sems.at[k]))
        writes[-1].start()

    seen = products - 0.5 * times_gram(mix)
    cross = lax.dot_general(mix, seen, NT, preferred_element_type=f32, precision=highest)
    cross_t = lax.dot_general(seen, mix, NT, preferred_element_type=f32, precision=highest)
    own = pltpu.roll(sums, width - count, 1)[:, 0:8]
    squares = (own - cross - cross_t) * scale
    norm[0] = squares[0:4, 0:4]
    norm[1] = squares[0:4, 4:8]

    row = lax.broadcasted_iota(jnp.int32, (width, 128), 0)
    column = lax.broadcasted_iota(jnp.int32, (width, 128), 1)
    wanted = ((row & 4) == 0) & (column == (row & 7) * 32 + lax.shift_right_logical(row, 3))
    top, rest = split(mix)
    least = (mix - top.astype(f32) - rest.astype(f32)).astype(bf16)
    chosen = jnp.dot(
        jnp.concatenate([top, rest, least], 0),
        jnp.where(wanted, 1.0, 0.0).astype(bf16),
        preferred_element_type=f32,
    )
    chosen = chosen[:8] + chosen[8:16] + chosen[16:]
    blocks = coef.shape[3]
    for k in range(4):
        moved = pltpu.roll(chosen, (128 - 32 * k) % 128, 1)
        coef[0, k] = moved[0:4, 0:blocks]
        coef[1, k] = moved[4:8, 0:blocks]
    for write in writes:
        write.wait()


def gather_all(x, axis):
    length = lax.axis_size(axis)
    return lax.all_to_all(jnp.broadcast_to(x[None], (length, *x.shape)), axis, 0, 0, tiled=True)


VMEM = pl.BlockSpec(memory_space=pltpu.VMEM)
SMEM = pl.BlockSpec(memory_space=pltpu.SMEM)
HBM = pl.BlockSpec(memory_space=pltpu.HBM)


def params(room=16 << 20):
    return pltpu.CompilerParams(vmem_limit_bytes=room)


def cost(flops, size):
    return pl.CostEstimate(flops=flops, bytes_accessed=size, transcendentals=0)


def local(krylov_basis, lattice, strength_index, strength_table):
    blocks, channels, points = krylov_basis.shape
    inc = channels // 2
    count = blocks * channels
    rows = lax.axis_size("row")
    groups = lax.axis_size("grp")
    parts = lax.axis_size(("col", "grp"))
    total = points * rows
    own = points // parts
    wide = own * groups
    length = points // groups
    flat = krylov_basis.reshape(count, points)
    stay = points // 2
    spread, ready = pl.pallas_call(
        prepare_kernel,
        in_specs=[HBM, HBM, HBM, HBM],
        out_specs=(VMEM, VMEM),
        out_shape=(
            jax.ShapeDtypeStruct((rows, 8, length + 3 * (length // 8)), bf16),
            jax.ShapeDtypeStruct((16, length + wide), bf16),
        ),
        scratch_shapes=[
            pltpu.VMEM((channels, length), f32),
            pltpu.VMEM((1, length), jnp.int32),
            pltpu.VMEM((1, strength_table.shape[0]), f32),
            pltpu.VMEM((3, length), jnp.int32),
            pltpu.VMEM((3, wide), jnp.int32),
            pltpu.SemaphoreType.DMA((5,)),
        ],
        compiler_params=params((64 << 20) - (64 << 10)),
        name="prepare",
    )(flat, lattice, strength_index[None, :], strength_table[None, :])
    gathered = lax.all_to_all(spread, "row", 0, 0, tiled=True)

    half = jax.ShapeDtypeStruct((channels, own), f32)
    held = pltpu.VMEM((2, STEP, wide), f32)
    begun, gram, direction, high, low, kept = pl.pallas_call(
        local_kernel,
        in_specs=[VMEM, HBM],
        out_specs=(VMEM,) * 6,
        out_shape=(
            jax.ShapeDtypeStruct((16, wide), f32),
            jax.ShapeDtypeStruct((16, 128), f32),
            half,
            jax.ShapeDtypeStruct((count, own), bf16),
            jax.ShapeDtypeStruct((count, own), bf16),
            jax.ShapeDtypeStruct((count, stay), f32),
        ),
        scratch_shapes=[
            held,
            pltpu.VMEM((count, points - stay), f32),
            pltpu.VMEM((count, points), bf16),
            pltpu.VMEM((count, points), bf16),
            pltpu.SemaphoreType.DMA((9,)),
        ],
        compiler_params=params(50 << 20),
        cost_estimate=cost(5_000_000_000, 8_000_000),
        name="scatter_local",
    )(ready, flat)

    keep, send = pl.pallas_call(
        remote_kernel,
        out_shape=(half, half),
        in_specs=[VMEM, VMEM, VMEM],
        out_specs=(VMEM, VMEM),
        scratch_shapes=[
            held,
            pltpu.VMEM((16, wide), f32),
            pltpu.VMEM((rows, 8, length), bf16),
        ],
        compiler_params=params(),
        cost_estimate=cost(20_000_000_000, 800_000),
        name="scatter_remote",
    )(ready, gathered, begun)
    got = lax.ppermute(send, "grp", [(i, groups - 1 - i) for i in range(groups)])

    initial, partial = pl.pallas_call(
        project_kernel,
        in_specs=[VMEM] * 6,
        out_specs=(VMEM, VMEM),
        out_shape=(jax.ShapeDtypeStruct((16, 128), f32), jax.ShapeDtypeStruct((24, 128), f32)),
        compiler_params=params(),
        name="project",
    )(keep, got, direction, high, low, gram)

    row_sums = jnp.sum(gather_all(partial, "row"), axis=0)
    shared = gather_all(jnp.concatenate([initial, row_sums], 0), ("col", "grp"))

    new_block, coef, norm = pl.pallas_call(
        functools.partial(final_kernel, total),
        in_specs=[VMEM, VMEM, HBM],
        out_specs=(HBM, VMEM, VMEM),
        out_shape=(
            jax.ShapeDtypeStruct((channels, points), f32),
            jax.ShapeDtypeStruct((2, inc, inc, blocks), f32),
            jax.ShapeDtypeStruct((2, inc, inc), f32),
        ),
        scratch_shapes=[
            pltpu.VMEM((256, 256), bf16),
            pltpu.VMEM((256, 256), bf16),
            pltpu.VMEM((count, points - stay), f32),
            pltpu.VMEM((channels, points), f32),
            pltpu.SemaphoreType.DMA(((points - stay) // 512,)),
            pltpu.SemaphoreType.DMA((points // 512,)),
        ],
        compiler_params=params(50 << 20),
        name="finish",
    )(shared, kept, flat)
    return new_block, coef.transpose(3, 0, 1, 2), norm


def solution(mesh):
    in_specs = (P(None, None, "row"), P(None, "row"), P("row"), P())
    out_specs = (P(None, "row"), P(), P())
    return jax.shard_map(local, mesh=mesh, in_specs=in_specs, out_specs=out_specs, check_vma=False)
```

```python
import functools

import jax
import jax.numpy as jnp
import numpy as np
from jax import lax
from jax.experimental import pallas as pl
from jax.experimental.pallas import tpu as pltpu
from jax.sharding import PartitionSpec as P

f32 = jnp.float32
bf16 = jnp.bfloat16
highest = lax.Precision.HIGHEST
NT = (((1,), (1,)), ((), ()))
TN = (((0,), (0,)), ((), ()))

SINE = (4.4428816249751035, -7.307782340256801, 3.5971494246649565, -0.7893218692014636)
SUB = 256
STEP = 512


def green_pair(squared, masked):
    if masked:
        distinct = squared > 0.5
        squared = jnp.maximum(squared, 1.0)
    inverse = lax.rsqrt(squared)
    turns = (squared * inverse) * np.float32(1.0 / np.pi)
    part = turns - jnp.round(turns)
    z = part * part
    poly = z * np.float32(SINE[3]) + np.float32(SINE[2])
    poly = poly * z + np.float32(SINE[1])
    poly = poly * z + np.float32(SINE[0])
    sine = part * poly
    rest = 2.0 - sine * sine
    both = rest * inverse
    real_part = both - inverse
    imag_part = (sine * both) * lax.rsqrt(rest)
    if masked:
        real_part = jnp.where(distinct, real_part, 0.0)
        imag_part = jnp.where(distinct, imag_part, 0.0)
    return real_part.astype(bf16), imag_part.astype(bf16)


def scatter_tiles(tiles, sites_of, weights_of, targets, held, acc, masked, unroll):
    width = targets.shape[1]

    def fill(i, slot):
        held[slot] = lax.dot_general(sites_of(i), targets[...], TN, preferred_element_type=f32)

    def work(i, slot):
        weights = weights_of(i)
        for k in range(width // SUB):
            cut = slice(k * SUB, (k + 1) * SUB)
            real_part, imag_part = green_pair(held[slot, :, cut], masked)
            acc[0:8, cut] += jnp.dot(weights, real_part, preferred_element_type=f32)
            acc[8:16, cut] += jnp.dot(weights, imag_part, preferred_element_type=f32)

    fill(0, 0)

    def body(h, carry):
        for u in range(unroll):
            i = unroll * h + u
            fill(jnp.minimum(i + 1, tiles - 1), 1 - u % 2)
            work(i, u % 2)
        return carry

    lax.fori_loop(0, tiles // unroll, body, 0)


def remote_kernel(ready, sources, begun, keep, send, held, acc, spots):
    rows, _, length = spots.shape
    per_row = length // STEP
    row = lax.axis_index("row")
    targets = ready.at[8:16, length:]
    acc[...] = begun[...]
    width = length // 8

    def spread_sites(c, carry):
        x, y, z = [
            sources[c, :, length + k * width : length + (k + 1) * width].astype(f32)
            for k in range(3)
        ]
        norm = x * x + y * y + z * z
        high = jnp.floor(norm * np.float32(1.0 / 256.0))
        low = norm - 256.0 * high
        one = jnp.ones((2, width), f32)
        for k in range(8):
            parts = [p[k : k + 1] for p in (x, y, z, high, low)] + [one, 0.0 * one[0:1]]
            spots[c, :, k * width : (k + 1) * width] = jnp.concatenate(parts, 0).astype(bf16)
        return carry

    lax.fori_loop(0, rows, spread_sites, 0)

    def where(i):
        chunk = lax.rem(row + 1 + i // per_row, rows)
        return chunk, pl.ds(pl.multiple_of(lax.rem(i, per_row) * STEP, STEP), STEP)

    def sites_of(i):
        chunk, cut = where(i)
        return spots[chunk, :, cut]

    def weights_of(i):
        chunk, cut = where(i)
        return sources[chunk, :, cut]

    scatter_tiles((rows - 1) * per_row, sites_of, weights_of, targets, held, acc, False, 4)
    real = acc[0:8]
    imag = acc[8:16]
    upper = real[0:4] - imag[4:8]
    lower = real[4:8] + imag[0:4]
    both = jnp.concatenate([upper, lower], 0)
    half = both.shape[1] // 2
    first, second = both[:, :half], both[:, half:]
    mine = lax.axis_index("grp") == 0
    keep[...] = jnp.where(mine, first, second)
    send[...] = jnp.where(mine, second, first)


def split(x):
    high = x.astype(bf16)
    return high, (x - high.astype(f32)).astype(bf16)


def swap_parts(x, rows):
    lane = lax.broadcasted_iota(jnp.int32, x.shape, 1)
    width = x.shape[1]
    rolled = pltpu.roll(x, rows - 4, 0)
    return jnp.where((lane & 4) == 0, pltpu.roll(rolled, width - 4, 1), pltpu.roll(rolled, 4, 1))


def complex_mix(products):
    lane = lax.broadcasted_iota(jnp.int32, products.shape, 1)
    sub = lax.broadcasted_iota(jnp.int32, products.shape, 0)
    swapped = swap_parts(products, products.shape[0])
    same = ((lane & 4) == 0) == ((sub & 4) == 0)
    return products + jnp.where(same, swapped, -swapped)


def prepare_kernel(basis, lattice, index, table, spread, ready, *scratch):
    direction, chosen, held_table, points, aims, sems = scratch
    rows = spread.shape[0]
    length = points.shape[1]
    wide = aims.shape[1]
    channels = direction.shape[0]
    aim = pl.multiple_of(lax.axis_index("col") * wide, 128)
    start = pl.multiple_of(lax.axis_index("grp") * length, 128)
    last = basis.shape[0] - channels
    copies = [
        pltpu.make_async_copy(lattice.at[:, pl.ds(start, length)], points, sems.at[0]),
        pltpu.make_async_copy(index.at[:, pl.ds(start, length)], chosen, sems.at[1]),
        pltpu.make_async_copy(table, held_table, sems.at[2]),
        pltpu.make_async_copy(
            basis.at[last : last + channels, pl.ds(start, length)], direction, sems.at[3]
        ),
        pltpu.make_async_copy(lattice.at[:, pl.ds(aim, wide)], aims, sems.at[4]),
    ]
    for copy in copies:
        copy.start()

    def shared_rows(part):
        x, y, z = part[0:1], part[1:2], part[2:3]
        norm = x * x + y * y + z * z
        return x, y, z, lax.shift_right_logical(norm, 8), norm & 255, jnp.ones_like(x)

    def stacked(parts):
        return jnp.concatenate([p.astype(f32) for p in parts], 0)

    copies[0].wait()
    x, y, z, high, low, one = shared_rows(points[...])
    sites = stacked([x, y, z, high, low, one, one, 0 * one])
    copies[1].wait()
    copies[2].wait()
    strength = jnp.zeros(chosen.shape, f32)
    for k in range(table.shape[1]):
        strength = jnp.where(chosen[...] == k, held_table[0:1, k : k + 1], strength)
    copies[3].wait()
    weighted = (direction[...] * strength).astype(bf16)
    ready[0:8, :length] = weighted
    ready[8:16, :length] = sites.astype(bf16)
    width = length // 8
    dense = [
        jnp.concatenate([sites[p : p + 1, k * width : (k + 1) * width] for k in range(8)], 0)
        for p in range(3)
    ]
    packed = jnp.concatenate([weighted] + [d.astype(bf16) for d in dense], 1)
    for k in range(rows):
        spread[k] = packed
    copies[4].wait()
    x, y, z, high, low, one = shared_rows(aims[...])
    sites = stacked([-2 * x, -2 * y, -2 * z, 256 * one, one, 256 * high, low, 0 * one])
    ready[:, length:] = jnp.concatenate([jnp.zeros_like(sites), sites], 0).astype(bf16)


def local_kernel(ready, basis, *rest):
    acc, gram, direction, own_high, own_low, kept, tiles, held, high, low, sems = rest
    half = kept.shape[1]
    length = ready.shape[1] - tiles.shape[2]
    targets = ready.at[8:16, length:]
    part = lax.axis_index(("col", "grp"))
    count, points = basis.shape
    pieces = sems.shape[0] - 1
    chunk = points // pieces
    channels, width = direction.shape
    here = pl.ds(pl.multiple_of(part * width, 128), width)
    own = pltpu.make_async_copy(
        basis.at[count - channels : count, here], direction, sems.at[pieces]
    )
    own.start()
    start = pl.multiple_of(jnp.minimum(part * 16, count - 16), 16)

    def place_of(k):
        first = k * chunk
        if first < half:
            return kept.at[:, first : first + chunk]
        return held.at[:, first - half : first - half + chunk]

    copies = []
    for k in range(points // chunk):
        cut = slice(k * chunk, (k + 1) * chunk)
        copies.append(pltpu.make_async_copy(basis.at[:, cut], place_of(k), sems.at[k]))
        copies[-1].start()

    acc[...] = jnp.zeros_like(acc)

    def sites_of(i):
        return ready[8:16, pl.ds(pl.multiple_of(i * STEP, STEP), STEP)]

    def weights_of(i):
        return ready[0:8, pl.ds(pl.multiple_of(i * STEP, STEP), STEP)]

    scatter_tiles(length // STEP, sites_of, weights_of, targets, tiles, acc, True, 2)

    total = jnp.zeros((16, count), f32)
    for k in range(points // chunk):
        cut = slice(k * chunk, (k + 1) * chunk)
        copies[k].wait()
        top, rest = split(place_of(k)[...])
        high[:, cut] = top
        low[:, cut] = rest
        mine = jnp.concatenate([high[pl.ds(start, 16), cut], low[pl.ds(start, 16), cut]], 0)
        first = lax.dot_general(mine, top, NT, preferred_element_type=f32)
        second = lax.dot_general(mine[:16], rest, NT, preferred_element_type=f32)
        total = total + (first[:16] + first[16:] + second)
    total = jnp.concatenate([total, jnp.zeros((16, 256 - count), f32)], 1)
    mixed = complex_mix(total)
    gram[...] = stack_halves(jnp.concatenate([mixed[0:4], mixed[8:12]], 0))
    own.wait()
    own_high[...] = high[:, here]
    own_low[...] = low[:, here]


def stack_halves(x):
    return jnp.concatenate([x[:, :128], x[:, 128:]], 0)


def join_halves(x):
    rows = x.shape[0] // 2
    return jnp.concatenate([x[:rows], x[rows:]], 1)


def project_kernel(keep, got, direction, high, low, gram, initial, packed):
    field = direction[...] - (keep[...] + got[...])
    initial[...] = stack_halves(field)
    count = high.shape[0]
    field_high, field_low = split(field)
    both = jnp.concatenate([field_high, field_low], 0)
    first = lax.dot_general(both, high[...], NT, preferred_element_type=f32)
    second = lax.dot_general(field_high, low[...], NT, preferred_element_type=f32)
    own = lax.dot_general(field, field, NT, preferred_element_type=f32, precision=highest)
    rest = jnp.zeros((8, 256 - count - 8), f32)
    products = jnp.concatenate([first[:8] + first[8:] + second, own, rest], 1)
    packed[0:8, :] = stack_halves(complex_mix(products)[0:4])
    packed[8:, :] = gram[...]


def preload_kernel(sums, basis, ahead, sems):
    del sums
    chunk = 512
    first = basis.shape[1] // 2
    copies = []
    for k in range(sems.shape[0]):
        cut = slice(k * chunk, (k + 1) * chunk)
        there = slice(first + k * chunk, first + (k + 1) * chunk)
        copies.append(pltpu.make_async_copy(basis.at[:, there], ahead.at[:, cut], sems.at[k]))
        copies[-1].start()
    for copy in copies:
        copy.wait()


def final_kernel(total, shared, kept, ahead, basis, new, coef, norm, *scratch):
    gram_high, gram_low, held, sems = scratch
    parts = shared.shape[0]
    count, points = basis.shape
    width = 256
    chunk = 512
    half = kept.shape[1]
    last = points - held.shape[1]
    copies = []
    for k in range(sems.shape[0]):
        cut = slice(k * chunk, (k + 1) * chunk)
        there = slice(last + k * chunk, last + (k + 1) * chunk)
        copies.append(pltpu.make_async_copy(basis.at[:, there], held.at[:, cut], sems.at[k]))
        copies[-1].start()
    scale = np.float32(1.0 / total)
    sums = shared[0, 16:24, :]
    for q in range(1, parts):
        sums = sums + shared[q, 16:24, :]
    upper = join_halves(sums)
    lane = lax.broadcasted_iota(jnp.int32, upper.shape, 1)
    lower = jnp.where(
        (lane & 4) == 0, -pltpu.roll(upper, width - 4, 1), pltpu.roll(upper, 4, 1)
    )
    sums = jnp.concatenate([upper, lower], 0)
    lane = lax.broadcasted_iota(jnp.int32, sums.shape, 1)
    sub = lax.broadcasted_iota(jnp.int32, sums.shape, 0)
    gram_high[...] = jnp.zeros_like(gram_high)
    gram_low[...] = jnp.zeros_like(gram_low)
    for q in range(count // 16):
        part = join_halves(shared[q, 24:40, :])
        pair = jnp.concatenate(
            [jnp.where(sub < 4, part, 0.0), jnp.where(sub < 4, pltpu.roll(part, 4, 0), 0.0)], 0
        )
        top, rest = split(pair)
        gram_high[16 * q : 16 * q + 16, :] = top
        gram_low[16 * q : 16 * q + 16, :] = rest

    def times_gram(x):
        top, rest = split(x)
        first = jnp.dot(
            jnp.concatenate([top, rest], 0), gram_high[...], preferred_element_type=f32
        )
        second = jnp.dot(top, gram_low[...], preferred_element_type=f32)
        return complex_mix(first[:8] + first[8:] + second)

    products = jnp.where(lane < count, sums, 0.0)
    once = products * scale
    mix = 2.0 * once - times_gram(once) * scale
    mix_high, mix_low = split(mix[:, :count])
    both = jnp.concatenate([mix_high, mix_low], 0)
    for k in range(points // chunk):
        cut = slice(k * chunk, (k + 1) * chunk)
        if k * chunk < half:
            columns = kept[:, cut]
        elif k * chunk < last:
            columns = ahead[:, k * chunk - half : (k + 1) * chunk - half]
        else:
            later = k - last // chunk
            copies[later].wait()
            columns = held[:, later * chunk : (later + 1) * chunk]
        top, rest = split(columns)
        first = jnp.dot(both, top, preferred_element_type=f32)
        second = jnp.dot(mix_high, rest, preferred_element_type=f32)
        each = chunk // width
        field = jnp.concatenate(
            [join_halves(shared[each * k + i, 0:16, :]) for i in range(each)], 1
        )
        new[:, cut] = field - (first[:8] + first[8:] + second)

    seen = products - 0.5 * times_gram(mix)
    cross = lax.dot_general(mix, seen, NT, preferred_element_type=f32, precision=highest)
    cross_t = lax.dot_general(seen, mix, NT, preferred_element_type=f32, precision=highest)
    own = pltpu.roll(sums, width - count, 1)[:, 0:8]
    result = (own - cross - cross_t) * scale
    norm[0] = result[0:4, 0:4]
    norm[1] = result[0:4, 4:8]

    row = lax.broadcasted_iota(jnp.int32, (width, 128), 0)
    column = lax.broadcasted_iota(jnp.int32, (width, 128), 1)
    wanted = ((row & 4) == 0) & (column == (row & 7) * 32 + lax.shift_right_logical(row, 3))
    top, rest = split(mix)
    least = (mix - top.astype(f32) - rest.astype(f32)).astype(bf16)
    chosen = jnp.dot(
        jnp.concatenate([top, rest, least], 0),
        jnp.where(wanted, 1.0, 0.0).astype(bf16),
        preferred_element_type=f32,
    )
    chosen = chosen[:8] + chosen[8:16] + chosen[16:]
    blocks = coef.shape[3]
    for k in range(4):
        moved = pltpu.roll(chosen, (128 - 32 * k) % 128, 1)
        coef[0, k] = moved[0:4, 0:blocks]
        coef[1, k] = moved[4:8, 0:blocks]


def gather_all(x, axis):
    length = lax.axis_size(axis)
    return lax.all_to_all(jnp.broadcast_to(x[None], (length, *x.shape)), axis, 0, 0, tiled=True)


VMEM = pl.BlockSpec(memory_space=pltpu.VMEM)
SMEM = pl.BlockSpec(memory_space=pltpu.SMEM)
HBM = pl.BlockSpec(memory_space=pltpu.HBM)


def params(room=16 << 20):
    return pltpu.CompilerParams(vmem_limit_bytes=room)


def cost(flops, size):
    return pl.CostEstimate(flops=flops, bytes_accessed=size, transcendentals=0)


def local(krylov_basis, lattice, strength_index, strength_table):
    blocks, channels, points = krylov_basis.shape
    inc = channels // 2
    count = blocks * channels
    rows = lax.axis_size("row")
    groups = lax.axis_size("grp")
    parts = lax.axis_size(("col", "grp"))
    total = points * rows
    own = points // parts
    wide = own * groups
    length = points // groups
    flat = krylov_basis.reshape(count, points)
    spread, ready = pl.pallas_call(
        prepare_kernel,
        in_specs=[HBM, HBM, HBM, HBM],
        out_specs=(VMEM, VMEM),
        out_shape=(
            jax.ShapeDtypeStruct((rows, 8, length + 3 * (length // 8)), bf16),
            jax.ShapeDtypeStruct((16, length + wide), bf16),
        ),
        scratch_shapes=[
            pltpu.VMEM((channels, length), f32),
            pltpu.VMEM((1, length), jnp.int32),
            pltpu.VMEM((1, strength_table.shape[0]), f32),
            pltpu.VMEM((3, length), jnp.int32),
            pltpu.VMEM((3, wide), jnp.int32),
            pltpu.SemaphoreType.DMA((5,)),
        ],
        compiler_params=params((64 << 20) - (64 << 10)),
        name="prepare",
    )(flat, lattice, strength_index[None, :], strength_table[None, :])
    gathered = lax.all_to_all(spread, "row", 0, 0, tiled=True)

    half = jax.ShapeDtypeStruct((channels, own), f32)
    held = pltpu.VMEM((2, STEP, wide), f32)
    begun, gram, direction, high, low, kept = pl.pallas_call(
        local_kernel,
        in_specs=[VMEM, HBM],
        out_specs=(VMEM,) * 6,
        out_shape=(
            jax.ShapeDtypeStruct((16, wide), f32),
            jax.ShapeDtypeStruct((16, 128), f32),
            half,
            jax.ShapeDtypeStruct((count, own), bf16),
            jax.ShapeDtypeStruct((count, own), bf16),
            jax.ShapeDtypeStruct((count, points // 2), f32),
        ),
        scratch_shapes=[
            held,
            pltpu.VMEM((count, points // 2), f32),
            pltpu.VMEM((count, points), bf16),
            pltpu.VMEM((count, points), bf16),
            pltpu.SemaphoreType.DMA((9,)),
        ],
        compiler_params=params(50 << 20),
        cost_estimate=cost(5_000_000_000, 8_000_000),
        name="scatter_local",
    )(ready, flat)

    keep, send = pl.pallas_call(
        remote_kernel,
        out_shape=(half, half),
        in_specs=[VMEM, VMEM, VMEM],
        out_specs=(VMEM, VMEM),
        scratch_shapes=[
            held,
            pltpu.VMEM((16, wide), f32),
            pltpu.VMEM((rows, 8, length), bf16),
        ],
        compiler_params=params(),
        cost_estimate=cost(20_000_000_000, 800_000),
        name="scatter_remote",
    )(ready, gathered, begun)
    got = lax.ppermute(send, "grp", [(i, groups - 1 - i) for i in range(groups)])

    initial, partial = pl.pallas_call(
        project_kernel,
        in_specs=[VMEM] * 6,
        out_specs=(VMEM, VMEM),
        out_shape=(jax.ShapeDtypeStruct((16, 128), f32), jax.ShapeDtypeStruct((24, 128), f32)),
        compiler_params=params(),
        name="project",
    )(keep, got, direction, high, low, gram)

    row_sums = jnp.sum(gather_all(partial, "row"), axis=0)
    shared = gather_all(jnp.concatenate([initial, row_sums], 0), ("col", "grp"))

    ahead = pl.pallas_call(
        preload_kernel,
        in_specs=[VMEM, HBM],
        out_specs=VMEM,
        out_shape=jax.ShapeDtypeStruct((count, points // 4), f32),
        scratch_shapes=[pltpu.SemaphoreType.DMA((points // 4 // 512,))],
        compiler_params=params(50 << 20),
        cost_estimate=cost(3_000_000_000, 8_000_000),
        name="preload",
    )(row_sums, flat)

    new_block, coef, norm = pl.pallas_call(
        functools.partial(final_kernel, total),
        in_specs=[VMEM, VMEM, VMEM, HBM],
        out_specs=(VMEM, VMEM, VMEM),
        out_shape=(
            jax.ShapeDtypeStruct((channels, points), f32),
            jax.ShapeDtypeStruct((2, inc, inc, blocks), f32),
            jax.ShapeDtypeStruct((2, inc, inc), f32),
        ),
        scratch_shapes=[
            pltpu.VMEM((256, 256), bf16),
            pltpu.VMEM((256, 256), bf16),
            pltpu.VMEM((count, points // 4), f32),
            pltpu.SemaphoreType.DMA((points // 4 // 512,)),
        ],
        compiler_params=params(50 << 20),
        name="finish",
    )(shared, kept, ahead, flat)
    return new_block, coef.transpose(3, 0, 1, 2), norm


def solution(mesh):
    in_specs = (P(None, None, "row"), P(None, "row"), P("row"), P())
    out_specs = (P(None, "row"), P(), P())
    return jax.shard_map(local, mesh=mesh, in_specs=in_specs, out_specs=out_specs, check_vma=False)
```

```python
import functools

import jax
import jax.numpy as jnp
import numpy as np
from jax import lax
from jax.experimental import pallas as pl
from jax.experimental.pallas import tpu as pltpu
from jax.sharding import PartitionSpec as P

f32 = jnp.float32
bf16 = jnp.bfloat16
highest = lax.Precision.HIGHEST
NT = (((1,), (1,)), ((), ()))
TN = (((0,), (0,)), ((), ()))

SINE = (4.4428816249751035, -7.307782340256801, 3.5971494246649565, -0.7893218692014636)
SUB = 256
STEP = 512


def green_pair(squared, masked):
    if masked:
        distinct = squared > 0.5
        squared = jnp.maximum(squared, 1.0)
    inverse = lax.rsqrt(squared)
    turns = (squared * inverse) * np.float32(1.0 / np.pi)
    part = turns - jnp.round(turns)
    z = part * part
    poly = z * np.float32(SINE[3]) + np.float32(SINE[2])
    poly = poly * z + np.float32(SINE[1])
    poly = poly * z + np.float32(SINE[0])
    sine = part * poly
    rest = 2.0 - sine * sine
    both = rest * inverse
    real_part = both - inverse
    imag_part = (sine * both) * lax.rsqrt(rest)
    if masked:
        real_part = jnp.where(distinct, real_part, 0.0)
        imag_part = jnp.where(distinct, imag_part, 0.0)
    return real_part.astype(bf16), imag_part.astype(bf16)


def scatter_tiles(tiles, sites_of, weights_of, targets, held, acc, masked, unroll):
    width = targets.shape[1]

    def fill(i, slot):
        held[slot] = lax.dot_general(sites_of(i), targets[...], TN, preferred_element_type=f32)

    def work(i, slot):
        weights = weights_of(i)
        for k in range(width // SUB):
            cut = slice(k * SUB, (k + 1) * SUB)
            real_part, imag_part = green_pair(held[slot, :, cut], masked)
            acc[0:8, cut] += jnp.dot(weights, real_part, preferred_element_type=f32)
            acc[8:16, cut] += jnp.dot(weights, imag_part, preferred_element_type=f32)

    fill(0, 0)

    def body(h, carry):
        for u in range(unroll):
            i = unroll * h + u
            fill(jnp.minimum(i + 1, tiles - 1), 1 - u % 2)
            work(i, u % 2)
        return carry

    lax.fori_loop(0, tiles // unroll, body, 0)


def remote_kernel(ready, sources, begun, keep, send, held, acc, spots):
    rows, _, length = spots.shape
    per_row = length // STEP
    row = lax.axis_index("row")
    targets = ready.at[8:16, length:]
    acc[...] = begun[...]
    width = length // 8

    def spread_sites(c, carry):
        x, y, z = [
            sources[c, :, length + k * width : length + (k + 1) * width].astype(f32)
            for k in range(3)
        ]
        norm = x * x + y * y + z * z
        high = jnp.floor(norm * np.float32(1.0 / 256.0))
        low = norm - 256.0 * high
        one = jnp.ones((2, width), f32)
        for k in range(8):
            parts = [p[k : k + 1] for p in (x, y, z, high, low)] + [one, 0.0 * one[0:1]]
            spots[c, :, k * width : (k + 1) * width] = jnp.concatenate(parts, 0).astype(bf16)
        return carry

    lax.fori_loop(0, rows, spread_sites, 0)

    def where(i):
        chunk = lax.rem(row + 1 + i // per_row, rows)
        return chunk, pl.ds(pl.multiple_of(lax.rem(i, per_row) * STEP, STEP), STEP)

    def sites_of(i):
        chunk, cut = where(i)
        return spots[chunk, :, cut]

    def weights_of(i):
        chunk, cut = where(i)
        return sources[chunk, :, cut]

    scatter_tiles((rows - 1) * per_row, sites_of, weights_of, targets, held, acc, False, 4)
    real = acc[0:8]
    imag = acc[8:16]
    upper = real[0:4] - imag[4:8]
    lower = real[4:8] + imag[0:4]
    both = jnp.concatenate([upper, lower], 0)
    half = both.shape[1] // 2
    first, second = both[:, :half], both[:, half:]
    mine = lax.axis_index("grp") == 0
    keep[...] = jnp.where(mine, first, second)
    send[...] = jnp.where(mine, second, first)


def split(x):
    high = x.astype(bf16)
    return high, (x - high.astype(f32)).astype(bf16)


def swap_parts(x, rows):
    lane = lax.broadcasted_iota(jnp.int32, x.shape, 1)
    width = x.shape[1]
    rolled = pltpu.roll(x, rows - 4, 0)
    return jnp.where((lane & 4) == 0, pltpu.roll(rolled, width - 4, 1), pltpu.roll(rolled, 4, 1))


def complex_mix(products):
    lane = lax.broadcasted_iota(jnp.int32, products.shape, 1)
    sub = lax.broadcasted_iota(jnp.int32, products.shape, 0)
    swapped = swap_parts(products, products.shape[0])
    same = ((lane & 4) == 0) == ((sub & 4) == 0)
    return products + jnp.where(same, swapped, -swapped)


def prepare_kernel(basis, lattice, index, table, spread, ready, *scratch):
    direction, chosen, held_table, points, aims, packed, sems, out_sems = scratch
    rows = spread.shape[0]
    length = points.shape[1]
    wide = aims.shape[1]
    channels = direction.shape[0]
    aim = pl.multiple_of(lax.axis_index("col") * wide, 128)
    start = pl.multiple_of(lax.axis_index("grp") * length, 128)
    last = basis.shape[0] - channels
    copies = [
        pltpu.make_async_copy(lattice.at[:, pl.ds(start, length)], points, sems.at[0]),
        pltpu.make_async_copy(index.at[:, pl.ds(start, length)], chosen, sems.at[1]),
        pltpu.make_async_copy(table, held_table, sems.at[2]),
        pltpu.make_async_copy(
            basis.at[last : last + channels, pl.ds(start, length)], direction, sems.at[3]
        ),
        pltpu.make_async_copy(lattice.at[:, pl.ds(aim, wide)], aims, sems.at[4]),
    ]
    for copy in copies:
        copy.start()

    def shared_rows(part):
        x, y, z = part[0:1], part[1:2], part[2:3]
        norm = x * x + y * y + z * z
        return x, y, z, lax.shift_right_logical(norm, 8), norm & 255, jnp.ones_like(x)

    def stacked(parts):
        return jnp.concatenate([p.astype(f32) for p in parts], 0)

    copies[0].wait()
    x, y, z, high, low, one = shared_rows(points[...])
    sites = stacked([x, y, z, high, low, one, one, 0 * one])
    copies[1].wait()
    copies[2].wait()
    strength = jnp.zeros(chosen.shape, f32)
    for k in range(table.shape[1]):
        strength = jnp.where(chosen[...] == k, held_table[0:1, k : k + 1], strength)
    copies[3].wait()
    weighted = (direction[...] * strength).astype(bf16)
    width = length // 8
    dense = [
        jnp.concatenate([sites[p : p + 1, k * width : (k + 1) * width] for k in range(8)], 0)
        for p in range(3)
    ]
    packed[...] = jnp.concatenate([weighted] + [d.astype(bf16) for d in dense], 1)
    writes = [
        pltpu.make_async_copy(packed, spread.at[k], out_sems.at[k]) for k in range(rows)
    ]
    for write in writes:
        write.start()
    ready[0:8, :length] = weighted
    ready[8:16, :length] = sites.astype(bf16)
    copies[4].wait()
    x, y, z, high, low, one = shared_rows(aims[...])
    sites = stacked([-2 * x, -2 * y, -2 * z, 256 * one, one, 256 * high, low, 0 * one])
    ready[:, length:] = jnp.concatenate([jnp.zeros_like(sites), sites], 0).astype(bf16)
    for write in writes:
        write.wait()


def local_kernel(ready, basis, *rest):
    acc, gram, direction, own_high, own_low, kept, tiles, held, high, low, sems = rest
    half = kept.shape[1]
    length = ready.shape[1] - tiles.shape[2]
    targets = ready.at[8:16, length:]
    part = lax.axis_index(("col", "grp"))
    count, points = basis.shape
    pieces = sems.shape[0] - 1
    chunk = points // pieces
    channels, width = direction.shape
    here = pl.ds(pl.multiple_of(part * width, 128), width)
    own = pltpu.make_async_copy(
        basis.at[count - channels : count, here], direction, sems.at[pieces]
    )
    own.start()
    start = pl.multiple_of(jnp.minimum(part * 16, count - 16), 16)

    def place_of(k):
        first = k * chunk
        if first < half:
            return kept.at[:, first : first + chunk]
        return held.at[:, first - half : first - half + chunk]

    copies = []
    for k in range(points // chunk):
        cut = slice(k * chunk, (k + 1) * chunk)
        copies.append(pltpu.make_async_copy(basis.at[:, cut], place_of(k), sems.at[k]))
        copies[-1].start()

    acc[...] = jnp.zeros_like(acc)

    def sites_of(i):
        return ready[8:16, pl.ds(pl.multiple_of(i * STEP, STEP), STEP)]

    def weights_of(i):
        return ready[0:8, pl.ds(pl.multiple_of(i * STEP, STEP), STEP)]

    scatter_tiles(length // STEP, sites_of, weights_of, targets, tiles, acc, True, 2)

    total = jnp.zeros((16, count), f32)
    for k in range(points // chunk):
        cut = slice(k * chunk, (k + 1) * chunk)
        copies[k].wait()
        top, rest = split(place_of(k)[...])
        high[:, cut] = top
        low[:, cut] = rest
        mine = jnp.concatenate([high[pl.ds(start, 16), cut], low[pl.ds(start, 16), cut]], 0)
        first = lax.dot_general(mine, top, NT, preferred_element_type=f32)
        second = lax.dot_general(mine[:16], rest, NT, preferred_element_type=f32)
        total = total + (first[:16] + first[16:] + second)
    total = jnp.concatenate([total, jnp.zeros((16, 256 - count), f32)], 1)
    mixed = complex_mix(total)
    gram[...] = stack_halves(jnp.concatenate([mixed[0:4], mixed[8:12]], 0))
    own.wait()
    own_high[...] = high[:, here]
    own_low[...] = low[:, here]


def stack_halves(x):
    return jnp.concatenate([x[:, :128], x[:, 128:]], 0)


def join_halves(x):
    rows = x.shape[0] // 2
    return jnp.concatenate([x[:rows], x[rows:]], 1)


def project_kernel(keep, got, direction, high, low, gram, initial, packed):
    field = direction[...] - (keep[...] + got[...])
    initial[...] = stack_halves(field)
    count = high.shape[0]
    field_high, field_low = split(field)
    both = jnp.concatenate([field_high, field_low], 0)
    first = lax.dot_general(both, high[...], NT, preferred_element_type=f32)
    second = lax.dot_general(field_high, low[...], NT, preferred_element_type=f32)
    own = lax.dot_general(field, field, NT, preferred_element_type=f32, precision=highest)
    rest = jnp.zeros((8, 256 - count - 8), f32)
    products = jnp.concatenate([first[:8] + first[8:] + second, own, rest], 1)
    packed[0:8, :] = stack_halves(complex_mix(products)[0:4])
    packed[8:, :] = gram[...]


def final_kernel(total, shared, kept, basis, new, coef, norm, gram_high, gram_low, held, sems):
    parts = shared.shape[0]
    count, points = basis.shape
    width = 256
    chunk = 512
    half = points - held.shape[1]
    copies = []
    for k in range(sems.shape[0]):
        cut = slice(k * chunk, (k + 1) * chunk)
        there = slice(half + k * chunk, half + (k + 1) * chunk)
        copies.append(pltpu.make_async_copy(basis.at[:, there], held.at[:, cut], sems.at[k]))
        copies[-1].start()
    scale = np.float32(1.0 / total)
    sums = shared[0, 16:24, :]
    for q in range(1, parts):
        sums = sums + shared[q, 16:24, :]
    upper = join_halves(sums)
    lane = lax.broadcasted_iota(jnp.int32, upper.shape, 1)
    lower = jnp.where(
        (lane & 4) == 0, -pltpu.roll(upper, width - 4, 1), pltpu.roll(upper, 4, 1)
    )
    sums = jnp.concatenate([upper, lower], 0)
    lane = lax.broadcasted_iota(jnp.int32, sums.shape, 1)
    sub = lax.broadcasted_iota(jnp.int32, sums.shape, 0)
    gram_high[...] = jnp.zeros_like(gram_high)
    gram_low[...] = jnp.zeros_like(gram_low)
    for q in range(count // 16):
        part = join_halves(shared[q, 24:40, :])
        pair = jnp.concatenate(
            [jnp.where(sub < 4, part, 0.0), jnp.where(sub < 4, pltpu.roll(part, 4, 0), 0.0)], 0
        )
        top, rest = split(pair)
        gram_high[16 * q : 16 * q + 16, :] = top
        gram_low[16 * q : 16 * q + 16, :] = rest

    def times_gram(x):
        top, rest = split(x)
        first = jnp.dot(
            jnp.concatenate([top, rest], 0), gram_high[...], preferred_element_type=f32
        )
        second = jnp.dot(top, gram_low[...], preferred_element_type=f32)
        return complex_mix(first[:8] + first[8:] + second)

    products = jnp.where(lane < count, sums, 0.0)
    once = products * scale
    mix = 2.0 * once - times_gram(once) * scale
    mix_high, mix_low = split(mix[:, :count])
    both = jnp.concatenate([mix_high, mix_low], 0)
    for k in range(points // chunk):
        cut = slice(k * chunk, (k + 1) * chunk)
        if k * chunk < half:
            columns = kept[:, cut]
        else:
            later = k - half // chunk
            copies[later].wait()
            columns = held[:, later * chunk : (later + 1) * chunk]
        top, rest = split(columns)
        first = jnp.dot(both, top, preferred_element_type=f32)
        second = jnp.dot(mix_high, rest, preferred_element_type=f32)
        each = chunk // width
        field = jnp.concatenate(
            [join_halves(shared[each * k + i, 0:16, :]) for i in range(each)], 1
        )
        new[:, cut] = field - (first[:8] + first[8:] + second)

    seen = products - 0.5 * times_gram(mix)
    cross = lax.dot_general(mix, seen, NT, preferred_element_type=f32, precision=highest)
    cross_t = lax.dot_general(seen, mix, NT, preferred_element_type=f32, precision=highest)
    own = pltpu.roll(sums, width - count, 1)[:, 0:8]
    result = (own - cross - cross_t) * scale
    norm[0] = result[0:4, 0:4]
    norm[1] = result[0:4, 4:8]

    row = lax.broadcasted_iota(jnp.int32, (width, 128), 0)
    column = lax.broadcasted_iota(jnp.int32, (width, 128), 1)
    wanted = ((row & 4) == 0) & (column == (row & 7) * 32 + lax.shift_right_logical(row, 3))
    top, rest = split(mix)
    least = (mix - top.astype(f32) - rest.astype(f32)).astype(bf16)
    chosen = jnp.dot(
        jnp.concatenate([top, rest, least], 0),
        jnp.where(wanted, 1.0, 0.0).astype(bf16),
        preferred_element_type=f32,
    )
    chosen = chosen[:8] + chosen[8:16] + chosen[16:]
    blocks = coef.shape[3]
    for k in range(4):
        moved = pltpu.roll(chosen, (128 - 32 * k) % 128, 1)
        coef[0, k] = moved[0:4, 0:blocks]
        coef[1, k] = moved[4:8, 0:blocks]


def gather_all(x, axis):
    length = lax.axis_size(axis)
    return lax.all_to_all(jnp.broadcast_to(x[None], (length, *x.shape)), axis, 0, 0, tiled=True)


VMEM = pl.BlockSpec(memory_space=pltpu.VMEM)
SMEM = pl.BlockSpec(memory_space=pltpu.SMEM)
HBM = pl.BlockSpec(memory_space=pltpu.HBM)


def params(room=16 << 20):
    return pltpu.CompilerParams(vmem_limit_bytes=room)


def cost(flops, size):
    return pl.CostEstimate(flops=flops, bytes_accessed=size, transcendentals=0)


def local(krylov_basis, lattice, strength_index, strength_table):
    blocks, channels, points = krylov_basis.shape
    inc = channels // 2
    count = blocks * channels
    rows = lax.axis_size("row")
    groups = lax.axis_size("grp")
    parts = lax.axis_size(("col", "grp"))
    total = points * rows
    own = points // parts
    wide = own * groups
    length = points // groups
    flat = krylov_basis.reshape(count, points)
    spread, ready = pl.pallas_call(
        prepare_kernel,
        in_specs=[HBM, HBM, HBM, HBM],
        out_specs=(HBM, VMEM),
        out_shape=(
            jax.ShapeDtypeStruct((rows, 8, length + 3 * (length // 8)), bf16),
            jax.ShapeDtypeStruct((16, length + wide), bf16),
        ),
        scratch_shapes=[
            pltpu.VMEM((channels, length), f32),
            pltpu.VMEM((1, length), jnp.int32),
            pltpu.VMEM((1, strength_table.shape[0]), f32),
            pltpu.VMEM((3, length), jnp.int32),
            pltpu.VMEM((3, wide), jnp.int32),
            pltpu.VMEM((8, length + 3 * (length // 8)), bf16),
            pltpu.SemaphoreType.DMA((5,)),
            pltpu.SemaphoreType.DMA((rows,)),
        ],
        compiler_params=params((64 << 20) - (64 << 10)),
        name="prepare",
    )(flat, lattice, strength_index[None, :], strength_table[None, :])
    gathered = lax.all_to_all(spread, "row", 0, 0, tiled=True)

    half = jax.ShapeDtypeStruct((channels, own), f32)
    held = pltpu.VMEM((2, STEP, wide), f32)
    begun, gram, direction, high, low, kept = pl.pallas_call(
        local_kernel,
        in_specs=[VMEM, HBM],
        out_specs=(VMEM,) * 6,
        out_shape=(
            jax.ShapeDtypeStruct((16, wide), f32),
            jax.ShapeDtypeStruct((16, 128), f32),
            half,
            jax.ShapeDtypeStruct((count, own), bf16),
            jax.ShapeDtypeStruct((count, own), bf16),
            jax.ShapeDtypeStruct((count, points // 2), f32),
        ),
        scratch_shapes=[
            held,
            pltpu.VMEM((count, points // 2), f32),
            pltpu.VMEM((count, points), bf16),
            pltpu.VMEM((count, points), bf16),
            pltpu.SemaphoreType.DMA((9,)),
        ],
        compiler_params=params(50 << 20),
        cost_estimate=cost(5_000_000_000, 8_000_000),
        name="scatter_local",
    )(ready, flat)

    keep, send = pl.pallas_call(
        remote_kernel,
        out_shape=(half, half),
        in_specs=[VMEM, VMEM, VMEM],
        out_specs=(VMEM, VMEM),
        scratch_shapes=[
            held,
            pltpu.VMEM((16, wide), f32),
            pltpu.VMEM((rows, 8, length), bf16),
        ],
        compiler_params=params(),
        cost_estimate=cost(20_000_000_000, 800_000),
        name="scatter_remote",
    )(ready, gathered, begun)
    got = lax.ppermute(send, "grp", [(i, groups - 1 - i) for i in range(groups)])

    initial, partial = pl.pallas_call(
        project_kernel,
        in_specs=[VMEM] * 6,
        out_specs=(VMEM, VMEM),
        out_shape=(jax.ShapeDtypeStruct((16, 128), f32), jax.ShapeDtypeStruct((24, 128), f32)),
        compiler_params=params(),
        name="project",
    )(keep, got, direction, high, low, gram)

    row_sums = jnp.sum(gather_all(partial, "row"), axis=0)
    shared = gather_all(jnp.concatenate([initial, row_sums], 0), ("col", "grp"))

    new_block, coef, norm = pl.pallas_call(
        functools.partial(final_kernel, total),
        in_specs=[VMEM, VMEM, HBM],
        out_specs=(VMEM, VMEM, VMEM),
        out_shape=(
            jax.ShapeDtypeStruct((channels, points), f32),
            jax.ShapeDtypeStruct((2, inc, inc, blocks), f32),
            jax.ShapeDtypeStruct((2, inc, inc), f32),
        ),
        scratch_shapes=[
            pltpu.VMEM((256, 256), bf16),
            pltpu.VMEM((256, 256), bf16),
            pltpu.VMEM((count, points // 2), f32),
            pltpu.SemaphoreType.DMA((points // 2 // 512,)),
        ],
        compiler_params=params(50 << 20),
        name="finish",
    )(shared, kept, flat)
    return new_block, coef.transpose(3, 0, 1, 2), norm


def solution(mesh):
    in_specs = (P(None, None, "row"), P(None, "row"), P("row"), P())
    out_specs = (P(None, "row"), P(), P())
    return jax.shard_map(local, mesh=mesh, in_specs=in_specs, out_specs=out_specs, check_vma=False)
```

```python
import functools

import jax
import jax.numpy as jnp
import numpy as np
from jax import lax
from jax.experimental import pallas as pl
from jax.experimental.pallas import tpu as pltpu
from jax.sharding import PartitionSpec as P

f32 = jnp.float32
bf16 = jnp.bfloat16
highest = lax.Precision.HIGHEST
NT = (((1,), (1,)), ((), ()))
TN = (((0,), (0,)), ((), ()))

SINE = (4.4428816249751035, -7.307782340256801, 3.5971494246649565, -0.7893218692014636)
SUB = 256
STEP = 512


def green_pair(squared, masked):
    if masked:
        distinct = squared > 0.5
        squared = jnp.maximum(squared, 1.0)
    inverse = lax.rsqrt(squared)
    turns = (squared * inverse) * np.float32(1.0 / np.pi)
    part = turns - jnp.round(turns)
    z = part * part
    poly = z * np.float32(SINE[3]) + np.float32(SINE[2])
    poly = poly * z + np.float32(SINE[1])
    poly = poly * z + np.float32(SINE[0])
    sine = part * poly
    rest = 2.0 - sine * sine
    both = rest * inverse
    real_part = both - inverse
    imag_part = (sine * both) * lax.rsqrt(rest)
    if masked:
        real_part = jnp.where(distinct, real_part, 0.0)
        imag_part = jnp.where(distinct, imag_part, 0.0)
    return real_part.astype(bf16), imag_part.astype(bf16)


def scatter_tiles(tiles, sites_of, weights_of, targets, held, acc, masked, unroll):
    width = targets.shape[1]

    def fill(i, slot):
        held[slot] = lax.dot_general(sites_of(i), targets[...], TN, preferred_element_type=f32)

    def work(i, slot):
        weights = weights_of(i)
        for k in range(width // SUB):
            cut = slice(k * SUB, (k + 1) * SUB)
            real_part, imag_part = green_pair(held[slot, :, cut], masked)
            acc[0:8, cut] += jnp.dot(weights, real_part, preferred_element_type=f32)
            acc[8:16, cut] += jnp.dot(weights, imag_part, preferred_element_type=f32)

    fill(0, 0)

    def body(h, carry):
        for u in range(unroll):
            i = unroll * h + u
            fill(jnp.minimum(i + 1, tiles - 1), 1 - u % 2)
            work(i, u % 2)
        return carry

    lax.fori_loop(0, tiles // unroll, body, 0)


def remote_kernel(ready, sources, begun, keep, send, held, acc, spots):
    rows, _, length = spots.shape
    per_row = length // STEP
    row = lax.axis_index("row")
    targets = ready.at[8:16, length:]
    acc[...] = begun[...]
    width = length // 8

    def spread_sites(c, carry):
        x, y, z = [
            sources[c, :, length + k * width : length + (k + 1) * width].astype(f32)
            for k in range(3)
        ]
        norm = x * x + y * y + z * z
        high = jnp.floor(norm * np.float32(1.0 / 256.0))
        low = norm - 256.0 * high
        one = jnp.ones((2, width), f32)
        for k in range(8):
            parts = [p[k : k + 1] for p in (x, y, z, high, low)] + [one, 0.0 * one[0:1]]
            spots[c, :, k * width : (k + 1) * width] = jnp.concatenate(parts, 0).astype(bf16)
        return carry

    lax.fori_loop(0, rows, spread_sites, 0)

    def where(i):
        chunk = lax.rem(row + 1 + i // per_row, rows)
        return chunk, pl.ds(pl.multiple_of(lax.rem(i, per_row) * STEP, STEP), STEP)

    def sites_of(i):
        chunk, cut = where(i)
        return spots[chunk, :, cut]

    def weights_of(i):
        chunk, cut = where(i)
        return sources[chunk, :, cut]

    scatter_tiles((rows - 1) * per_row, sites_of, weights_of, targets, held, acc, False, 4)
    real = acc[0:8]
    imag = acc[8:16]
    upper = real[0:4] - imag[4:8]
    lower = real[4:8] + imag[0:4]
    both = jnp.concatenate([upper, lower], 0)
    half = both.shape[1] // 2
    first, second = both[:, :half], both[:, half:]
    mine = lax.axis_index("grp") == 0
    keep[...] = jnp.where(mine, first, second)
    send[...] = jnp.where(mine, second, first)


def split(x):
    high = x.astype(bf16)
    return high, (x - high.astype(f32)).astype(bf16)


def swap_parts(x, rows):
    lane = lax.broadcasted_iota(jnp.int32, x.shape, 1)
    width = x.shape[1]
    rolled = pltpu.roll(x, rows - 4, 0)
    return jnp.where((lane & 4) == 0, pltpu.roll(rolled, width - 4, 1), pltpu.roll(rolled, 4, 1))


def complex_mix(products):
    lane = lax.broadcasted_iota(jnp.int32, products.shape, 1)
    sub = lax.broadcasted_iota(jnp.int32, products.shape, 0)
    swapped = swap_parts(products, products.shape[0])
    same = ((lane & 4) == 0) == ((sub & 4) == 0)
    return products + jnp.where(same, swapped, -swapped)


def prepare_kernel(basis, lattice, index, table, spread, ready, *scratch):
    direction, chosen, held_table, points, sems = scratch
    rows = spread.shape[0]
    length = chosen.shape[1]
    wide = ready.shape[1] - length
    channels = direction.shape[0]
    aim = pl.multiple_of(lax.axis_index("col") * wide, 128)
    start = pl.multiple_of(lax.axis_index("grp") * length, 128)
    last = basis.shape[0] - channels
    copies = [
        pltpu.make_async_copy(lattice, points, sems.at[0]),
        pltpu.make_async_copy(index.at[:, pl.ds(start, length)], chosen, sems.at[1]),
        pltpu.make_async_copy(table, held_table, sems.at[2]),
        pltpu.make_async_copy(
            basis.at[last : last + channels, pl.ds(start, length)], direction, sems.at[3]
        ),
    ]
    for copy in copies:
        copy.start()

    def shared_rows(part):
        x, y, z = part[0:1], part[1:2], part[2:3]
        norm = x * x + y * y + z * z
        return x, y, z, lax.shift_right_logical(norm, 8), norm & 255, jnp.ones_like(x)

    def stacked(parts):
        return jnp.concatenate([p.astype(f32) for p in parts], 0)

    copies[0].wait()
    x, y, z, high, low, one = shared_rows(points[:, pl.ds(start, length)])
    sites = stacked([x, y, z, high, low, one, one, 0 * one])
    copies[1].wait()
    copies[2].wait()
    strength = jnp.zeros(chosen.shape, f32)
    for k in range(table.shape[1]):
        strength = jnp.where(chosen[...] == k, held_table[0:1, k : k + 1], strength)
    copies[3].wait()
    weighted = (direction[...] * strength).astype(bf16)
    ready[0:8, :length] = weighted
    ready[8:16, :length] = sites.astype(bf16)
    width = length // 8
    dense = [
        jnp.concatenate([sites[p : p + 1, k * width : (k + 1) * width] for k in range(8)], 0)
        for p in range(3)
    ]
    packed = jnp.concatenate([weighted] + [d.astype(bf16) for d in dense], 1)
    for k in range(rows):
        spread[k] = packed
    x, y, z, high, low, one = shared_rows(points[:, pl.ds(aim, wide)])
    sites = stacked([-2 * x, -2 * y, -2 * z, 256 * one, one, 256 * high, low, 0 * one])
    ready[:, length:] = jnp.concatenate([jnp.zeros_like(sites), sites], 0).astype(bf16)


def local_kernel(ready, basis, *rest):
    acc, gram, direction, own_high, own_low, kept, tiles, held, high, low, sems = rest
    half = kept.shape[1]
    length = ready.shape[1] - tiles.shape[2]
    targets = ready.at[8:16, length:]
    part = lax.axis_index(("col", "grp"))
    count, points = basis.shape
    pieces = sems.shape[0] - 1
    chunk = points // pieces
    channels, width = direction.shape
    here = pl.ds(pl.multiple_of(part * width, 128), width)
    own = pltpu.make_async_copy(
        basis.at[count - channels : count, here], direction, sems.at[pieces]
    )
    own.start()
    start = pl.multiple_of(jnp.minimum(part * 16, count - 16), 16)

    def place_of(k):
        first = k * chunk
        if first < half:
            return kept.at[:, first : first + chunk]
        return held.at[:, first - half : first - half + chunk]

    copies = []
    for k in range(points // chunk):
        cut = slice(k * chunk, (k + 1) * chunk)
        copies.append(pltpu.make_async_copy(basis.at[:, cut], place_of(k), sems.at[k]))
        copies[-1].start()

    acc[...] = jnp.zeros_like(acc)

    def sites_of(i):
        return ready[8:16, pl.ds(pl.multiple_of(i * STEP, STEP), STEP)]

    def weights_of(i):
        return ready[0:8, pl.ds(pl.multiple_of(i * STEP, STEP), STEP)]

    scatter_tiles(length // STEP, sites_of, weights_of, targets, tiles, acc, True, 2)

    total = jnp.zeros((16, count), f32)
    for k in range(points // chunk):
        cut = slice(k * chunk, (k + 1) * chunk)
        copies[k].wait()
        top, rest = split(place_of(k)[...])
        high[:, cut] = top
        low[:, cut] = rest
        mine = jnp.concatenate([high[pl.ds(start, 16), cut], low[pl.ds(start, 16), cut]], 0)
        first = lax.dot_general(mine, top, NT, preferred_element_type=f32)
        second = lax.dot_general(mine[:16], rest, NT, preferred_element_type=f32)
        total = total + (first[:16] + first[16:] + second)
    total = jnp.concatenate([total, jnp.zeros((16, 256 - count), f32)], 1)
    mixed = complex_mix(total)
    gram[...] = stack_halves(jnp.concatenate([mixed[0:4], mixed[8:12]], 0))
    own.wait()
    own_high[...] = high[:, here]
    own_low[...] = low[:, here]


def stack_halves(x):
    return jnp.concatenate([x[:, :128], x[:, 128:]], 0)


def join_halves(x):
    rows = x.shape[0] // 2
    return jnp.concatenate([x[:rows], x[rows:]], 1)


def project_kernel(keep, got, direction, high, low, gram, initial, packed):
    field = direction[...] - (keep[...] + got[...])
    initial[...] = stack_halves(field)
    count = high.shape[0]
    field_high, field_low = split(field)
    both = jnp.concatenate([field_high, field_low], 0)
    first = lax.dot_general(both, high[...], NT, preferred_element_type=f32)
    second = lax.dot_general(field_high, low[...], NT, preferred_element_type=f32)
    own = lax.dot_general(field, field, NT, preferred_element_type=f32, precision=highest)
    rest = jnp.zeros((8, 256 - count - 8), f32)
    products = jnp.concatenate([first[:8] + first[8:] + second, own, rest], 1)
    packed[0:8, :] = stack_halves(complex_mix(products)[0:4])
    packed[8:, :] = gram[...]


def final_kernel(total, shared, kept, basis, new, coef, norm, gram_high, gram_low, held, sems):
    parts = shared.shape[0]
    count, points = basis.shape
    width = 256
    chunk = 1024
    half = points - held.shape[1]
    copies = []
    for k in range(sems.shape[0]):
        cut = slice(k * chunk, (k + 1) * chunk)
        there = slice(half + k * chunk, half + (k + 1) * chunk)
        copies.append(pltpu.make_async_copy(basis.at[:, there], held.at[:, cut], sems.at[k]))
        copies[-1].start()
    scale = np.float32(1.0 / total)
    sums = shared[0, 16:24, :]
    for q in range(1, parts):
        sums = sums + shared[q, 16:24, :]
    upper = join_halves(sums)
    lane = lax.broadcasted_iota(jnp.int32, upper.shape, 1)
    lower = jnp.where(
        (lane & 4) == 0, -pltpu.roll(upper, width - 4, 1), pltpu.roll(upper, 4, 1)
    )
    sums = jnp.concatenate([upper, lower], 0)
    lane = lax.broadcasted_iota(jnp.int32, sums.shape, 1)
    sub = lax.broadcasted_iota(jnp.int32, sums.shape, 0)
    gram_high[...] = jnp.zeros_like(gram_high)
    gram_low[...] = jnp.zeros_like(gram_low)
    for q in range(count // 16):
        part = join_halves(shared[q, 24:40, :])
        pair = jnp.concatenate(
            [jnp.where(sub < 4, part, 0.0), jnp.where(sub < 4, pltpu.roll(part, 4, 0), 0.0)], 0
        )
        top, rest = split(pair)
        gram_high[16 * q : 16 * q + 16, :] = top
        gram_low[16 * q : 16 * q + 16, :] = rest

    def times_gram(x):
        top, rest = split(x)
        first = jnp.dot(
            jnp.concatenate([top, rest], 0), gram_high[...], preferred_element_type=f32
        )
        second = jnp.dot(top, gram_low[...], preferred_element_type=f32)
        return complex_mix(first[:8] + first[8:] + second)

    products = jnp.where(lane < count, sums, 0.0)
    once = products * scale
    mix = 2.0 * once - times_gram(once) * scale
    mix_high, mix_low = split(mix[:, :count])
    both = jnp.concatenate([mix_high, mix_low], 0)
    for k in range(points // chunk):
        cut = slice(k * chunk, (k + 1) * chunk)
        if k * chunk < half:
            columns = kept[:, cut]
        else:
            later = k - half // chunk
            copies[later].wait()
            columns = held[:, later * chunk : (later + 1) * chunk]
        top, rest = split(columns)
        first = jnp.dot(both, top, preferred_element_type=f32)
        second = jnp.dot(mix_high, rest, preferred_element_type=f32)
        each = chunk // width
        field = jnp.concatenate(
            [join_halves(shared[each * k + i, 0:16, :]) for i in range(each)], 1
        )
        new[:, cut] = field - (first[:8] + first[8:] + second)

    seen = products - 0.5 * times_gram(mix)
    cross = lax.dot_general(mix, seen, NT, preferred_element_type=f32, precision=highest)
    cross_t = lax.dot_general(seen, mix, NT, preferred_element_type=f32, precision=highest)
    own = pltpu.roll(sums, width - count, 1)[:, 0:8]
    result = (own - cross - cross_t) * scale
    norm[0] = result[0:4, 0:4]
    norm[1] = result[0:4, 4:8]

    row = lax.broadcasted_iota(jnp.int32, (width, 128), 0)
    column = lax.broadcasted_iota(jnp.int32, (width, 128), 1)
    wanted = ((row & 4) == 0) & (column == (row & 7) * 32 + lax.shift_right_logical(row, 3))
    top, rest = split(mix)
    least = (mix - top.astype(f32) - rest.astype(f32)).astype(bf16)
    chosen = jnp.dot(
        jnp.concatenate([top, rest, least], 0),
        jnp.where(wanted, 1.0, 0.0).astype(bf16),
        preferred_element_type=f32,
    )
    chosen = chosen[:8] + chosen[8:16] + chosen[16:]
    blocks = coef.shape[3]
    for k in range(4):
        moved = pltpu.roll(chosen, (128 - 32 * k) % 128, 1)
        coef[0, k] = moved[0:4, 0:blocks]
        coef[1, k] = moved[4:8, 0:blocks]


def gather_all(x, axis):
    length = lax.axis_size(axis)
    return lax.all_to_all(jnp.broadcast_to(x[None], (length, *x.shape)), axis, 0, 0, tiled=True)


VMEM = pl.BlockSpec(memory_space=pltpu.VMEM)
SMEM = pl.BlockSpec(memory_space=pltpu.SMEM)
HBM = pl.BlockSpec(memory_space=pltpu.HBM)


def params(room=16 << 20):
    return pltpu.CompilerParams(vmem_limit_bytes=room)


def cost(flops, size):
    return pl.CostEstimate(flops=flops, bytes_accessed=size, transcendentals=0)


def local(krylov_basis, lattice, strength_index, strength_table):
    blocks, channels, points = krylov_basis.shape
    inc = channels // 2
    count = blocks * channels
    rows = lax.axis_size("row")
    groups = lax.axis_size("grp")
    parts = lax.axis_size(("col", "grp"))
    total = points * rows
    own = points // parts
    wide = own * groups
    length = points // groups
    flat = krylov_basis.reshape(count, points)
    spread, ready = pl.pallas_call(
        prepare_kernel,
        in_specs=[HBM, HBM, HBM, HBM],
        out_specs=(VMEM, VMEM),
        out_shape=(
            jax.ShapeDtypeStruct((rows, 8, length + 3 * (length // 8)), bf16),
            jax.ShapeDtypeStruct((16, length + wide), bf16),
        ),
        scratch_shapes=[
            pltpu.VMEM((channels, length), f32),
            pltpu.VMEM((1, length), jnp.int32),
            pltpu.VMEM((1, strength_table.shape[0]), f32),
            pltpu.VMEM((3, points), jnp.int32),
            pltpu.SemaphoreType.DMA((4,)),
        ],
        compiler_params=params((64 << 20) - (64 << 10)),
        name="prepare",
    )(flat, lattice, strength_index[None, :], strength_table[None, :])
    gathered = lax.all_to_all(spread, "row", 0, 0, tiled=True)

    half = jax.ShapeDtypeStruct((channels, own), f32)
    held = pltpu.VMEM((2, STEP, wide), f32)
    begun, gram, direction, high, low, kept = pl.pallas_call(
        local_kernel,
        in_specs=[VMEM, HBM],
        out_specs=(VMEM,) * 6,
        out_shape=(
            jax.ShapeDtypeStruct((16, wide), f32),
            jax.ShapeDtypeStruct((16, 128), f32),
            half,
            jax.ShapeDtypeStruct((count, own), bf16),
            jax.ShapeDtypeStruct((count, own), bf16),
            jax.ShapeDtypeStruct((count, points // 2), f32),
        ),
        scratch_shapes=[
            held,
            pltpu.VMEM((count, points // 2), f32),
            pltpu.VMEM((count, points), bf16),
            pltpu.VMEM((count, points), bf16),
            pltpu.SemaphoreType.DMA((5,)),
        ],
        compiler_params=params(50 << 20),
        cost_estimate=cost(5_000_000_000, 8_000_000),
        name="scatter_local",
    )(ready, flat)

    keep, send = pl.pallas_call(
        remote_kernel,
        out_shape=(half, half),
        in_specs=[VMEM, VMEM, VMEM],
        out_specs=(VMEM, VMEM),
        scratch_shapes=[
            held,
            pltpu.VMEM((16, wide), f32),
            pltpu.VMEM((rows, 8, length), bf16),
        ],
        compiler_params=params(),
        cost_estimate=cost(20_000_000_000, 800_000),
        name="scatter_remote",
    )(ready, gathered, begun)
    got = lax.ppermute(send, "grp", [(i, groups - 1 - i) for i in range(groups)])

    initial, partial = pl.pallas_call(
        project_kernel,
        in_specs=[VMEM] * 6,
        out_specs=(VMEM, VMEM),
        out_shape=(jax.ShapeDtypeStruct((16, 128), f32), jax.ShapeDtypeStruct((24, 128), f32)),
        compiler_params=params(),
        name="project",
    )(keep, got, direction, high, low, gram)

    row_sums = jnp.sum(gather_all(partial, "row"), axis=0)
    shared = gather_all(jnp.concatenate([initial, row_sums], 0), ("col", "grp"))

    new_block, coef, norm = pl.pallas_call(
        functools.partial(final_kernel, total),
        in_specs=[VMEM, VMEM, HBM],
        out_specs=(VMEM, VMEM, VMEM),
        out_shape=(
            jax.ShapeDtypeStruct((channels, points), f32),
            jax.ShapeDtypeStruct((2, inc, inc, blocks), f32),
            jax.ShapeDtypeStruct((2, inc, inc), f32),
        ),
        scratch_shapes=[
            pltpu.VMEM((256, 256), bf16),
            pltpu.VMEM((256, 256), bf16),
            pltpu.VMEM((count, points // 2), f32),
            pltpu.SemaphoreType.DMA((points // 2 // 1024,)),
        ],
        compiler_params=params(50 << 20),
        name="finish",
    )(shared, kept, flat)
    return new_block, coef.transpose(3, 0, 1, 2), norm


def solution(mesh):
    in_specs = (P(None, None, "row"), P(None, "row"), P("row"), P())
    out_specs = (P(None, "row"), P(), P())
    return jax.shard_map(local, mesh=mesh, in_specs=in_specs, out_specs=out_specs, check_vma=False)
```

```python
import functools

import jax
import jax.numpy as jnp
import numpy as np
from jax import lax
from jax.experimental import pallas as pl
from jax.experimental.pallas import tpu as pltpu
from jax.sharding import PartitionSpec as P

f32 = jnp.float32
bf16 = jnp.bfloat16
highest = lax.Precision.HIGHEST
NT = (((1,), (1,)), ((), ()))
TN = (((0,), (0,)), ((), ()))

SINE = (4.4428816249751035, -7.307782340256801, 3.5971494246649565, -0.7893218692014636)
SUB = 256
STEP = 512


def green_pair(squared, masked):
    if masked:
        distinct = squared > 0.5
        squared = jnp.maximum(squared, 1.0)
    inverse = lax.rsqrt(squared)
    turns = (squared * inverse) * np.float32(1.0 / np.pi)
    part = turns - jnp.round(turns)
    z = part * part
    poly = z * np.float32(SINE[3]) + np.float32(SINE[2])
    poly = poly * z + np.float32(SINE[1])
    poly = poly * z + np.float32(SINE[0])
    sine = part * poly
    rest = 2.0 - sine * sine
    both = rest * inverse
    real_part = both - inverse
    imag_part = (sine * both) * lax.rsqrt(rest)
    if masked:
        real_part = jnp.where(distinct, real_part, 0.0)
        imag_part = jnp.where(distinct, imag_part, 0.0)
    return real_part.astype(bf16), imag_part.astype(bf16)


def scatter_tiles(tiles, sites_of, weights_of, targets, held, acc, masked, unroll):
    width = targets.shape[1]

    def fill(i, slot):
        held[slot] = lax.dot_general(sites_of(i), targets[...], TN, preferred_element_type=f32)

    def work(i, slot):
        weights = weights_of(i)
        for k in range(width // SUB):
            cut = slice(k * SUB, (k + 1) * SUB)
            real_part, imag_part = green_pair(held[slot, :, cut], masked)
            acc[0:8, cut] += jnp.dot(weights, real_part, preferred_element_type=f32)
            acc[8:16, cut] += jnp.dot(weights, imag_part, preferred_element_type=f32)

    fill(0, 0)

    def body(h, carry):
        for u in range(unroll):
            i = unroll * h + u
            fill(jnp.minimum(i + 1, tiles - 1), 1 - u % 2)
            work(i, u % 2)
        return carry

    lax.fori_loop(0, tiles // unroll, body, 0)


def remote_kernel(ready, sources, begun, keep, send, held, acc, spots):
    rows, _, length = spots.shape
    per_row = length // STEP
    row = lax.axis_index("row")
    targets = ready.at[8:16, length:]
    acc[...] = begun[...]
    width = length // 8

    def spread_sites(c, carry):
        x, y, z = [
            sources[c, :, length + k * width : length + (k + 1) * width].astype(f32)
            for k in range(3)
        ]
        norm = x * x + y * y + z * z
        high = jnp.floor(norm * np.float32(1.0 / 256.0))
        low = norm - 256.0 * high
        one = jnp.ones((2, width), f32)
        for k in range(8):
            parts = [p[k : k + 1] for p in (x, y, z, high, low)] + [one, 0.0 * one[0:1]]
            spots[c, :, k * width : (k + 1) * width] = jnp.concatenate(parts, 0).astype(bf16)
        return carry

    lax.fori_loop(0, rows, spread_sites, 0)

    def where(i):
        chunk = lax.rem(row + 1 + i // per_row, rows)
        return chunk, pl.ds(pl.multiple_of(lax.rem(i, per_row) * STEP, STEP), STEP)

    def sites_of(i):
        chunk, cut = where(i)
        return spots[chunk, :, cut]

    def weights_of(i):
        chunk, cut = where(i)
        return sources[chunk, :, cut]

    scatter_tiles((rows - 1) * per_row, sites_of, weights_of, targets, held, acc, False, 4)
    real = acc[0:8]
    imag = acc[8:16]
    upper = real[0:4] - imag[4:8]
    lower = real[4:8] + imag[0:4]
    both = jnp.concatenate([upper, lower], 0)
    half = both.shape[1] // 2
    first, second = both[:, :half], both[:, half:]
    mine = lax.axis_index("grp") == 0
    keep[...] = jnp.where(mine, first, second)
    send[...] = jnp.where(mine, second, first)


def split(x):
    high = x.astype(bf16)
    return high, (x - high.astype(f32)).astype(bf16)


def swap_parts(x, rows):
    lane = lax.broadcasted_iota(jnp.int32, x.shape, 1)
    width = x.shape[1]
    rolled = pltpu.roll(x, rows - 4, 0)
    return jnp.where((lane & 4) == 0, pltpu.roll(rolled, width - 4, 1), pltpu.roll(rolled, 4, 1))


def complex_mix(products):
    lane = lax.broadcasted_iota(jnp.int32, products.shape, 1)
    sub = lax.broadcasted_iota(jnp.int32, products.shape, 0)
    swapped = swap_parts(products, products.shape[0])
    same = ((lane & 4) == 0) == ((sub & 4) == 0)
    return products + jnp.where(same, swapped, -swapped)


def prepare_kernel(basis, lattice, index, table, spread, ready, *scratch):
    direction, chosen, held_table, points, aims, sems = scratch
    rows = spread.shape[0]
    length = points.shape[1]
    wide = aims.shape[1]
    channels = direction.shape[0]
    aim = pl.multiple_of(lax.axis_index("col") * wide, 128)
    start = pl.multiple_of(lax.axis_index("grp") * length, 128)
    last = basis.shape[0] - channels
    copies = [
        pltpu.make_async_copy(lattice.at[:, pl.ds(start, length)], points, sems.at[0]),
        pltpu.make_async_copy(index.at[:, pl.ds(start, length)], chosen, sems.at[1]),
        pltpu.make_async_copy(table, held_table, sems.at[2]),
        pltpu.make_async_copy(
            basis.at[last : last + channels, pl.ds(start, length)], direction, sems.at[3]
        ),
        pltpu.make_async_copy(lattice.at[:, pl.ds(aim, wide)], aims, sems.at[4]),
    ]
    for copy in copies:
        copy.start()

    def shared_rows(part):
        x, y, z = part[0:1], part[1:2], part[2:3]
        norm = x * x + y * y + z * z
        return x, y, z, lax.shift_right_logical(norm, 8), norm & 255, jnp.ones_like(x)

    def stacked(parts):
        return jnp.concatenate([p.astype(f32) for p in parts], 0)

    copies[0].wait()
    x, y, z, high, low, one = shared_rows(points[...])
    sites = stacked([x, y, z, high, low, one, one, 0 * one])
    copies[1].wait()
    copies[2].wait()
    strength = jnp.zeros(chosen.shape, f32)
    for k in range(table.shape[1]):
        strength = jnp.where(chosen[...] == k, held_table[0:1, k : k + 1], strength)
    copies[3].wait()
    weighted = (direction[...] * strength).astype(bf16)
    ready[0:8, :length] = weighted
    ready[8:16, :length] = sites.astype(bf16)
    width = length // 8
    dense = [
        jnp.concatenate([sites[p : p + 1, k * width : (k + 1) * width] for k in range(8)], 0)
        for p in range(3)
    ]
    packed = jnp.concatenate([weighted] + [d.astype(bf16) for d in dense], 1)
    for k in range(rows):
        spread[k] = packed
    copies[4].wait()
    x, y, z, high, low, one = shared_rows(aims[...])
    sites = stacked([-2 * x, -2 * y, -2 * z, 256 * one, one, 256 * high, low, 0 * one])
    ready[:, length:] = jnp.concatenate([jnp.zeros_like(sites), sites], 0).astype(bf16)


def local_kernel(ready, basis, *rest):
    acc, gram, direction, own_high, own_low, kept_high, kept_low, tiles, kept, held, high, low, sems = rest
    half = kept.shape[1]
    length = ready.shape[1] - tiles.shape[2]
    targets = ready.at[8:16, length:]
    part = lax.axis_index(("col", "grp"))
    count, points = basis.shape
    pieces = sems.shape[0] - 1
    chunk = points // pieces
    channels, width = direction.shape
    here = pl.ds(pl.multiple_of(part * width, 128), width)
    own = pltpu.make_async_copy(
        basis.at[count - channels : count, here], direction, sems.at[pieces]
    )
    own.start()
    start = pl.multiple_of(jnp.minimum(part * 16, count - 16), 16)

    def place_of(k):
        first = k * chunk
        if first < half:
            return kept.at[:, first : first + chunk]
        return held.at[:, first - half : first - half + chunk]

    copies = []
    for k in range(points // chunk):
        cut = slice(k * chunk, (k + 1) * chunk)
        copies.append(pltpu.make_async_copy(basis.at[:, cut], place_of(k), sems.at[k]))
        copies[-1].start()

    acc[...] = jnp.zeros_like(acc)

    def sites_of(i):
        return ready[8:16, pl.ds(pl.multiple_of(i * STEP, STEP), STEP)]

    def weights_of(i):
        return ready[0:8, pl.ds(pl.multiple_of(i * STEP, STEP), STEP)]

    scatter_tiles(length // STEP, sites_of, weights_of, targets, tiles, acc, True, 2)

    total = jnp.zeros((16, count), f32)
    for k in range(points // chunk):
        cut = slice(k * chunk, (k + 1) * chunk)
        copies[k].wait()
        top, rest = split(place_of(k)[...])
        high[:, cut] = top
        low[:, cut] = rest
        mine = jnp.concatenate([high[pl.ds(start, 16), cut], low[pl.ds(start, 16), cut]], 0)
        first = lax.dot_general(mine, top, NT, preferred_element_type=f32)
        second = lax.dot_general(mine[:16], rest, NT, preferred_element_type=f32)
        total = total + (first[:16] + first[16:] + second)
    total = jnp.concatenate([total, jnp.zeros((16, 256 - count), f32)], 1)
    mixed = complex_mix(total)
    gram[...] = stack_halves(jnp.concatenate([mixed[0:4], mixed[8:12]], 0))
    own.wait()
    own_high[...] = high[:, here]
    own_low[...] = low[:, here]
    kept_high[...] = high[:, :half]
    kept_low[...] = low[:, :half]


def stack_halves(x):
    return jnp.concatenate([x[:, :128], x[:, 128:]], 0)


def join_halves(x):
    rows = x.shape[0] // 2
    return jnp.concatenate([x[:rows], x[rows:]], 1)


def project_kernel(keep, got, direction, high, low, gram, initial, packed):
    field = direction[...] - (keep[...] + got[...])
    initial[...] = stack_halves(field)
    count = high.shape[0]
    field_high, field_low = split(field)
    both = jnp.concatenate([field_high, field_low], 0)
    first = lax.dot_general(both, high[...], NT, preferred_element_type=f32)
    second = lax.dot_general(field_high, low[...], NT, preferred_element_type=f32)
    own = lax.dot_general(field, field, NT, preferred_element_type=f32, precision=highest)
    rest = jnp.zeros((8, 256 - count - 8), f32)
    products = jnp.concatenate([first[:8] + first[8:] + second, own, rest], 1)
    packed[0:8, :] = stack_halves(complex_mix(products)[0:4])
    packed[8:, :] = gram[...]


def final_kernel(total, shared, kept_high, kept_low, basis, new, coef, norm, *scratch):
    gram_high, gram_low, held, sems = scratch
    parts = shared.shape[0]
    count, points = basis.shape
    width = 256
    chunk = 512
    half = points - held.shape[1]
    copies = []
    for k in range(sems.shape[0]):
        cut = slice(k * chunk, (k + 1) * chunk)
        there = slice(half + k * chunk, half + (k + 1) * chunk)
        copies.append(pltpu.make_async_copy(basis.at[:, there], held.at[:, cut], sems.at[k]))
        copies[-1].start()
    scale = np.float32(1.0 / total)
    sums = shared[0, 16:24, :]
    for q in range(1, parts):
        sums = sums + shared[q, 16:24, :]
    upper = join_halves(sums)
    lane = lax.broadcasted_iota(jnp.int32, upper.shape, 1)
    lower = jnp.where(
        (lane & 4) == 0, -pltpu.roll(upper, width - 4, 1), pltpu.roll(upper, 4, 1)
    )
    sums = jnp.concatenate([upper, lower], 0)
    lane = lax.broadcasted_iota(jnp.int32, sums.shape, 1)
    sub = lax.broadcasted_iota(jnp.int32, sums.shape, 0)
    gram_high[...] = jnp.zeros_like(gram_high)
    gram_low[...] = jnp.zeros_like(gram_low)
    for q in range(count // 16):
        part = join_halves(shared[q, 24:40, :])
        pair = jnp.concatenate(
            [jnp.where(sub < 4, part, 0.0), jnp.where(sub < 4, pltpu.roll(part, 4, 0), 0.0)], 0
        )
        top, rest = split(pair)
        gram_high[16 * q : 16 * q + 16, :] = top
        gram_low[16 * q : 16 * q + 16, :] = rest

    def times_gram(x):
        top, rest = split(x)
        first = jnp.dot(
            jnp.concatenate([top, rest], 0), gram_high[...], preferred_element_type=f32
        )
        second = jnp.dot(top, gram_low[...], preferred_element_type=f32)
        return complex_mix(first[:8] + first[8:] + second)

    products = jnp.where(lane < count, sums, 0.0)
    once = products * scale
    mix = 2.0 * once - times_gram(once) * scale
    mix_high, mix_low = split(mix[:, :count])
    both = jnp.concatenate([mix_high, mix_low], 0)
    for k in range(points // chunk):
        cut = slice(k * chunk, (k + 1) * chunk)
        if k * chunk < half:
            top, rest = kept_high[:, cut], kept_low[:, cut]
        else:
            later = k - half // chunk
            copies[later].wait()
            top, rest = split(held[:, later * chunk : (later + 1) * chunk])
        first = jnp.dot(both, top, preferred_element_type=f32)
        second = jnp.dot(mix_high, rest, preferred_element_type=f32)
        each = chunk // width
        field = jnp.concatenate(
            [join_halves(shared[each * k + i, 0:16, :]) for i in range(each)], 1
        )
        new[:, cut] = field - (first[:8] + first[8:] + second)

    seen = products - 0.5 * times_gram(mix)
    cross = lax.dot_general(mix, seen, NT, preferred_element_type=f32, precision=highest)
    cross_t = lax.dot_general(seen, mix, NT, preferred_element_type=f32, precision=highest)
    own = pltpu.roll(sums, width - count, 1)[:, 0:8]
    result = (own - cross - cross_t) * scale
    norm[0] = result[0:4, 0:4]
    norm[1] = result[0:4, 4:8]

    row = lax.broadcasted_iota(jnp.int32, (width, 128), 0)
    column = lax.broadcasted_iota(jnp.int32, (width, 128), 1)
    wanted = ((row & 4) == 0) & (column == (row & 7) * 32 + lax.shift_right_logical(row, 3))
    top, rest = split(mix)
    least = (mix - top.astype(f32) - rest.astype(f32)).astype(bf16)
    chosen = jnp.dot(
        jnp.concatenate([top, rest, least], 0),
        jnp.where(wanted, 1.0, 0.0).astype(bf16),
        preferred_element_type=f32,
    )
    chosen = chosen[:8] + chosen[8:16] + chosen[16:]
    blocks = coef.shape[3]
    for k in range(4):
        moved = pltpu.roll(chosen, (128 - 32 * k) % 128, 1)
        coef[0, k] = moved[0:4, 0:blocks]
        coef[1, k] = moved[4:8, 0:blocks]


def gather_all(x, axis):
    length = lax.axis_size(axis)
    return lax.all_to_all(jnp.broadcast_to(x[None], (length, *x.shape)), axis, 0, 0, tiled=True)


VMEM = pl.BlockSpec(memory_space=pltpu.VMEM)
SMEM = pl.BlockSpec(memory_space=pltpu.SMEM)
HBM = pl.BlockSpec(memory_space=pltpu.HBM)


def params(room=16 << 20):
    return pltpu.CompilerParams(vmem_limit_bytes=room)


def cost(flops, size):
    return pl.CostEstimate(flops=flops, bytes_accessed=size, transcendentals=0)


def local(krylov_basis, lattice, strength_index, strength_table):
    blocks, channels, points = krylov_basis.shape
    inc = channels // 2
    count = blocks * channels
    rows = lax.axis_size("row")
    groups = lax.axis_size("grp")
    parts = lax.axis_size(("col", "grp"))
    total = points * rows
    own = points // parts
    wide = own * groups
    length = points // groups
    flat = krylov_basis.reshape(count, points)
    spread, ready = pl.pallas_call(
        prepare_kernel,
        in_specs=[HBM, HBM, HBM, HBM],
        out_specs=(VMEM, VMEM),
        out_shape=(
            jax.ShapeDtypeStruct((rows, 8, length + 3 * (length // 8)), bf16),
            jax.ShapeDtypeStruct((16, length + wide), bf16),
        ),
        scratch_shapes=[
            pltpu.VMEM((channels, length), f32),
            pltpu.VMEM((1, length), jnp.int32),
            pltpu.VMEM((1, strength_table.shape[0]), f32),
            pltpu.VMEM((3, length), jnp.int32),
            pltpu.VMEM((3, wide), jnp.int32),
            pltpu.SemaphoreType.DMA((5,)),
        ],
        compiler_params=params((64 << 20) - (64 << 10)),
        name="prepare",
    )(flat, lattice, strength_index[None, :], strength_table[None, :])
    gathered = lax.all_to_all(spread, "row", 0, 0, tiled=True)

    half = jax.ShapeDtypeStruct((channels, own), f32)
    held = pltpu.VMEM((2, STEP, wide), f32)
    begun, gram, direction, high, low, kept_high, kept_low = pl.pallas_call(
        local_kernel,
        in_specs=[VMEM, HBM],
        out_specs=(VMEM,) * 7,
        out_shape=(
            jax.ShapeDtypeStruct((16, wide), f32),
            jax.ShapeDtypeStruct((16, 128), f32),
            half,
            jax.ShapeDtypeStruct((count, own), bf16),
            jax.ShapeDtypeStruct((count, own), bf16),
            jax.ShapeDtypeStruct((count, points // 2), bf16),
            jax.ShapeDtypeStruct((count, points // 2), bf16),
        ),
        scratch_shapes=[
            held,
            pltpu.VMEM((count, points // 2), f32),
            pltpu.VMEM((count, points // 2), f32),
            pltpu.VMEM((count, points), bf16),
            pltpu.VMEM((count, points), bf16),
            pltpu.SemaphoreType.DMA((9,)),
        ],
        compiler_params=params(50 << 20),
        cost_estimate=cost(5_000_000_000, 8_000_000),
        name="scatter_local",
    )(ready, flat)

    keep, send = pl.pallas_call(
        remote_kernel,
        out_shape=(half, half),
        in_specs=[VMEM, VMEM, VMEM],
        out_specs=(VMEM, VMEM),
        scratch_shapes=[
            held,
            pltpu.VMEM((16, wide), f32),
            pltpu.VMEM((rows, 8, length), bf16),
        ],
        compiler_params=params(),
        cost_estimate=cost(20_000_000_000, 800_000),
        name="scatter_remote",
    )(ready, gathered, begun)
    got = lax.ppermute(send, "grp", [(i, groups - 1 - i) for i in range(groups)])

    initial, partial = pl.pallas_call(
        project_kernel,
        in_specs=[VMEM] * 6,
        out_specs=(VMEM, VMEM),
        out_shape=(jax.ShapeDtypeStruct((16, 128), f32), jax.ShapeDtypeStruct((24, 128), f32)),
        compiler_params=params(),
        name="project",
    )(keep, got, direction, high, low, gram)

    row_sums = jnp.sum(gather_all(partial, "row"), axis=0)
    shared = gather_all(jnp.concatenate([initial, row_sums], 0), ("col", "grp"))

    new_block, coef, norm = pl.pallas_call(
        functools.partial(final_kernel, total),
        in_specs=[VMEM, VMEM, VMEM, HBM],
        out_specs=(VMEM, VMEM, VMEM),
        out_shape=(
            jax.ShapeDtypeStruct((channels, points), f32),
            jax.ShapeDtypeStruct((2, inc, inc, blocks), f32),
            jax.ShapeDtypeStruct((2, inc, inc), f32),
        ),
        scratch_shapes=[
            pltpu.VMEM((256, 256), bf16),
            pltpu.VMEM((256, 256), bf16),
            pltpu.VMEM((count, points // 2), f32),
            pltpu.SemaphoreType.DMA((points // 2 // 512,)),
        ],
        compiler_params=params(50 << 20),
        name="finish",
    )(shared, kept_high, kept_low, flat)
    return new_block, coef.transpose(3, 0, 1, 2), norm


def solution(mesh):
    in_specs = (P(None, None, "row"), P(None, "row"), P("row"), P())
    out_specs = (P(None, "row"), P(), P())
    return jax.shard_map(local, mesh=mesh, in_specs=in_specs, out_specs=out_specs, check_vma=False)
```

```python
import functools

import jax
import jax.numpy as jnp
import numpy as np
from jax import lax
from jax.experimental import pallas as pl
from jax.experimental.pallas import tpu as pltpu
from jax.sharding import PartitionSpec as P

f32 = jnp.float32
bf16 = jnp.bfloat16
highest = lax.Precision.HIGHEST
NT = (((1,), (1,)), ((), ()))
TN = (((0,), (0,)), ((), ()))

SINE = (4.4428816249751035, -7.307782340256801, 3.5971494246649565, -0.7893218692014636)
SUB = 256
STEP = 512


def green_pair(squared, masked):
    if masked:
        distinct = squared > 0.5
        squared = jnp.maximum(squared, 1.0)
    inverse = lax.rsqrt(squared)
    turns = (squared * inverse) * np.float32(1.0 / np.pi)
    part = turns - jnp.round(turns)
    z = part * part
    poly = z * np.float32(SINE[3]) + np.float32(SINE[2])
    poly = poly * z + np.float32(SINE[1])
    poly = poly * z + np.float32(SINE[0])
    sine = part * poly
    rest = 2.0 - sine * sine
    both = rest * inverse
    real_part = both - inverse
    imag_part = (sine * both) * lax.rsqrt(rest)
    if masked:
        real_part = jnp.where(distinct, real_part, 0.0)
        imag_part = jnp.where(distinct, imag_part, 0.0)
    return real_part.astype(bf16), imag_part.astype(bf16)


def scatter_tiles(tiles, sites_of, weights_of, targets, held, acc, masked, unroll):
    width = targets.shape[1]

    def fill(i, slot):
        held[slot] = lax.dot_general(sites_of(i), targets[...], TN, preferred_element_type=f32)

    def work(i, slot):
        weights = weights_of(i)
        for k in range(width // SUB):
            cut = slice(k * SUB, (k + 1) * SUB)
            real_part, imag_part = green_pair(held[slot, :, cut], masked)
            acc[0:8, cut] += jnp.dot(weights, real_part, preferred_element_type=f32)
            acc[8:16, cut] += jnp.dot(weights, imag_part, preferred_element_type=f32)

    fill(0, 0)

    def body(h, carry):
        for u in range(unroll):
            i = unroll * h + u
            fill(jnp.minimum(i + 1, tiles - 1), 1 - u % 2)
            work(i, u % 2)
        return carry

    lax.fori_loop(0, tiles // unroll, body, 0)


def remote_kernel(ready, sources, begun, keep, send, held, acc, spots):
    rows, _, length = spots.shape
    per_row = length // STEP
    row = lax.axis_index("row")
    targets = ready.at[8:16, length:]
    acc[...] = begun[...]
    width = length // 8

    def spread_sites(c, carry):
        x, y, z = [
            sources[c, :, length + k * width : length + (k + 1) * width].astype(f32)
            for k in range(3)
        ]
        norm = x * x + y * y + z * z
        high = jnp.floor(norm * np.float32(1.0 / 256.0))
        low = norm - 256.0 * high
        one = jnp.ones((2, width), f32)
        for k in range(8):
            parts = [p[k : k + 1] for p in (x, y, z, high, low)] + [one, 0.0 * one[0:1]]
            spots[c, :, k * width : (k + 1) * width] = jnp.concatenate(parts, 0).astype(bf16)
        return carry

    lax.fori_loop(0, rows, spread_sites, 0)

    def where(i):
        chunk = lax.rem(row + 1 + i // per_row, rows)
        return chunk, pl.ds(pl.multiple_of(lax.rem(i, per_row) * STEP, STEP), STEP)

    def sites_of(i):
        chunk, cut = where(i)
        return spots[chunk, :, cut]

    def weights_of(i):
        chunk, cut = where(i)
        return sources[chunk, :, cut]

    scatter_tiles((rows - 1) * per_row, sites_of, weights_of, targets, held, acc, False, 4)
    real = acc[0:8]
    imag = acc[8:16]
    upper = real[0:4] - imag[4:8]
    lower = real[4:8] + imag[0:4]
    both = jnp.concatenate([upper, lower], 0)
    half = both.shape[1] // 2
    first, second = both[:, :half], both[:, half:]
    mine = lax.axis_index("grp") == 0
    keep[...] = jnp.where(mine, first, second)
    send[...] = jnp.where(mine, second, first)


def split(x):
    high = x.astype(bf16)
    return high, (x - high.astype(f32)).astype(bf16)


def swap_parts(x, rows):
    lane = lax.broadcasted_iota(jnp.int32, x.shape, 1)
    width = x.shape[1]
    rolled = pltpu.roll(x, rows - 4, 0)
    return jnp.where((lane & 4) == 0, pltpu.roll(rolled, width - 4, 1), pltpu.roll(rolled, 4, 1))


def complex_mix(products):
    lane = lax.broadcasted_iota(jnp.int32, products.shape, 1)
    sub = lax.broadcasted_iota(jnp.int32, products.shape, 0)
    swapped = swap_parts(products, products.shape[0])
    same = ((lane & 4) == 0) == ((sub & 4) == 0)
    return products + jnp.where(same, swapped, -swapped)


def prepare_kernel(basis, lattice, index, table, spread, ready, *scratch):
    direction, chosen, held_table, points, aims, sems = scratch
    rows = spread.shape[0]
    length = points.shape[1]
    wide = aims.shape[1]
    channels = direction.shape[0]
    aim = pl.multiple_of(lax.axis_index("col") * wide, 128)
    start = pl.multiple_of(lax.axis_index("grp") * length, 128)
    last = basis.shape[0] - channels
    copies = [
        pltpu.make_async_copy(lattice.at[:, pl.ds(start, length)], points, sems.at[0]),
        pltpu.make_async_copy(index.at[:, pl.ds(start, length)], chosen, sems.at[1]),
        pltpu.make_async_copy(table, held_table, sems.at[2]),
        pltpu.make_async_copy(
            basis.at[last : last + channels, pl.ds(start, length)], direction, sems.at[3]
        ),
        pltpu.make_async_copy(lattice.at[:, pl.ds(aim, wide)], aims, sems.at[4]),
    ]
    for copy in copies:
        copy.start()

    def shared_rows(part):
        x, y, z = part[0:1], part[1:2], part[2:3]
        norm = x * x + y * y + z * z
        return x, y, z, lax.shift_right_logical(norm, 8), norm & 255, jnp.ones_like(x)

    def stacked(parts):
        return jnp.concatenate([p.astype(f32) for p in parts], 0)

    copies[0].wait()
    x, y, z, high, low, one = shared_rows(points[...])
    sites = stacked([x, y, z, high, low, one, one, 0 * one])
    copies[1].wait()
    copies[2].wait()
    strength = jnp.zeros(chosen.shape, f32)
    for k in range(table.shape[1]):
        strength = jnp.where(chosen[...] == k, held_table[0:1, k : k + 1], strength)
    copies[3].wait()
    weighted = (direction[...] * strength).astype(bf16)
    ready[0:8, :length] = weighted
    ready[8:16, :length] = sites.astype(bf16)
    width = length // 8
    dense = [
        jnp.concatenate([sites[p : p + 1, k * width : (k + 1) * width] for k in range(8)], 0)
        for p in range(3)
    ]
    packed = jnp.concatenate([weighted] + [d.astype(bf16) for d in dense], 1)
    for k in range(rows):
        spread[k] = packed
    copies[4].wait()
    x, y, z, high, low, one = shared_rows(aims[...])
    sites = stacked([-2 * x, -2 * y, -2 * z, 256 * one, one, 256 * high, low, 0 * one])
    ready[:, length:] = jnp.concatenate([jnp.zeros_like(sites), sites], 0).astype(bf16)


def local_kernel(ready, basis, *rest):
    acc, gram, direction, own_high, own_low, kept, tiles, held, high, low, sems = rest
    half = kept.shape[1]
    length = ready.shape[1] - tiles.shape[2]
    targets = ready.at[8:16, length:]
    part = lax.axis_index(("col", "grp"))
    count, points = basis.shape
    pieces = sems.shape[0] - 1
    chunk = points // pieces
    channels, width = direction.shape
    here = pl.ds(pl.multiple_of(part * width, 128), width)
    own = pltpu.make_async_copy(
        basis.at[count - channels : count, here], direction, sems.at[pieces]
    )
    own.start()
    start = pl.multiple_of(jnp.minimum(part * 16, count - 16), 16)

    def place_of(k):
        first = k * chunk
        if first < half:
            return kept.at[:, first : first + chunk]
        return held.at[:, first - half : first - half + chunk]

    copies = []
    for k in range(points // chunk):
        cut = slice(k * chunk, (k + 1) * chunk)
        copies.append(pltpu.make_async_copy(basis.at[:, cut], place_of(k), sems.at[k]))
        copies[-1].start()

    acc[...] = jnp.zeros_like(acc)

    def sites_of(i):
        return ready[8:16, pl.ds(pl.multiple_of(i * STEP, STEP), STEP)]

    def weights_of(i):
        return ready[0:8, pl.ds(pl.multiple_of(i * STEP, STEP), STEP)]

    scatter_tiles(length // STEP, sites_of, weights_of, targets, tiles, acc, True, 2)

    total = jnp.zeros((16, count), f32)
    for k in range(points // chunk):
        cut = slice(k * chunk, (k + 1) * chunk)
        copies[k].wait()
        top, rest = split(place_of(k)[...])
        high[:, cut] = top
        low[:, cut] = rest
        mine = jnp.concatenate([high[pl.ds(start, 16), cut], low[pl.ds(start, 16), cut]], 0)
        first = lax.dot_general(mine, top, NT, preferred_element_type=f32)
        second = lax.dot_general(mine[:16], rest, NT, preferred_element_type=f32)
        total = total + (first[:16] + first[16:] + second)
    total = jnp.concatenate([total, jnp.zeros((16, 256 - count), f32)], 1)
    mixed = complex_mix(total)
    gram[...] = stack_halves(jnp.concatenate([mixed[0:4], mixed[8:12]], 0))
    own.wait()
    own_high[...] = high[:, here]
    own_low[...] = low[:, here]


def stack_halves(x):
    return jnp.concatenate([x[:, :128], x[:, 128:]], 0)


def join_halves(x):
    rows = x.shape[0] // 2
    return jnp.concatenate([x[:rows], x[rows:]], 1)


def project_kernel(keep, got, direction, high, low, gram, initial, packed):
    field = direction[...] - (keep[...] + got[...])
    initial[...] = stack_halves(field)
    count = high.shape[0]
    field_high, field_low = split(field)
    both = jnp.concatenate([field_high, field_low], 0)
    first = lax.dot_general(both, high[...], NT, preferred_element_type=f32)
    second = lax.dot_general(field_high, low[...], NT, preferred_element_type=f32)
    own = lax.dot_general(field, field, NT, preferred_element_type=f32, precision=highest)
    rest = jnp.zeros((8, 256 - count - 8), f32)
    products = jnp.concatenate([first[:8] + first[8:] + second, own, rest], 1)
    packed[0:8, :] = stack_halves(complex_mix(products)[0:4])
    packed[8:, :] = gram[...]


def final_kernel(total, shared, kept, basis, new, coef, norm, gram_high, gram_low, held, sems):
    parts = shared.shape[0]
    count, points = basis.shape
    width = 256
    chunk = 256
    half = points - held.shape[1]
    copies = []
    for k in range(sems.shape[0]):
        cut = slice(k * chunk, (k + 1) * chunk)
        there = slice(half + k * chunk, half + (k + 1) * chunk)
        copies.append(pltpu.make_async_copy(basis.at[:, there], held.at[:, cut], sems.at[k]))
        copies[-1].start()
    scale = np.float32(1.0 / total)
    sums = shared[0, 16:24, :]
    for q in range(1, parts):
        sums = sums + shared[q, 16:24, :]
    upper = join_halves(sums)
    lane = lax.broadcasted_iota(jnp.int32, upper.shape, 1)
    lower = jnp.where(
        (lane & 4) == 0, -pltpu.roll(upper, width - 4, 1), pltpu.roll(upper, 4, 1)
    )
    sums = jnp.concatenate([upper, lower], 0)
    lane = lax.broadcasted_iota(jnp.int32, sums.shape, 1)
    sub = lax.broadcasted_iota(jnp.int32, sums.shape, 0)
    gram_high[...] = jnp.zeros_like(gram_high)
    gram_low[...] = jnp.zeros_like(gram_low)
    for q in range(count // 16):
        part = join_halves(shared[q, 24:40, :])
        pair = jnp.concatenate(
            [jnp.where(sub < 4, part, 0.0), jnp.where(sub < 4, pltpu.roll(part, 4, 0), 0.0)], 0
        )
        top, rest = split(pair)
        gram_high[16 * q : 16 * q + 16, :] = top
        gram_low[16 * q : 16 * q + 16, :] = rest

    def times_gram(x):
        top, rest = split(x)
        first = jnp.dot(
            jnp.concatenate([top, rest], 0), gram_high[...], preferred_element_type=f32
        )
        second = jnp.dot(top, gram_low[...], preferred_element_type=f32)
        return complex_mix(first[:8] + first[8:] + second)

    products = jnp.where(lane < count, sums, 0.0)
    once = products * scale
    mix = 2.0 * once - times_gram(once) * scale
    mix_high, mix_low = split(mix[:, :count])
    both = jnp.concatenate([mix_high, mix_low], 0)
    for k in range(points // chunk):
        cut = slice(k * chunk, (k + 1) * chunk)
        if k * chunk < half:
            columns = kept[:, cut]
        else:
            later = k - half // chunk
            copies[later].wait()
            columns = held[:, later * chunk : (later + 1) * chunk]
        top, rest = split(columns)
        first = jnp.dot(both, top, preferred_element_type=f32)
        second = jnp.dot(mix_high, rest, preferred_element_type=f32)
        each = chunk // width
        field = jnp.concatenate(
            [join_halves(shared[each * k + i, 0:16, :]) for i in range(each)], 1
        )
        new[:, cut] = field - (first[:8] + first[8:] + second)

    seen = products - 0.5 * times_gram(mix)
    cross = lax.dot_general(mix, seen, NT, preferred_element_type=f32, precision=highest)
    cross_t = lax.dot_general(seen, mix, NT, preferred_element_type=f32, precision=highest)
    own = pltpu.roll(sums, width - count, 1)[:, 0:8]
    result = (own - cross - cross_t) * scale
    norm[0] = result[0:4, 0:4]
    norm[1] = result[0:4, 4:8]

    row = lax.broadcasted_iota(jnp.int32, (width, 128), 0)
    column = lax.broadcasted_iota(jnp.int32, (width, 128), 1)
    wanted = ((row & 4) == 0) & (column == (row & 7) * 32 + lax.shift_right_logical(row, 3))
    top, rest = split(mix)
    least = (mix - top.astype(f32) - rest.astype(f32)).astype(bf16)
    chosen = jnp.dot(
        jnp.concatenate([top, rest, least], 0),
        jnp.where(wanted, 1.0, 0.0).astype(bf16),
        preferred_element_type=f32,
    )
    chosen = chosen[:8] + chosen[8:16] + chosen[16:]
    blocks = coef.shape[3]
    for k in range(4):
        moved = pltpu.roll(chosen, (128 - 32 * k) % 128, 1)
        coef[0, k] = moved[0:4, 0:blocks]
        coef[1, k] = moved[4:8, 0:blocks]


def gather_all(x, axis):
    length = lax.axis_size(axis)
    return lax.all_to_all(jnp.broadcast_to(x[None], (length, *x.shape)), axis, 0, 0, tiled=True)


VMEM = pl.BlockSpec(memory_space=pltpu.VMEM)
SMEM = pl.BlockSpec(memory_space=pltpu.SMEM)
HBM = pl.BlockSpec(memory_space=pltpu.HBM)


def params(room=16 << 20):
    return pltpu.CompilerParams(vmem_limit_bytes=room)


def cost(flops, size):
    return pl.CostEstimate(flops=flops, bytes_accessed=size, transcendentals=0)


def local(krylov_basis, lattice, strength_index, strength_table):
    blocks, channels, points = krylov_basis.shape
    inc = channels // 2
    count = blocks * channels
    rows = lax.axis_size("row")
    groups = lax.axis_size("grp")
    parts = lax.axis_size(("col", "grp"))
    total = points * rows
    own = points // parts
    wide = own * groups
    length = points // groups
    flat = krylov_basis.reshape(count, points)
    spread, ready = pl.pallas_call(
        prepare_kernel,
        in_specs=[HBM, HBM, HBM, HBM],
        out_specs=(VMEM, VMEM),
        out_shape=(
            jax.ShapeDtypeStruct((rows, 8, length + 3 * (length // 8)), bf16),
            jax.ShapeDtypeStruct((16, length + wide), bf16),
        ),
        scratch_shapes=[
            pltpu.VMEM((channels, length), f32),
            pltpu.VMEM((1, length), jnp.int32),
            pltpu.VMEM((1, strength_table.shape[0]), f32),
            pltpu.VMEM((3, length), jnp.int32),
            pltpu.VMEM((3, wide), jnp.int32),
            pltpu.SemaphoreType.DMA((5,)),
        ],
        compiler_params=params((64 << 20) - (64 << 10)),
        name="prepare",
    )(flat, lattice, strength_index[None, :], strength_table[None, :])
    gathered = lax.all_to_all(spread, "row", 0, 0, tiled=True)

    half = jax.ShapeDtypeStruct((channels, own), f32)
    held = pltpu.VMEM((2, STEP, wide), f32)
    begun, gram, direction, high, low, kept = pl.pallas_call(
        local_kernel,
        in_specs=[VMEM, HBM],
        out_specs=(VMEM,) * 6,
        out_shape=(
            jax.ShapeDtypeStruct((16, wide), f32),
            jax.ShapeDtypeStruct((16, 128), f32),
            half,
            jax.ShapeDtypeStruct((count, own), bf16),
            jax.ShapeDtypeStruct((count, own), bf16),
            jax.ShapeDtypeStruct((count, points // 2), f32),
        ),
        scratch_shapes=[
            held,
            pltpu.VMEM((count, points // 2), f32),
            pltpu.VMEM((count, points), bf16),
            pltpu.VMEM((count, points), bf16),
            pltpu.SemaphoreType.DMA((9,)),
        ],
        compiler_params=params(50 << 20),
        cost_estimate=cost(5_000_000_000, 8_000_000),
        name="scatter_local",
    )(ready, flat)

    keep, send = pl.pallas_call(
        remote_kernel,
        out_shape=(half, half),
        in_specs=[VMEM, VMEM, VMEM],
        out_specs=(VMEM, VMEM),
        scratch_shapes=[
            held,
            pltpu.VMEM((16, wide), f32),
            pltpu.VMEM((rows, 8, length), bf16),
        ],
        compiler_params=params(),
        cost_estimate=cost(20_000_000_000, 800_000),
        name="scatter_remote",
    )(ready, gathered, begun)
    got = lax.ppermute(send, "grp", [(i, groups - 1 - i) for i in range(groups)])

    initial, partial = pl.pallas_call(
        project_kernel,
        in_specs=[VMEM] * 6,
        out_specs=(VMEM, VMEM),
        out_shape=(jax.ShapeDtypeStruct((16, 128), f32), jax.ShapeDtypeStruct((24, 128), f32)),
        compiler_params=params(),
        name="project",
    )(keep, got, direction, high, low, gram)

    row_sums = jnp.sum(gather_all(partial, "row"), axis=0)
    shared = gather_all(jnp.concatenate([initial, row_sums], 0), ("col", "grp"))

    new_block, coef, norm = pl.pallas_call(
        functools.partial(final_kernel, total),
        in_specs=[VMEM, VMEM, HBM],
        out_specs=(VMEM, VMEM, VMEM),
        out_shape=(
            jax.ShapeDtypeStruct((channels, points), f32),
            jax.ShapeDtypeStruct((2, inc, inc, blocks), f32),
            jax.ShapeDtypeStruct((2, inc, inc), f32),
        ),
        scratch_shapes=[
            pltpu.VMEM((256, 256), bf16),
            pltpu.VMEM((256, 256), bf16),
            pltpu.VMEM((count, points // 2), f32),
            pltpu.SemaphoreType.DMA((points // 2 // 256,)),
        ],
        compiler_params=params(50 << 20),
        name="finish",
    )(shared, kept, flat)
    return new_block, coef.transpose(3, 0, 1, 2), norm


def solution(mesh):
    in_specs = (P(None, None, "row"), P(None, "row"), P("row"), P())
    out_specs = (P(None, "row"), P(), P())
    return jax.shard_map(local, mesh=mesh, in_specs=in_specs, out_specs=out_specs, check_vma=False)
```
